32 devices in a mesh: dp: 8 (over z, y), sp: 4 (over x, core).
Axes of the slice: x: 2, y: 2, z: 4, core: 2. Of those that a mesh axis runs over, the one named last changes fastest.
Arguments:
- tokens: bfloat16 [32, 512, 768], P('dp', 'sp'), may hold values from -6 to 6
- output_grad: bfloat16 [32, 512, 768], P('dp', 'sp'), may hold values from -6 to 6
- segment_ids: int32 [32, 512], P('dp'), may hold values from 0 to 7, as said below
- lengths: int32 [32, 8], P('dp'), may hold values from 1 to 128, as said below
- owner_slot: int32 [48], replicated, may hold values from 0 to 47, as said below
- slot_weights: float32 [48, 384, 384], P('dp')
- first_moment: float32 [48, 384, 384], P('dp'), may hold values from -224 to 224
- second_moment: float32 [48, 384, 384], P('dp'), may hold values from 819.2 to 13107.2
- left_stats: float32 [48, 384, 384], P('dp'), as said below
- right_stats: float32 [48, 384, 384], P('dp'), as said below
- left_basis: float32 [48, 384, 384], P('dp'), as said below
- right_basis: float32 [48, 384, 384], P('dp'), as said below
- vector_values: float32 [3072], P('dp')
- vector_first: float32 [3072], P('dp'), may hold values from -768 to 768
- vector_second: float32 [3072], P('dp'), may hold values from 8192 to 131072
Outputs:
- block_out: bfloat16 [32, 512, 768], P('dp', 'sp')
- input_grad: float32 [32, 512, 768], P('dp', 'sp')
- moment_one: float32 [48, 384, 384], P('dp')
- moment_two: float32 [48, 384, 384], P('dp')
- left_new: float32 [48, 384, 384], P('dp')
- right_new: float32 [48, 384, 384], P('dp')
- weights_new: float32 [48, 384, 384], P('dp')
- weights_half: bfloat16 [48, 384, 384], P('dp')
- vector_one: float32 [3072], P('dp')
- vector_two: float32 [3072], P('dp')
- vector_new: float32 [3072], P('dp')
The draws below stay inside these ranges and needn't reach their ends.
Inputs may be any that keep to these rules, and one draw needn't show every extreme that they name: `segment_ids`: token t of a row carries passage p iff the sum of that row's first p lengths is at most t and the sum of its first p + 1 lengths is over t. Each row's lengths sum to 512; one length of every row is exactly 128. distinct; block b lies at place owner_slot[b] % 6 of index owner_slot[b] // 6 of dp; some index holds 6 blocks. `left_stats`: each block symmetric and positive definite. `right_stats`: each block symmetric and positive definite. `left_basis`: each block orthogonal. `right_basis`: each block orthogonal.
All inputs are finite; a program needn't handle non-finite values.
Results may differ from the reference program's by a relative error of at most 0.017.
Values may be sent and summed in bfloat16 or wider, within the bound.
A program may use at most 256 MiB of HBM per device.

```python
import math
import jax
import jax.numpy as jnp
from jax import lax

D = 768
HEADS = 12
HD = 64
FF = 3072
S = 512
NSEG = 8
MOST = 128
BLK = 384
STEP = 4
ROWS = 32
NBLK = 48
BLK_DEV = 6
SLOTS = 48


def passages(key):
    base_key = jax.random.fold_in(key, 11)
    row_keys = jax.random.split(base_key, ROWS)

    def one_row(row_key):
        first_key, second_key = jax.random.split(row_key)
        weights_int = jax.random.randint(first_key, (NSEG - 1,), 50, 100)
        leftover = S - MOST - (NSEG - 1)
        pieces = 1 + weights_int * leftover // jnp.sum(weights_int)
        missing = S - MOST - jnp.sum(pieces)
        pieces = pieces + (jnp.arange(NSEG - 1) < missing).astype(jnp.int32)
        joined = jnp.concatenate([jnp.full((1,), MOST, jnp.int32), pieces.astype(jnp.int32)])
        shuffle = jax.random.permutation(second_key, NSEG)
        length_row = joined[shuffle].astype(jnp.int32)
        closing = jnp.cumsum(length_row).astype(jnp.int32)
        places = jnp.arange(S, dtype=jnp.int32)
        segment_row = jnp.sum((places[:, None] >= closing[None, :]).astype(jnp.int32), axis=1)
        return (length_row, segment_row.astype(jnp.int32))
    return jax.vmap(one_row)(row_keys)


def draw_segment_ids(key, part):
    return passages(key)[1]


def draw_lengths(key, part):
    return passages(key)[0]


def owner_table(key):
    base_key = jax.random.fold_in(key, 23)
    first_key, second_key = jax.random.split(base_key)
    placing = jax.random.permutation(first_key, NBLK).astype(jnp.int32)
    holders = jax.random.permutation(second_key, SLOTS // BLK_DEV).astype(jnp.int32)
    return (holders[placing // BLK_DEV] * BLK_DEV + placing % BLK_DEV).astype(jnp.int32)


def draw_owner_slot(key, part):
    return owner_table(key)


def draw_slot_weights(key, part):
    owners = owner_table(key)
    square = (D // BLK) ** 2
    broad = D * FF // (BLK * BLK)
    numbers = jnp.arange(NBLK)
    narrow_scale = 1.0 / math.sqrt(D)
    scales = jnp.where(numbers < 3 * square, narrow_scale, jnp.where(numbers < 4 * square, 6.0 * narrow_scale, jnp.where(numbers < 4 * square + broad, narrow_scale, 2.0 / math.sqrt(FF))))
    slot_scale = jnp.full((SLOTS,), narrow_scale, jnp.float32).at[owners].set(scales.astype(jnp.float32))
    noise = jax.random.normal(jax.random.fold_in(key, 29), (SLOTS, BLK, BLK), jnp.float32)
    return noise * slot_scale[:, None, None]


def statistics(key, salt):
    first_key, second_key = jax.random.split(jax.random.fold_in(key, salt))
    noise = jax.random.normal(first_key, (SLOTS, BLK, BLK), jnp.float32)
    diagonal = jax.random.uniform(second_key, (SLOTS, BLK), jnp.float32, 1.0, 2.0)
    symmetric = (noise + jnp.swapaxes(noise, 1, 2)) * (0.4 / math.sqrt(2.0 * BLK))
    magnitude = BLK * 0.09 * ROWS * S
    return magnitude * (symmetric + diagonal[:, :, None] * jnp.eye(BLK, dtype=jnp.float32)[None])


def draw_left_stats(key, part):
    return statistics(key, 31)


def draw_right_stats(key, part):
    return statistics(key, 37)


def rotation(key, salt):
    block_keys = jax.random.split(jax.random.fold_in(key, salt), SLOTS)

    def one_block(block_key):
        row_key, col_key, row_sign_key, col_sign_key = jax.random.split(block_key, 4)
        freqs = jax.random.permutation(row_key, BLK).astype(jnp.int32)
        places = jax.random.permutation(col_key, BLK).astype(jnp.int32)
        row_signs = (2 * jax.random.randint(row_sign_key, (BLK,), 0, 2) - 1).astype(jnp.float32)
        col_signs = (2 * jax.random.randint(col_sign_key, (BLK,), 0, 2) - 1).astype(jnp.float32)
        phase = (2 * places[None, :] + 1) * freqs[:, None] % (4 * BLK)
        angle = phase.astype(jnp.float32) * (math.pi / (2.0 * BLK))
        scale = jnp.where(freqs == 0, math.sqrt(1.0 / BLK), math.sqrt(2.0 / BLK)).astype(jnp.float32)
        return (jnp.cos(angle) * scale[:, None] * row_signs[:, None] * col_signs[None, :]).astype(jnp.float32)
    return jax.vmap(one_block)(block_keys)


def draw_left_basis(key, part):
    return rotation(key, 41)


def draw_right_basis(key, part):
    return rotation(key, 43)


def draw_vector_values(key, part):
    numbers = jnp.arange(4 * D)
    kinds = numbers // D % 2
    gains = jax.random.uniform(jax.random.fold_in(key, 53), (4 * D,), jnp.float32, 0.6, 1.4)
    shifts = 0.3 * jax.random.normal(jax.random.fold_in(key, 59), (4 * D,), jnp.float32)
    return jnp.where(kinds == 0, gains, shifts)


def steps_of(key, extent, cuts, least, largest):
    loudness, own = 1.0, jax.random.fold_in(key, 6)
    for axis_at, shards_of in cuts:
        steps = jnp.exp(jax.random.uniform(jax.random.fold_in(own, axis_at), (shards_of,), jnp.float32, least / len(cuts), largest / len(cuts)))
        loudness = loudness * jnp.repeat(steps, extent[axis_at] // shards_of).reshape([-1 if axis == axis_at else 1 for axis in range(len(extent))])
    return loudness


def gaussian(rng, extent, scale, reach, shards=(), kind=jnp.bfloat16):
    loudness = steps_of(rng, extent, shards, -0.22, 0.18) if shards else 1.0
    drawn = jax.random.normal(rng, extent, jnp.float32) * scale * loudness
    return jnp.minimum(jnp.maximum(drawn, -reach), reach).astype(kind)


def setup_inputs(seed: int = 0) -> dict:
    streams_of = jax.random.split(jax.random.key(seed), 16)
    return {
        "tokens": gaussian(streams_of[0], (ROWS, S, D), 1.0, 6.0, ((0, 8), (1, 4))),
        "output_grad": gaussian(streams_of[1], (ROWS, S, D), 1.0, 6.0, ((0, 8), (1, 4))),
        "segment_ids": draw_segment_ids(jax.random.fold_in(streams_of[15], 71), 0),
        "lengths": draw_lengths(jax.random.fold_in(streams_of[15], 71), 0),
        "owner_slot": draw_owner_slot(jax.random.fold_in(streams_of[15], 71), 0),
        "slot_weights": draw_slot_weights(jax.random.fold_in(streams_of[15], 71), 0),
        "first_moment": gaussian(streams_of[6], (SLOTS, BLK, BLK), (0.3 * (ROWS * S) ** 0.5), 224.0, ((0, 8),), jnp.float32),
        "second_moment": jnp.clip(jnp.exp(math.log(13107.2) - 2.7725887 * jax.random.uniform(streams_of[7], (SLOTS, BLK, BLK), jnp.float32) ** steps_of(streams_of[7], (SLOTS, BLK, BLK), ((0, 8),), -0.2, 0.2)), 819.2, 13107.2),
        "left_stats": draw_left_stats(jax.random.fold_in(streams_of[15], 71), 0),
        "right_stats": draw_right_stats(jax.random.fold_in(streams_of[15], 71), 0),
        "left_basis": draw_left_basis(jax.random.fold_in(streams_of[15], 71), 0),
        "right_basis": draw_right_basis(jax.random.fold_in(streams_of[15], 71), 0),
        "vector_values": draw_vector_values(jax.random.fold_in(streams_of[15], 71), 0),
        "vector_first": gaussian(streams_of[13], (4 * D,), ((ROWS * S) ** 0.5), 768.0, ((0, 8),), jnp.float32),
        "vector_second": jnp.clip(jnp.exp(math.log(131072.0) - 2.7725887 * jax.random.uniform(streams_of[14], (4 * D,), jnp.float32) ** steps_of(streams_of[14], (4 * D,), ((0, 8),), -0.2, 0.2)), 8192.0, 131072.0),
    }


highest = lax.Precision.HIGHEST
rate_matrix = 0.04
rate_vector = 0.2

@jax.custom_vjp
def low(v):
    return lax.optimization_barrier(v.astype(jnp.bfloat16)).astype(jnp.float32)

@jax.custom_vjp
def low_back(v):
    return v

def low_keep(v):
    return (low(v), None)

def low_pass(kept, grad):
    return (grad,)

def back_keep(v):
    return (v, None)

def back_low(kept, grad):
    return (low(grad),)
low.defvjp(low_keep, low_pass)
low_back.defvjp(back_keep, back_low)

def matmul(left_mat, right_mat):
    return jnp.dot(left_mat, right_mat, precision=highest, preferred_element_type=jnp.float32)

def layer_norm(summed, gain, shift):
    centre = lax.optimization_barrier(jnp.mean(summed, axis=-1, keepdims=True))
    centred = summed - centre
    spread = lax.optimization_barrier(jnp.mean(centred * centred, axis=-1, keepdims=True))
    return centred * lax.rsqrt(spread + 1e-06) * gain + shift

def passage_mask(segment_row, length_row):
    starts = (jnp.cumsum(length_row) - length_row).astype(jnp.int32)
    number = length_row.shape[0]
    onehot = (segment_row[:, None] == jnp.arange(number, dtype=jnp.int32)[None, :]).astype(jnp.int32)
    opening = lax.optimization_barrier(jnp.sum(onehot * starts[None, :], axis=1))
    closing = opening + lax.optimization_barrier(jnp.sum(onehot * length_row[None, :], axis=1))
    places = jnp.arange(segment_row.shape[0], dtype=jnp.int32)
    return (places[None, :] >= opening[:, None]) & (places[None, :] < closing[:, None])

def into_blocks(matrix):
    height, breadth = matrix.shape
    return matrix.reshape(height // BLK, BLK, breadth // BLK, BLK).transpose(0, 2, 1, 3).reshape(-1, BLK, BLK)

def from_blocks(blocks, height, breadth):
    return blocks.reshape(height // BLK, breadth // BLK, BLK, BLK).transpose(0, 2, 1, 3).reshape(height, breadth)

def split_blocks(blocks):
    square = (D // BLK) ** 2
    broad = D * FF // (BLK * BLK)
    w_query = from_blocks(blocks[0:square], D, D)
    w_key = from_blocks(blocks[square:2 * square], D, D)
    w_value = from_blocks(blocks[2 * square:3 * square], D, D)
    w_output = from_blocks(blocks[3 * square:4 * square], D, D)
    w_upward = from_blocks(blocks[4 * square:4 * square + broad], D, FF)
    w_downward = from_blocks(blocks[4 * square + broad:4 * square + 2 * broad], FF, D)
    return (w_query, w_key, w_value, w_output, w_upward, w_downward)

def soap_update(gradient, weights, moment_old, second_old, left_old, right_old, left_rot, right_rot):
    left_next = 0.95 * left_old + 0.05 * jnp.einsum('nij,nkj->nik', gradient, gradient, precision=highest)
    right_next = 0.95 * right_old + 0.05 * jnp.einsum('nji,njk->nik', gradient, gradient, precision=highest)
    turned = jnp.einsum('nji,njk->nik', left_rot, gradient, precision=highest)
    turned = jnp.einsum('nij,njk->nik', turned, right_rot, precision=highest)
    moment_next = 0.5 * moment_old + 0.5 * turned
    second_next = 0.5 * second_old + 0.5 * turned * turned
    correct = 1.0 - 0.5 ** STEP
    ratio = moment_next / correct / (jnp.sqrt(second_next / correct) + 1e-08)
    stepped = jnp.einsum('nij,njk->nik', left_rot, ratio, precision=highest)
    stepped = jnp.einsum('nij,nkj->nik', stepped, right_rot, precision=highest)
    return (moment_next, second_next, left_next, right_next, weights - rate_matrix * stepped)

def adam_update(gradient, values, moment_old, second_old):
    moment_next = 0.5 * moment_old + 0.5 * gradient
    second_next = 0.5 * second_old + 0.5 * gradient * gradient
    correct = 1.0 - 0.5 ** STEP
    ratio = moment_next / correct / (jnp.sqrt(second_next / correct) + 1e-08)
    return (moment_next, second_next, values - rate_vector * ratio)

def attend(joint_row, segment_row, length_row):
    query = joint_row[:, 0]
    keyed = joint_row[:, 1]
    valued = joint_row[:, 2]
    scores = low_back(jnp.einsum('qhd,khd->hqk', query, keyed, precision=highest) * 0.125)
    scores = jnp.where(passage_mask(segment_row, length_row)[None], scores, -1e+30)
    probs = jax.nn.softmax(scores, axis=-1)
    return jnp.einsum('hqk,khd->qhd', low(probs), valued, precision=highest)

def forward(params, inputs, segment_rows, length_rows):
    w_joint, w_output, w_upward, w_downward, vector = params
    gains = vector.reshape(4, D)
    row_count = inputs.shape[0]
    flat_tokens = inputs.reshape(-1, D)
    joint = low(low_back(matmul(flat_tokens, w_joint))).reshape(row_count, S, 3, HEADS, HD)
    context = jax.vmap(attend)(joint, segment_rows, length_rows)
    context = low(low_back(context.reshape(-1, D)))
    attended = low_back(matmul(context, w_output))
    hidden = layer_norm(flat_tokens + attended, gains[0], gains[1])
    upward = low_back(matmul(low(hidden), w_upward))
    active = low(jax.nn.gelu(upward, approximate=False))
    downward = low_back(matmul(active, w_downward))
    return layer_norm(hidden + downward, gains[2], gains[3])

def reference(tokens, output_grad, segment_ids, lengths, owner_slot, slot_weights, first_moment, second_moment, left_stats, right_stats, left_basis, right_basis, vector_values, vector_first, vector_second):
    blocks = low(jnp.take(slot_weights, owner_slot, axis=0))
    w_query, w_key, w_value, w_output, w_upward, w_downward = split_blocks(blocks)
    params = (jnp.concatenate([w_query, w_key, w_value], axis=1), w_output, w_upward, w_downward, low(vector_values))
    group_rows = math.gcd(ROWS, 8)
    group_count = ROWS // group_rows
    inputs = tokens.astype(jnp.float32).reshape(group_count, group_rows, S, D)
    cotangents = output_grad.astype(jnp.float32).reshape(group_count, group_rows * S, D)
    segment_groups = segment_ids.reshape(group_count, group_rows, S)
    length_groups = lengths.reshape(group_count, group_rows, NSEG)

    def one_group(totals, item):
        group_in, group_cot, group_seg, group_len = item
        value, pullback = jax.vjp(lambda weights, given: forward(weights, given, group_seg, group_len), params, group_in)
        grad_params, grad_in = pullback(group_cot)
        totals = jax.tree.map(lambda old, new: old + new, totals, grad_params)
        return (totals, (value, grad_in))
    zeros = jax.tree.map(jnp.zeros_like, params)
    grads, (outputs, input_grads) = lax.scan(one_group, zeros, (inputs, cotangents, segment_groups, length_groups))
    grad_joint, grad_output, grad_upward, grad_downward, grad_vector = grads
    block_out = outputs.reshape(ROWS, S, D).astype(jnp.bfloat16)
    input_grad = input_grads.reshape(ROWS, S, D)
    grad_blocks = jnp.concatenate([into_blocks(grad_joint[:, :D]), into_blocks(grad_joint[:, D:2 * D]), into_blocks(grad_joint[:, 2 * D:]), into_blocks(grad_output), into_blocks(grad_upward), into_blocks(grad_downward)], axis=0)
    grad_slots = jnp.zeros((SLOTS, BLK, BLK), jnp.float32).at[owner_slot].set(grad_blocks)
    moment_one, moment_two, left_new, right_new, weights_new = soap_update(grad_slots, slot_weights, first_moment, second_moment, left_stats, right_stats, left_basis, right_basis)
    vector_one, vector_two, vector_new = adam_update(grad_vector, vector_values, vector_first, vector_second)
    return (block_out, input_grad, moment_one, moment_two, left_new, right_new, weights_new, weights_new.astype(jnp.bfloat16), vector_one, vector_two, vector_new)
```

```python
import functools
import jax
import jax.numpy as jnp
from jax import lax
from jax.experimental import pallas as pl
from jax.experimental.pallas import tpu as pltpu
from jax.sharding import PartitionSpec as P

D = 768
HD = 64
FF = 3072
BLK = 384
STEP = 4


highest = lax.Precision.HIGHEST
rate_matrix = 0.04
rate_vector = 0.2


def layer_norm(summed, gain, shift):
    centre = jnp.mean(summed, axis=-1, keepdims=True)
    centred = summed - centre
    spread = jnp.mean(centred * centred, axis=-1, keepdims=True)
    return centred * lax.rsqrt(spread + 1e-06) * gain + shift


def exact_gelu(values):
    return jax.nn.gelu(values, approximate=False)


def passage_mask(segment_row, length_row):
    starts = jnp.cumsum(length_row) - length_row
    number = length_row.shape[0]
    onehot = (segment_row[:, None] == jnp.arange(number, dtype=jnp.int32)[None, :]).astype(
        jnp.int32
    )
    opening = jnp.sum(onehot * starts[None, :], axis=1)
    closing = opening + jnp.sum(onehot * length_row[None, :], axis=1)
    places = jnp.arange(segment_row.shape[0], dtype=jnp.int32)
    return (places[None, :] >= opening[:, None]) & (places[None, :] < closing[:, None])


def into_blocks(matrix):
    height, breadth = matrix.shape
    return (
        matrix.reshape(height // BLK, BLK, breadth // BLK, BLK)
        .transpose(0, 2, 1, 3)
        .reshape(-1, BLK, BLK)
    )


def from_blocks(blocks, height, breadth):
    return (
        blocks.reshape(height // BLK, breadth // BLK, BLK, BLK)
        .transpose(0, 2, 1, 3)
        .reshape(height, breadth)
    )


def split_blocks(blocks):
    square = (D // BLK) ** 2
    broad = D * FF // (BLK * BLK)
    w_query = from_blocks(blocks[0:square], D, D)
    w_key = from_blocks(blocks[square : 2 * square], D, D)
    w_value = from_blocks(blocks[2 * square : 3 * square], D, D)
    w_output = from_blocks(blocks[3 * square : 4 * square], D, D)
    w_upward = from_blocks(blocks[4 * square : 4 * square + broad], D, FF)
    w_downward = from_blocks(blocks[4 * square + broad : 4 * square + 2 * broad], FF, D)
    return (w_query, w_key, w_value, w_output, w_upward, w_downward)


def contract_rows(left_mat, right_mat):
    return lax.dot_general(
        left_mat, right_mat, (((0,), (0,)), ((), ())), preferred_element_type=jnp.float32
    )


def contract_cols(left_mat, right_mat):
    return lax.dot_general(
        left_mat, right_mat, (((1,), (1,)), ((), ())), preferred_element_type=jnp.float32
    )


def soap_update(
    gradient, weights, moment_old, second_old, left_old, right_old, left_rot, right_rot
):
    left_next = 0.95 * left_old + 0.05 * jnp.einsum(
        "nij,nkj->nik", gradient, gradient, precision=highest
    )
    right_next = 0.95 * right_old + 0.05 * jnp.einsum(
        "nji,njk->nik", gradient, gradient, precision=highest
    )
    turned = jnp.einsum("nji,njk->nik", left_rot, gradient, precision=highest)
    turned = jnp.einsum("nij,njk->nik", turned, right_rot, precision=highest)
    moment_next = 0.5 * moment_old + 0.5 * turned
    second_next = 0.5 * second_old + 0.5 * turned * turned
    correct = 1.0 - 0.5**STEP
    ratio = moment_next / correct / (jnp.sqrt(second_next / correct) + 1e-08)
    stepped = jnp.einsum("nij,njk->nik", left_rot, ratio, precision=highest)
    stepped = jnp.einsum("nij,nkj->nik", stepped, right_rot, precision=highest)
    return (moment_next, second_next, left_next, right_next, weights - rate_matrix * stepped)


def adam_update(gradient, values, moment_old, second_old):
    moment_next = 0.5 * moment_old + 0.5 * gradient
    second_next = 0.5 * second_old + 0.5 * gradient * gradient
    correct = 1.0 - 0.5**STEP
    ratio = moment_next / correct / (jnp.sqrt(second_next / correct) + 1e-08)
    return (moment_next, second_next, values - rate_vector * ratio)


def masked_scores(joint_row, segment_row, length_row):
    positions = joint_row.shape[0]
    query = joint_row[:, 0].reshape(positions, -1, HD)
    keyed = joint_row[:, 1].reshape(positions, -1, HD)
    valued = joint_row[:, 2].reshape(positions, -1, HD)
    scores = jnp.einsum("qhd,khd->hqk", query, keyed, preferred_element_type=jnp.float32) * 0.125
    visible = passage_mask(segment_row, length_row)
    return (jnp.where(visible[None], scores, -1e30), query, keyed, valued)


def attend_rows(item):
    joint_row, segment_row, length_row = item
    scores, query, keyed, valued = masked_scores(joint_row, segment_row, length_row)
    largest = jnp.max(scores, axis=-1, keepdims=True)
    raised = jnp.exp(scores - largest)
    totals = jnp.sum(raised, axis=-1, keepdims=True)
    probs = raised / totals
    logsum = (largest + jnp.log(totals))[..., 0]
    context = jnp.einsum(
        "hqk,khd->qhd", probs.astype(jnp.bfloat16), valued, preferred_element_type=jnp.float32
    )
    return (context.reshape(joint_row.shape[0], -1).astype(jnp.bfloat16), logsum)


def back_rows(item):
    joint_row, logsum, delta_context, segment_row, length_row = item
    positions = joint_row.shape[0]
    scores, query, keyed, valued = masked_scores(joint_row, segment_row, length_row)
    probs = jnp.exp(scores - logsum[..., None])
    delta_ctx = delta_context.reshape(positions, -1, HD)
    delta_value = jnp.einsum(
        "hqk,qhd->khd", probs.astype(jnp.bfloat16), delta_ctx, preferred_element_type=jnp.float32
    )
    delta_prob = jnp.einsum("qhd,khd->hqk", delta_ctx, valued, preferred_element_type=jnp.float32)
    weighted = jnp.sum(probs * delta_prob, axis=-1, keepdims=True)
    delta_score = (probs * (delta_prob - weighted)).astype(jnp.bfloat16)
    delta_query = (
        jnp.einsum("hqk,khd->qhd", delta_score, keyed, preferred_element_type=jnp.float32) * 0.125
    )
    delta_key = (
        jnp.einsum("hqk,qhd->khd", delta_score, query, preferred_element_type=jnp.float32) * 0.125
    )
    stacked = jnp.stack(
        [
            delta_query.reshape(positions, -1),
            delta_key.reshape(positions, -1),
            delta_value.reshape(positions, -1),
        ],
        axis=1,
    )
    return stacked.astype(jnp.bfloat16)


def pick_blocks(source, slot_index, owner_slot, fanout, part_index):
    matches = owner_slot[None, :] == slot_index[:, None]
    present = jnp.any(matches, axis=1).astype(jnp.float32)
    chosen = jnp.sum(
        matches.astype(jnp.int32) * jnp.arange(owner_slot.shape[0], dtype=jnp.int32)[None, :],
        axis=1,
    )
    picked = jnp.take(source, chosen * fanout + part_index, axis=0)
    return picked * present[:, None, None]


def per_device(
    tokens,
    output_grad,
    segment_ids,
    lengths,
    owner_slot,
    slot_weights,
    first_moment,
    second_moment,
    left_stats,
    right_stats,
    left_basis,
    right_basis,
    vector_values,
    vector_first,
    vector_second,
):
    holding = slot_weights.shape[0]
    row_count = tokens.shape[0]
    token_count = tokens.shape[1]
    gathered, vector_half = (
        lax.all_gather(slot_weights.astype(jnp.bfloat16), "dp", axis=0, tiled=True),
        lax.all_gather(vector_values.astype(jnp.bfloat16), "dp", axis=0, tiled=True),
    )
    blocks = jnp.take(gathered, owner_slot, axis=0)
    w_query, w_key, w_value, w_output, w_upward, w_downward = split_blocks(blocks)
    w_joint = jnp.concatenate([w_query, w_key, w_value], axis=1)
    gains = vector_half.astype(jnp.float32).reshape(4, D)
    flat_tokens = tokens.reshape(-1, D)
    projected = jnp.dot(flat_tokens, w_joint, preferred_element_type=jnp.float32).astype(
        jnp.bfloat16
    )
    projected = projected.reshape(row_count, token_count, 3, D)
    heads = lax.all_to_all(projected, "sp", split_axis=3, concat_axis=1, tiled=True)
    context, logsum = lax.map(attend_rows, (heads, segment_ids, lengths))
    context_tok = lax.all_to_all(context, "sp", split_axis=1, concat_axis=2, tiled=True).reshape(
        -1, D
    )
    attended = jnp.dot(context_tok, w_output, preferred_element_type=jnp.float32)
    summed_one = flat_tokens.astype(jnp.float32) + attended
    hidden, norm_one_pull = jax.vjp(layer_norm, summed_one, gains[0], gains[1])
    hidden_half = hidden.astype(jnp.bfloat16)
    upward = jnp.dot(hidden_half, w_upward, preferred_element_type=jnp.float32)
    activated, gelu_pull = jax.vjp(exact_gelu, upward)
    active_half = activated.astype(jnp.bfloat16)
    downward = jnp.dot(active_half, w_downward, preferred_element_type=jnp.float32)
    result, norm_two_pull = jax.vjp(layer_norm, hidden + downward, gains[2], gains[3])
    block_out = result.astype(jnp.bfloat16).reshape(row_count, token_count, D)
    cotangent = output_grad.reshape(-1, D).astype(jnp.float32)
    delta_two, delta_gain_two, delta_shift_two = norm_two_pull(cotangent)
    delta_down = delta_two.astype(jnp.bfloat16)
    grad_down = contract_rows(active_half, delta_down)
    delta_active = contract_cols(delta_down, w_downward)
    (delta_upward,) = gelu_pull(delta_active)
    delta_up = delta_upward.astype(jnp.bfloat16)
    grad_up = contract_rows(hidden_half, delta_up)
    delta_hidden = delta_two + contract_cols(delta_up, w_upward)
    delta_one, delta_gain_one, delta_shift_one = norm_one_pull(delta_hidden)
    delta_attn = delta_one.astype(jnp.bfloat16)
    grad_output = contract_rows(context_tok, delta_attn)
    delta_context = (
        contract_cols(delta_attn, w_output).astype(jnp.bfloat16).reshape(row_count, token_count, D)
    )
    delta_heads = lax.all_to_all(delta_context, "sp", split_axis=2, concat_axis=1, tiled=True)
    delta_projected = lax.map(back_rows, (heads, logsum, delta_heads, segment_ids, lengths))
    delta_joint = lax.all_to_all(
        delta_projected, "sp", split_axis=1, concat_axis=3, tiled=True
    ).reshape(-1, 3 * D)
    grad_joint = contract_rows(flat_tokens, delta_joint)
    input_grad = (delta_one + contract_cols(delta_joint, w_joint)).reshape(
        row_count, token_count, D
    )
    grad_blocks = jnp.concatenate(
        [
            into_blocks(grad_joint[:, :D]),
            into_blocks(grad_joint[:, D : 2 * D]),
            into_blocks(grad_joint[:, 2 * D :]),
            into_blocks(grad_output),
            into_blocks(grad_up),
            into_blocks(grad_down),
        ],
        axis=0,
    )
    vector_grad = jnp.concatenate(
        [delta_gain_one, delta_shift_one, delta_gain_two, delta_shift_two]
    )
    vector_total = lax.psum(vector_grad, ("dp", "sp"))
    piece_len = vector_values.shape[0]
    vector_piece = lax.dynamic_slice_in_dim(
        vector_total, lax.axis_index("dp") * piece_len, piece_len
    )
    slot_index = jnp.arange(holding * lax.axis_size("dp"), dtype=jnp.int32)
    owned = lax.psum_scatter(
        pick_blocks(grad_blocks, slot_index, owner_slot, 1, 0),
        "dp",
        scatter_dimension=0,
        tiled=True,
    )
    owned = lax.psum(owned.astype(jnp.bfloat16), "sp").astype(jnp.float32)
    moment_one, moment_two, left_new, right_new, weights_new = soap_update(
        owned,
        slot_weights,
        first_moment,
        second_moment,
        left_stats,
        right_stats,
        left_basis,
        right_basis,
    )
    vector_one, vector_two, vector_new = adam_update(
        vector_piece, vector_values, vector_first, vector_second
    )
    return (
        block_out,
        input_grad,
        moment_one,
        moment_two,
        left_new,
        right_new,
        weights_new,
        weights_new.astype(jnp.bfloat16),
        vector_one,
        vector_two,
        vector_new,
    )


PITCH = BLK + 16
MESH = pl.DeviceIdType.MESH
NZ = 4


def place():
    dp = lax.axis_index("dp")
    sp = lax.axis_index("sp")
    return dp // 2, dp % 2, sp // 2, sp % 2


def greet(z, y, x, c):
    barrier = pltpu.get_barrier_semaphore()
    dp = z * 2 + y
    sp = x * 2 + c

    def signal(target):
        pl.semaphore_signal(barrier, 1, device_id=target, device_id_type=MESH)

    for step in range(1, 4):
        signal((dp, (sp + step) % 4))
    signal((z * 2 + 1 - y, sp))

    @pl.when(z < NZ - 1)
    def _():
        signal((dp + 2, sp))

    @pl.when(z > 0)
    def _():
        signal((dp - 2, sp))

    pl.semaphore_wait(barrier, 4 + (z < NZ - 1).astype(jnp.int32) + (z > 0).astype(jnp.int32))


def gather_kernel(
    weights, vector, tokens, grads, out, token_row, grad_row,
    wide, narrow, load_sem, keep_sem, send_sem, recv_sem, row_send, row_recv, row_keep,
):
    z, y, x, c = place()
    dp = z * 2 + y
    sp = x * 2 + c
    loads = [pltpu.make_async_copy(weights.at[i], wide.at[i], load_sem.at[i]) for i in range(6)]
    for load in loads:
        load.start()
    keeps = [
        pltpu.make_async_copy(tokens.at[sp], token_row.at[sp], row_keep.at[0]),
        pltpu.make_async_copy(grads.at[sp], grad_row.at[sp], row_keep.at[1]),
    ]
    for keep in keeps:
        keep.start()
    gains = jnp.broadcast_to(vector[...], (16, BLK)).astype(jnp.bfloat16)
    greet(z, y, x, c)

    def rows_copy(which, source, landing, step):
        peer = (sp + step) % 4
        return pltpu.make_async_remote_copy(
            src_ref=source.at[peer], dst_ref=landing.at[sp],
            send_sem=row_send.at[which, step - 1], recv_sem=row_recv.at[which, sp],
            device_id=(dp, peer), device_id_type=MESH,
        )

    def rows_arrival(which, source, landing, step):
        peer = (sp + step) % 4
        return pltpu.make_async_remote_copy(
            src_ref=source.at[peer], dst_ref=landing.at[peer],
            send_sem=row_send.at[which, step - 1], recv_sem=row_recv.at[which, peer],
            device_id=(dp, peer), device_id_type=MESH,
        )

    for step in (2, 3, 1):
        rows_copy(0, tokens, token_row, step).start()

    for i in range(6):
        loads[i].wait()
        narrow[i, :BLK, :] = wide[i].astype(jnp.bfloat16)
        narrow[i, BLK:, :] = gains
    own = [pltpu.make_async_copy(narrow.at[i], out.at[dp * 6 + i], keep_sem.at[i]) for i in range(6)]

    def piece(part):
        return (c, BLK + 16) if part == 0 else (2 + 2 * x + c, BLK)

    targets = {
        "up": (dp + 2, sp), "down": (dp - 2, sp), "y": (z * 2 + 1 - y, sp),
        "x": (dp, (1 - x) * 2 + c), "core": (dp, x * 2 + 1 - c),
    }
    number = {"up": 0, "down": 1, "y": 2, "x": 3, "core": 4}

    def copy(way, holder, slot, height, index, source=None):
        at = holder * 6 + slot
        src = out.at[at, pl.ds(0, height)] if source is None else source
        return pltpu.make_async_remote_copy(
            src_ref=src, dst_ref=out.at[at, pl.ds(0, height)],
            send_sem=send_sem.at[number[way], index], recv_sem=recv_sem.at[at],
            device_id=targets[way], device_id_type=MESH,
        )

    started = []

    def start(way, holder, slot, height, index, valid=None, source=None):
        item = copy(way, holder, slot, height, index, source)
        if valid is None:
            item.start()
        else:
            pl.when(valid)(item.start)
        started.append((item, valid))

    def arrive(holder, slot, height, valid=None):
        item = copy("core", holder, slot, height, 0)
        if valid is None:
            item.wait_recv()
        else:
            pl.when(valid)(item.wait_recv)

    counts = {}

    def fresh(way):
        counts[way] = counts.get(way, -1) + 1
        return counts[way]

    for part in (1, 0):
        slot, height = piece(part)
        src = narrow.at[slot, pl.ds(0, height)]
        start("up", dp, slot, height, fresh("up"), z < NZ - 1, src)
        start("down", dp, slot, height, fresh("down"), z > 0, src)
        start("y", dp, slot, height, fresh("y"), None, src)
    for item in own:
        item.start()

    def from_z(sign, far, part):
        origin = z + sign * far
        inside = (origin >= 0) if sign < 0 else (origin <= NZ - 1)
        holder = origin * 2 + y
        slot, height = piece(part)
        arrive(holder, slot, height, inside)
        if far < NZ - 1:
            if sign < 0:
                start("up", holder, slot, height, fresh("up"), inside & (z < NZ - 1))
            else:
                start("down", holder, slot, height, fresh("down"), inside & (z > 0))
        start("y", holder, slot, height, fresh("y"), inside)
        if part == 1:
            start("x", holder, slot, height, fresh("x"), inside)
        start("core", holder, slot, height, fresh("core"), inside)

    def signs(far):
        return (0,) if far == 0 else (-1, 1)

    def valid_of(sign, far):
        origin = z + sign * far
        if far == 0:
            return origin, None
        return origin, ((origin >= 0) if sign < 0 else (origin <= NZ - 1))

    def from_y(sign, far, part):
        origin, inside = valid_of(sign, far)
        holder = origin * 2 + 1 - y
        slot, height = piece(part)
        arrive(holder, slot, height, inside)
        if part == 1:
            start("x", holder, slot, height, fresh("x"), inside)
        start("core", holder, slot, height, fresh("core"), inside)

    def from_x(sign, far, side):
        origin, inside = valid_of(sign, far)
        holder = origin * 2 + (y if side == 0 else 1 - y)
        slot = 2 + 2 * (1 - x) + c
        arrive(holder, slot, BLK, inside)
        start("core", holder, slot, BLK, fresh("core"), inside)

    for far in range(1, NZ):
        for part in (1, 0):
            for sign in (-1, 1):
                from_z(sign, far, part)
            for sign in signs(far - 1):
                from_y(sign, far - 1, part)
        if far == 1:
            for step in (2, 3, 1):
                rows_copy(1, grads, grad_row, step).start()
        if far >= 2:
            for sign in signs(far - 1):
                from_x(sign, far - 1, 0)
            for sign in signs(far - 2):
                from_x(sign, far - 2, 1)
    for part in (1, 0):
        for sign in (-1, 1):
            from_y(sign, NZ - 1, part)
    for sign in (-1, 1):
        from_x(sign, NZ - 1, 0)
    for far in (NZ - 2, NZ - 1):
        for sign in signs(far):
            from_x(sign, far, 1)

    for far in range(NZ):
        for sign in signs(far):
            origin, inside = valid_of(sign, far)
            for side in (0, 1):
                if far == 0 and side == 0:
                    continue
                holder = origin * 2 + (y if side == 0 else 1 - y)
                for slot, height in ((1 - c, BLK + 16), (3 - c, BLK), (5 - c, BLK)):
                    arrive(holder, slot, height, inside)
    for step in (2, 3, 1):
        rows_arrival(0, tokens, token_row, step).wait_recv()
        rows_arrival(1, grads, grad_row, step).wait_recv()
        rows_copy(0, tokens, token_row, step).wait_send()
        rows_copy(1, grads, grad_row, step).wait_send()
    for item, valid in started:
        if valid is None:
            item.wait_send()
        else:
            pl.when(valid)(item.wait_send)
    for item in own + keeps:
        item.wait()


def gather_all(weights, vector, tokens, grads):
    anywhere = pl.BlockSpec(memory_space=pl.ANY)
    return pl.pallas_call(
        gather_kernel,
        name="gather_all",
        out_shape=[
            jax.ShapeDtypeStruct((48, PITCH, BLK), jnp.bfloat16),
            jax.ShapeDtypeStruct(tokens.shape, jnp.bfloat16),
            jax.ShapeDtypeStruct(grads.shape, jnp.bfloat16),
        ],
        in_specs=[anywhere, pl.BlockSpec(memory_space=pltpu.VMEM), anywhere, anywhere],
        out_specs=[anywhere, anywhere, anywhere],
        scratch_shapes=[
            pltpu.VMEM((6, BLK, BLK), jnp.float32),
            pltpu.VMEM((6, PITCH, BLK), jnp.bfloat16),
            pltpu.SemaphoreType.DMA((6,)),
            pltpu.SemaphoreType.DMA((6,)),
            pltpu.SemaphoreType.DMA((5, 40)),
            pltpu.SemaphoreType.DMA((48,)),
            pltpu.SemaphoreType.DMA((2, 3)),
            pltpu.SemaphoreType.DMA((2, 4)),
            pltpu.SemaphoreType.DMA((2,)),
        ],
        compiler_params=pltpu.CompilerParams(
            collective_id=0, has_side_effects=True, vmem_limit_bytes=24 << 20
        ),
    )(weights, vector.reshape(1, BLK), tokens, grads)


BLANK = BLK + 16
HALF = BLK // 2


def reduce_kernel(
    grads, rows_a, rows_b, total, land_a, land_b,
    mine0, mine1, mine2, mine3, core0, core1, core2, core3, cross, side0, side1, side2,
    line0, line1, line2, last0, last1,
    load_sem, core_send, core_recv, x_send, x_recv, y_send, y_recv, z_send, z_recv,
    last_send, last_recv, give_send, give_recv, keep_sem, row_send, row_recv, row_keep,
):
    z, y, x, c = place()
    dp = z * 2 + y
    sp = x * 2 + c
    mine = (mine0, mine1, mine2, mine3)
    core = (core0, core1, core2, core3)
    side = (side0, side1, side2)
    line = (line0, line1, line2)
    last = (last0, last1)
    high = z // 2
    order = (3 - 3 * high, 2 - high, 1 - z + 4 * high, z)
    twin = (dp, (1 - x) * 2 + c)
    mate = (dp, x * 2 + 1 - c)
    beside = (z * 2 + 1 - y, sp)
    inner = (z > 0) & (z < NZ - 1)

    def view(ref, stream, dest, core_of):
        base = dest * 6
        if stream == 0:
            return ref.at[base + core_of, pl.ds(0, BLANK)]
        if stream == 1:
            return ref.at[base + 2 + core_of, pl.ds(0, BLK)]
        slot = base + (4 + x if stream == 2 else 5 - x)
        return ref.at[slot, pl.ds(pl.multiple_of(core_of * HALF, HALF), HALF)]

    def remote(src, dst, send, recv, target):
        return pltpu.make_async_remote_copy(
            src_ref=src, dst_ref=dst, send_sem=send, recv_sem=recv,
            device_id=target, device_id_type=MESH,
        )

    def load(stream, dest):
        return pltpu.make_async_copy(
            view(grads, stream, dest, c), mine[stream].at[dest], load_sem.at[stream, dest]
        )

    def to_mate(stream, dest):
        return remote(
            view(grads, stream, dest, 1 - c), core[stream].at[dest],
            core_send.at[stream, dest], core_recv.at[stream, dest], mate,
        )

    def to_twin(dest):
        return remote(mine3.at[dest], cross.at[dest], x_send.at[dest], x_recv.at[dest], twin)

    def to_side(stream, goal):
        dest = goal * 2 + 1 - y
        return remote(
            mine[stream].at[dest], side[stream].at[goal],
            y_send.at[stream, goal], y_recv.at[stream, goal], beside,
        )

    def row_copy(which, source, landing, step, arrival):
        peer = (sp + step) % 4
        at = peer if arrival else sp
        return remote(
            source.at[peer], landing.at[at],
            row_send.at[which, step - 1], row_recv.at[which, at], (dp, peer),
        )

    sequence = []
    for i in range(4):
        away = order[i] * 2 + 1 - y
        sequence += [(3, away), (0, away), (1, away)]
    for i in range(4):
        sequence += [(3, order[i] * 2 + y)]
    for i in range(4):
        sequence += [(2, order[i] * 2 + 1 - y)]
    for i in range(4):
        home = order[i] * 2 + y
        sequence += [(0, home), (1, home)]
    for i in range(4):
        sequence += [(2, order[i] * 2 + y)]
    for stream, dest in sequence:
        load(stream, dest).start()
    keeps = [
        pltpu.make_async_copy(rows_a.at[sp], land_a.at[sp], row_keep.at[0]),
        pltpu.make_async_copy(rows_b.at[sp], land_b.at[sp], row_keep.at[1]),
    ]
    for keep in keeps:
        keep.start()
    greet(z, y, x, c)
    for stream, dest in sequence:
        to_mate(stream, dest).start()

    def merge(stream, dest):
        load(stream, dest).wait()
        to_mate(stream, dest).wait_recv()
        mine[stream][dest] = mine[stream][dest] + core[stream][dest]

    def along(stream, goal):
        dest = goal * 2 + y
        upward = (goal > z).astype(jnp.int32)
        step = 2 * upward - 1
        way = 1 - upward
        item = remote(
            mine[stream].at[dest], line[stream].at[way, goal],
            z_send.at[stream, goal], z_recv.at[stream, way, goal], (dp + 2 * step, sp),
        )

        @pl.when(inner)
        def _():
            item.wait_recv()
            mine[stream][dest] = mine[stream][dest] + line[stream][way, goal]

        item.start()

    def settle(stream):
        for way, valid, step in ((0, z > 0, 1), (1, z < NZ - 1, -1)):
            @pl.when(valid)
            def _():
                remote(
                    mine[stream].at[dp], line[stream].at[way, z],
                    z_send.at[stream, z], z_recv.at[stream, way, z], (dp - 2 * step, sp),
                ).wait_recv()
                mine[stream][dp] = mine[stream][dp] + line[stream][way, z]

    for i in range(4):
        away = order[i] * 2 + 1 - y
        merge(3, away)
        to_twin(away).start()
        for stream in (0, 1):
            merge(stream, away)
            to_side(stream, order[i]).start()
    for i in range(4):
        home = order[i] * 2 + y
        merge(3, home)
        to_twin(home).start()
    for step in (2, 3, 1):
        row_copy(0, rows_a, land_a, step, False).start()
    for i in range(4):
        away = order[i] * 2 + 1 - y
        merge(2, away)
        to_twin(away).wait_recv()
        mine2[away] = mine2[away] + cross[away]
        to_side(2, order[i]).start()
        home = order[i] * 2 + y
        for stream in (0, 1):
            merge(stream, home)
            to_side(stream, order[i]).wait_recv()
            mine[stream][home] = mine[stream][home] + side[stream][order[i]]
            if i < 3:
                along(stream, order[i])
    for step in (2, 3, 1):
        row_copy(1, rows_b, land_b, step, False).start()
    for i in range(4):
        home = order[i] * 2 + y
        merge(2, home)
        to_twin(home).wait_recv()
        mine2[home] = mine2[home] + cross[home]
        to_side(2, order[i]).wait_recv()
        mine2[home] = mine2[home] + side2[order[i]]
        if i < 3:
            along(2, order[i])

    def swap_last(stream):
        return remote(
            mine[stream].at[dp], last[stream], last_send.at[stream], last_recv.at[stream], twin
        )

    for stream in (0, 1):
        settle(stream)
        swap_last(stream).start()
    settle(2)

    def place_of(stream, core_of):
        return view(total, stream, 0, core_of)

    def give(stream, index, target, source, core_of):
        return remote(
            source, place_of(stream, core_of), give_send.at[index], give_recv.at[index], target
        )

    own_twin = give(2, 0, twin, mine2.at[dp], c)
    own_twin.start()
    own_mate = give(2, 1, mate, mine2.at[dp], c)
    own_mate.start()
    kept = [pltpu.make_async_copy(mine2.at[dp], place_of(2, c), keep_sem.at[2])]
    kept[0].start()
    gifts = [own_twin, own_mate]
    for stream in (0, 1):
        swap_last(stream).wait_recv()
        core[stream][dp] = mine[stream][dp] + last[stream][...]
        gift = give(stream, 2 + stream, mate, core[stream].at[dp], c)
        gift.start()
        gifts.append(gift)
        keep = pltpu.make_async_copy(core[stream].at[dp], place_of(stream, c), keep_sem.at[stream])
        keep.start()
        kept.append(keep)
    give(3, 0, twin, place_of(3, c), c).wait_recv()
    passed = give(3, 4, mate, place_of(3, c), c)
    passed.start()
    gifts.append(passed)
    for stream, index in ((2, 1), (0, 2), (1, 3), (3, 4)):
        give(stream, index, mate, place_of(stream, 1 - c), 1 - c).wait_recv()
    for step in (2, 3, 1):
        for which, source, landing in ((0, rows_a, land_a), (1, rows_b, land_b)):
            row_copy(which, source, landing, step, True).wait_recv()
            row_copy(which, source, landing, step, False).wait_send()
    for stream, dest in sequence:
        to_mate(stream, dest).wait_send()
    for i in range(4):
        for side_of in (0, 1):
            to_twin(order[i] * 2 + side_of).wait_send()
        for stream in range(3):
            to_side(stream, order[i]).wait_send()
            if i < 3:
                remote(
                    mine[stream].at[order[i] * 2 + y], line[stream].at[0, order[i]],
                    z_send.at[stream, order[i]], z_recv.at[stream, 0, order[i]], twin,
                ).wait_send()
    for stream in (0, 1):
        swap_last(stream).wait_send()
    for item in gifts:
        item.wait_send()
    for item in kept + keeps:
        item.wait()


def reduce_all(grads, rows_a, rows_b):
    anywhere = pl.BlockSpec(memory_space=pl.ANY)
    half = jnp.bfloat16
    heights = (BLANK, BLK, HALF, HALF)
    dma = pltpu.SemaphoreType.DMA
    return pl.pallas_call(
        reduce_kernel,
        name="reduce_all",
        out_shape=[
            jax.ShapeDtypeStruct((6, PITCH, BLK), half),
            jax.ShapeDtypeStruct(rows_a.shape, half),
            jax.ShapeDtypeStruct(rows_b.shape, half),
        ],
        in_specs=[anywhere] * 3,
        out_specs=[anywhere] * 3,
        scratch_shapes=[pltpu.VMEM((8, h, BLK), half) for h in heights]
        + [pltpu.VMEM((8, h, BLK), half) for h in heights]
        + [pltpu.VMEM((8, HALF, BLK), half)]
        + [pltpu.VMEM((4, h, BLK), half) for h in heights[:3]]
        + [pltpu.VMEM((2, 4, h, BLK), half) for h in heights[:3]]
        + [pltpu.VMEM((h, BLK), half) for h in heights[:2]]
        + [
            dma((4, 8)), dma((4, 8)), dma((4, 8)), dma((8,)), dma((8,)), dma((3, 4)), dma((3, 4)),
            dma((3, 4)), dma((3, 2, 4)), dma((2,)), dma((2,)), dma((5,)), dma((5,)), dma((3,)),
            dma((2, 3)), dma((2, 4)), dma((2,)),
        ],
        compiler_params=pltpu.CompilerParams(
            collective_id=1, has_side_effects=True, vmem_limit_bytes=30 << 20
        ),
    )(grads, rows_a, rows_b)


def attend_dense(joint, segment_row, length_row):
    return attend_rows((joint, segment_row, length_row))


def fast_device(
    tokens, output_grad, segment_ids, lengths, owner_slot, slot_weights, first_moment, second_moment,
    left_stats, right_stats, left_basis, right_basis, vector_values, vector_first, vector_second,
):
    row_count, token_count = tokens.shape[0], tokens.shape[1]
    place_sp = lax.axis_index("sp")
    gathered, token_row, grad_row = gather_all(slot_weights, vector_values, tokens, output_grad)
    gains = gathered[::6, BLK].reshape(4, D).astype(jnp.float32)
    segment_row = lax.dynamic_index_in_dim(segment_ids, place_sp, 0, False)
    length_row = lax.dynamic_index_in_dim(lengths, place_sp, 0, False)
    blocks = jnp.take(gathered, owner_slot, axis=0)[:, :BLK]
    w_query, w_key, w_value, w_output, w_upward, w_downward = split_blocks(blocks)
    w_joint = jnp.concatenate([w_query, w_key, w_value], axis=1)
    flat_tokens = token_row.reshape(-1, D)
    count = flat_tokens.shape[0]
    projected = jnp.dot(flat_tokens, w_joint, preferred_element_type=jnp.float32).astype(jnp.bfloat16)
    joint = projected.reshape(count, 3, D)
    context_tok, logsum = attend_rows((joint, segment_row, length_row))
    attended = jnp.dot(context_tok, w_output, preferred_element_type=jnp.float32)
    summed_one = flat_tokens.astype(jnp.float32) + attended
    hidden, norm_one_pull = jax.vjp(layer_norm, summed_one, gains[0], gains[1])
    hidden_half = hidden.astype(jnp.bfloat16)
    upward = jnp.dot(hidden_half, w_upward, preferred_element_type=jnp.float32)
    activated, gelu_pull = jax.vjp(exact_gelu, upward)
    active_half = activated.astype(jnp.bfloat16)
    downward = jnp.dot(active_half, w_downward, preferred_element_type=jnp.float32)
    result, norm_two_pull = jax.vjp(layer_norm, hidden + downward, gains[2], gains[3])
    block_row = result.astype(jnp.bfloat16)
    cotangent = grad_row.reshape(-1, D).astype(jnp.float32)
    delta_two, delta_gain_two, delta_shift_two = norm_two_pull(cotangent)
    delta_down = delta_two.astype(jnp.bfloat16)
    grad_down = contract_rows(active_half, delta_down)
    (delta_upward,) = gelu_pull(contract_cols(delta_down, w_downward))
    delta_up = delta_upward.astype(jnp.bfloat16)
    grad_up = contract_rows(hidden_half, delta_up)
    delta_hidden = delta_two + contract_cols(delta_up, w_upward)
    delta_one, delta_gain_one, delta_shift_one = norm_one_pull(delta_hidden)
    delta_attn = delta_one.astype(jnp.bfloat16)
    grad_output = contract_rows(context_tok, delta_attn)
    delta_context = contract_cols(delta_attn, w_output).astype(jnp.bfloat16)
    delta_joint = back_rows((joint, logsum, delta_context, segment_row, length_row)).reshape(-1, 3 * D)
    grad_joint = contract_rows(flat_tokens, delta_joint)
    input_row = (delta_one + contract_cols(delta_joint, w_joint)).astype(jnp.bfloat16)
    grad_blocks = jnp.concatenate(
        [
            into_blocks(grad_joint[:, :D]),
            into_blocks(grad_joint[:, D : 2 * D]),
            into_blocks(grad_joint[:, 2 * D :]),
            into_blocks(grad_output),
            into_blocks(grad_up),
            into_blocks(grad_down),
        ],
        axis=0,
    ).astype(jnp.bfloat16)
    vector_grad = jnp.concatenate([delta_gain_one, delta_shift_one, delta_gain_two, delta_shift_two])
    slot_index = jnp.arange(48, dtype=jnp.int32)
    placed = pick_blocks(grad_blocks, slot_index, owner_slot, 1, 0).astype(jnp.bfloat16)
    extra = jnp.broadcast_to(
        vector_grad.astype(jnp.bfloat16).reshape(8, 1, 1, BLK), (8, 6, 16, BLK)
    ).reshape(48, 16, BLK)
    placed = jnp.concatenate([placed, extra], axis=1)
    rows_of = lambda row: row.reshape(row_count, token_count, D)
    total, block_out, input_half = reduce_all(placed, rows_of(block_row), rows_of(input_row))
    owned = total[:, :BLK].astype(jnp.float32)
    vector_piece = total[0, BLK].astype(jnp.float32)
    moment_one, moment_two, left_new, right_new, weights_new = soap_update(
        owned, slot_weights, first_moment, second_moment, left_stats, right_stats, left_basis, right_basis
    )
    vector_one, vector_two, vector_new = adam_update(vector_piece, vector_values, vector_first, vector_second)
    return (
        block_out, input_half.astype(jnp.float32), moment_one, moment_two, left_new, right_new, weights_new,
        weights_new.astype(jnp.bfloat16), vector_one, vector_two, vector_new,
    )


def solution(mesh):
    in_specs = (
        P("dp", "sp", None),
        P("dp", "sp", None),
        P("dp", None),
        P("dp", None),
        P(),
        P("dp", None, None),
        P("dp", None, None),
        P("dp", None, None),
        P("dp", None, None),
        P("dp", None, None),
        P("dp", None, None),
        P("dp", None, None),
        P("dp"),
        P("dp"),
        P("dp"),
    )
    out_specs = (
        P("dp", "sp", None),
        P("dp", "sp", None),
        P("dp", None, None),
        P("dp", None, None),
        P("dp", None, None),
        P("dp", None, None),
        P("dp", None, None),
        P("dp", None, None),
        P("dp"),
        P("dp"),
        P("dp"),
    )
    chosen = fast_device if dict(mesh.shape) == {"dp": 8, "sp": 4} else per_device
    return jax.shard_map(
        chosen, mesh=mesh, in_specs=in_specs, out_specs=out_specs, check_vma=False
    )
```

```python
import math

import jax
import jax.numpy as jnp
from jax import lax
from jax.experimental import pallas as pl
from jax.experimental.pallas import tpu as pltpu
from jax.sharding import PartitionSpec as P

D = 768
HD = 64
FF = 3072
BLK = 384
STEP = 4


highest = lax.Precision.HIGHEST
rate_matrix = 0.04
rate_vector = 0.2


def layer_norm(summed, gain, shift):
    centre = jnp.mean(summed, axis=-1, keepdims=True)
    centred = summed - centre
    spread = jnp.mean(centred * centred, axis=-1, keepdims=True)
    return centred * lax.rsqrt(spread + 1e-06) * gain + shift


def exact_gelu(values):
    return jax.nn.gelu(values, approximate=False)


def passage_mask(segment_row, length_row):
    starts = jnp.cumsum(length_row) - length_row
    number = length_row.shape[0]
    onehot = (segment_row[:, None] == jnp.arange(number, dtype=jnp.int32)[None, :]).astype(
        jnp.int32
    )
    opening = jnp.sum(onehot * starts[None, :], axis=1)
    closing = opening + jnp.sum(onehot * length_row[None, :], axis=1)
    places = jnp.arange(segment_row.shape[0], dtype=jnp.int32)
    return (places[None, :] >= opening[:, None]) & (places[None, :] < closing[:, None])


def into_blocks(matrix):
    height, breadth = matrix.shape
    return (
        matrix.reshape(height // BLK, BLK, breadth // BLK, BLK)
        .transpose(0, 2, 1, 3)
        .reshape(-1, BLK, BLK)
    )


def from_blocks(blocks, height, breadth):
    return (
        blocks.reshape(height // BLK, breadth // BLK, BLK, BLK)
        .transpose(0, 2, 1, 3)
        .reshape(height, breadth)
    )


def split_blocks(blocks):
    square = (D // BLK) ** 2
    broad = D * FF // (BLK * BLK)
    w_query = from_blocks(blocks[0:square], D, D)
    w_key = from_blocks(blocks[square : 2 * square], D, D)
    w_value = from_blocks(blocks[2 * square : 3 * square], D, D)
    w_output = from_blocks(blocks[3 * square : 4 * square], D, D)
    w_upward = from_blocks(blocks[4 * square : 4 * square + broad], D, FF)
    w_downward = from_blocks(blocks[4 * square + broad : 4 * square + 2 * broad], FF, D)
    return (w_query, w_key, w_value, w_output, w_upward, w_downward)


def contract_rows(left_mat, right_mat):
    return lax.dot_general(
        left_mat, right_mat, (((0,), (0,)), ((), ())), preferred_element_type=jnp.float32
    )


def contract_cols(left_mat, right_mat):
    return lax.dot_general(
        left_mat, right_mat, (((1,), (1,)), ((), ())), preferred_element_type=jnp.float32
    )


def soap_update(
    gradient, weights, moment_old, second_old, left_old, right_old, left_rot, right_rot
):
    left_next = 0.95 * left_old + 0.05 * jnp.einsum(
        "nij,nkj->nik", gradient, gradient, precision=highest
    )
    right_next = 0.95 * right_old + 0.05 * jnp.einsum(
        "nji,njk->nik", gradient, gradient, precision=highest
    )
    turned = jnp.einsum("nji,njk->nik", left_rot, gradient, precision=highest)
    turned = jnp.einsum("nij,njk->nik", turned, right_rot, precision=highest)
    moment_next = 0.5 * moment_old + 0.5 * turned
    second_next = 0.5 * second_old + 0.5 * turned * turned
    correct = 1.0 - 0.5**STEP
    ratio = moment_next / correct / (jnp.sqrt(second_next / correct) + 1e-08)
    stepped = jnp.einsum("nij,njk->nik", left_rot, ratio, precision=highest)
    stepped = jnp.einsum("nij,nkj->nik", stepped, right_rot, precision=highest)
    return (moment_next, second_next, left_next, right_next, weights - rate_matrix * stepped)


def adam_update(gradient, values, moment_old, second_old):
    moment_next = 0.5 * moment_old + 0.5 * gradient
    second_next = 0.5 * second_old + 0.5 * gradient * gradient
    correct = 1.0 - 0.5**STEP
    ratio = moment_next / correct / (jnp.sqrt(second_next / correct) + 1e-08)
    return (moment_next, second_next, values - rate_vector * ratio)


def masked_scores(joint_row, segment_row, length_row):
    positions = joint_row.shape[0]
    query = joint_row[:, 0].reshape(positions, -1, HD)
    keyed = joint_row[:, 1].reshape(positions, -1, HD)
    valued = joint_row[:, 2].reshape(positions, -1, HD)
    scores = jnp.einsum("qhd,khd->hqk", query, keyed, preferred_element_type=jnp.float32) * 0.125
    visible = passage_mask(segment_row, length_row)
    return (jnp.where(visible[None], scores, -1e30), query, keyed, valued)


def attend_rows(item):
    joint_row, segment_row, length_row = item
    scores, query, keyed, valued = masked_scores(joint_row, segment_row, length_row)
    largest = jnp.max(scores, axis=-1, keepdims=True)
    raised = jnp.exp(scores - largest)
    totals = jnp.sum(raised, axis=-1, keepdims=True)
    probs = raised / totals
    logsum = (largest + jnp.log(totals))[..., 0]
    context = jnp.einsum(
        "hqk,khd->qhd", probs.astype(jnp.bfloat16), valued, preferred_element_type=jnp.float32
    )
    return (context.reshape(joint_row.shape[0], -1).astype(jnp.bfloat16), logsum)


def back_rows(item):
    joint_row, logsum, delta_context, segment_row, length_row = item
    positions = joint_row.shape[0]
    scores, query, keyed, valued = masked_scores(joint_row, segment_row, length_row)
    probs = jnp.exp(scores - logsum[..., None])
    delta_ctx = delta_context.reshape(positions, -1, HD)
    delta_value = jnp.einsum(
        "hqk,qhd->khd", probs.astype(jnp.bfloat16), delta_ctx, preferred_element_type=jnp.float32
    )
    delta_prob = jnp.einsum("qhd,khd->hqk", delta_ctx, valued, preferred_element_type=jnp.float32)
    weighted = jnp.sum(probs * delta_prob, axis=-1, keepdims=True)
    delta_score = (probs * (delta_prob - weighted)).astype(jnp.bfloat16)
    delta_query = (
        jnp.einsum("hqk,khd->qhd", delta_score, keyed, preferred_element_type=jnp.float32) * 0.125
    )
    delta_key = (
        jnp.einsum("hqk,qhd->khd", delta_score, query, preferred_element_type=jnp.float32) * 0.125
    )
    stacked = jnp.stack(
        [
            delta_query.reshape(positions, -1),
            delta_key.reshape(positions, -1),
            delta_value.reshape(positions, -1),
        ],
        axis=1,
    )
    return stacked.astype(jnp.bfloat16)


def pick_blocks(source, slot_index, owner_slot, fanout, part_index):
    matches = owner_slot[None, :] == slot_index[:, None]
    present = jnp.any(matches, axis=1).astype(jnp.float32)
    chosen = jnp.sum(
        matches.astype(jnp.int32) * jnp.arange(owner_slot.shape[0], dtype=jnp.int32)[None, :],
        axis=1,
    )
    picked = jnp.take(source, chosen * fanout + part_index, axis=0)
    return picked * present[:, None, None]


def per_device(
    tokens,
    output_grad,
    segment_ids,
    lengths,
    owner_slot,
    slot_weights,
    first_moment,
    second_moment,
    left_stats,
    right_stats,
    left_basis,
    right_basis,
    vector_values,
    vector_first,
    vector_second,
):
    holding = slot_weights.shape[0]
    row_count = tokens.shape[0]
    token_count = tokens.shape[1]
    gathered, vector_half = (
        lax.all_gather(slot_weights.astype(jnp.bfloat16), "dp", axis=0, tiled=True),
        lax.all_gather(vector_values.astype(jnp.bfloat16), "dp", axis=0, tiled=True),
    )
    blocks = jnp.take(gathered, owner_slot, axis=0)
    w_query, w_key, w_value, w_output, w_upward, w_downward = split_blocks(blocks)
    w_joint = jnp.concatenate([w_query, w_key, w_value], axis=1)
    gains = vector_half.astype(jnp.float32).reshape(4, D)
    flat_tokens = tokens.reshape(-1, D)
    projected = jnp.dot(flat_tokens, w_joint, preferred_element_type=jnp.float32).astype(
        jnp.bfloat16
    )
    projected = projected.reshape(row_count, token_count, 3, D)
    heads = lax.all_to_all(projected, "sp", split_axis=3, concat_axis=1, tiled=True)
    context, logsum = lax.map(attend_rows, (heads, segment_ids, lengths))
    context_tok = lax.all_to_all(context, "sp", split_axis=1, concat_axis=2, tiled=True).reshape(
        -1, D
    )
    attended = jnp.dot(context_tok, w_output, preferred_element_type=jnp.float32)
    summed_one = flat_tokens.astype(jnp.float32) + attended
    hidden, norm_one_pull = jax.vjp(layer_norm, summed_one, gains[0], gains[1])
    hidden_half = hidden.astype(jnp.bfloat16)
    upward = jnp.dot(hidden_half, w_upward, preferred_element_type=jnp.float32)
    activated, gelu_pull = jax.vjp(exact_gelu, upward)
    active_half = activated.astype(jnp.bfloat16)
    downward = jnp.dot(active_half, w_downward, preferred_element_type=jnp.float32)
    result, norm_two_pull = jax.vjp(layer_norm, hidden + downward, gains[2], gains[3])
    block_out = result.astype(jnp.bfloat16).reshape(row_count, token_count, D)
    cotangent = output_grad.reshape(-1, D).astype(jnp.float32)
    delta_two, delta_gain_two, delta_shift_two = norm_two_pull(cotangent)
    delta_down = delta_two.astype(jnp.bfloat16)
    grad_down = contract_rows(active_half, delta_down)
    delta_active = contract_cols(delta_down, w_downward)
    (delta_upward,) = gelu_pull(delta_active)
    delta_up = delta_upward.astype(jnp.bfloat16)
    grad_up = contract_rows(hidden_half, delta_up)
    delta_hidden = delta_two + contract_cols(delta_up, w_upward)
    delta_one, delta_gain_one, delta_shift_one = norm_one_pull(delta_hidden)
    delta_attn = delta_one.astype(jnp.bfloat16)
    grad_output = contract_rows(context_tok, delta_attn)
    delta_context = (
        contract_cols(delta_attn, w_output).astype(jnp.bfloat16).reshape(row_count, token_count, D)
    )
    delta_heads = lax.all_to_all(delta_context, "sp", split_axis=2, concat_axis=1, tiled=True)
    delta_projected = lax.map(back_rows, (heads, logsum, delta_heads, segment_ids, lengths))
    delta_joint = lax.all_to_all(
        delta_projected, "sp", split_axis=1, concat_axis=3, tiled=True
    ).reshape(-1, 3 * D)
    grad_joint = contract_rows(flat_tokens, delta_joint)
    input_grad = (delta_one + contract_cols(delta_joint, w_joint)).reshape(
        row_count, token_count, D
    )
    grad_blocks = jnp.concatenate(
        [
            into_blocks(grad_joint[:, :D]),
            into_blocks(grad_joint[:, D : 2 * D]),
            into_blocks(grad_joint[:, 2 * D :]),
            into_blocks(grad_output),
            into_blocks(grad_up),
            into_blocks(grad_down),
        ],
        axis=0,
    )
    vector_grad = jnp.concatenate(
        [delta_gain_one, delta_shift_one, delta_gain_two, delta_shift_two]
    )
    vector_total = lax.psum(vector_grad, ("dp", "sp"))
    piece_len = vector_values.shape[0]
    vector_piece = lax.dynamic_slice_in_dim(
        vector_total, lax.axis_index("dp") * piece_len, piece_len
    )
    slot_index = jnp.arange(holding * lax.axis_size("dp"), dtype=jnp.int32)
    owned = lax.psum_scatter(
        pick_blocks(grad_blocks, slot_index, owner_slot, 1, 0),
        "dp",
        scatter_dimension=0,
        tiled=True,
    )
    owned = lax.psum(owned.astype(jnp.bfloat16), "sp").astype(jnp.float32)
    moment_one, moment_two, left_new, right_new, weights_new = soap_update(
        owned,
        slot_weights,
        first_moment,
        second_moment,
        left_stats,
        right_stats,
        left_basis,
        right_basis,
    )
    vector_one, vector_two, vector_new = adam_update(
        vector_piece, vector_values, vector_first, vector_second
    )
    return (
        block_out,
        input_grad,
        moment_one,
        moment_two,
        left_new,
        right_new,
        weights_new,
        weights_new.astype(jnp.bfloat16),
        vector_one,
        vector_two,
        vector_new,
    )


PITCH = BLK + 16
MESH = pl.DeviceIdType.MESH
NZ = 4


def in_hbm(value):
    return pltpu.with_memory_space_constraint(value, pltpu.HBM)


def place():
    dp = lax.axis_index("dp")
    sp = lax.axis_index("sp")
    return dp // 2, dp % 2, sp // 2, sp % 2


def greet(z, y, x, c):
    barrier = pltpu.get_barrier_semaphore()
    dp = z * 2 + y
    sp = x * 2 + c

    def signal(target):
        pl.semaphore_signal(barrier, 1, device_id=target, device_id_type=MESH)

    for step in range(1, 4):
        signal((dp, (sp + step) % 4))
    signal((z * 2 + 1 - y, sp))

    @pl.when(z < NZ - 1)
    def _():
        signal((dp + 2, sp))

    @pl.when(z > 0)
    def _():
        signal((dp - 2, sp))

    pl.semaphore_wait(barrier, 4 + (z < NZ - 1).astype(jnp.int32) + (z > 0).astype(jnp.int32))


def gather_kernel(
    weights, vector, tokens, grads, out, token_row, grad_row,
    wide, narrow, load_sem, keep_sem, send_sem, recv_sem, row_send, row_recv, row_keep,
):
    z, y, x, c = place()
    dp = z * 2 + y
    sp = x * 2 + c
    loads = [pltpu.make_async_copy(weights.at[i], wide.at[i], load_sem.at[i]) for i in range(6)]
    for load in loads:
        load.start()
    keeps = [
        pltpu.make_async_copy(tokens.at[sp], token_row.at[sp], row_keep.at[0]),
        pltpu.make_async_copy(grads.at[sp], grad_row.at[sp], row_keep.at[1]),
    ]
    for keep in keeps:
        keep.start()
    gains = jnp.broadcast_to(vector[...], (16, BLK)).astype(jnp.bfloat16)
    greet(z, y, x, c)

    def rows_copy(which, source, landing, step):
        peer = (sp + step) % 4
        return pltpu.make_async_remote_copy(
            src_ref=source.at[peer], dst_ref=landing.at[sp],
            send_sem=row_send.at[which, step - 1], recv_sem=row_recv.at[which, sp],
            device_id=(dp, peer), device_id_type=MESH,
        )

    def rows_arrival(which, source, landing, step):
        peer = (sp + step) % 4
        return pltpu.make_async_remote_copy(
            src_ref=source.at[peer], dst_ref=landing.at[peer],
            send_sem=row_send.at[which, step - 1], recv_sem=row_recv.at[which, peer],
            device_id=(dp, peer), device_id_type=MESH,
        )

    for step in (2, 3, 1):
        rows_copy(0, tokens, token_row, step).start()

    for i in range(6):
        loads[i].wait()
        narrow[i, :BLK, :] = wide[i].astype(jnp.bfloat16)
        narrow[i, BLK:, :] = gains
    own = [pltpu.make_async_copy(narrow.at[i], out.at[dp * 6 + i], keep_sem.at[i]) for i in range(6)]

    def piece(part):
        return (c, BLK + 16) if part == 0 else (2 + 2 * x + c, BLK)

    targets = {
        "up": (dp + 2, sp), "down": (dp - 2, sp), "y": (z * 2 + 1 - y, sp),
        "x": (dp, (1 - x) * 2 + c), "core": (dp, x * 2 + 1 - c),
    }
    number = {"up": 0, "down": 1, "y": 2, "x": 3, "core": 4}

    def copy(way, holder, slot, height, index, source=None):
        at = holder * 6 + slot
        src = out.at[at, pl.ds(0, height)] if source is None else source
        return pltpu.make_async_remote_copy(
            src_ref=src, dst_ref=out.at[at, pl.ds(0, height)],
            send_sem=send_sem.at[number[way], index], recv_sem=recv_sem.at[at],
            device_id=targets[way], device_id_type=MESH,
        )

    started = []

    def start(way, holder, slot, height, index, valid=None, source=None):
        item = copy(way, holder, slot, height, index, source)
        if valid is None:
            item.start()
        else:
            pl.when(valid)(item.start)
        started.append((item, valid))

    def arrive(holder, slot, height, valid=None):
        item = copy("core", holder, slot, height, 0)
        if valid is None:
            item.wait_recv()
        else:
            pl.when(valid)(item.wait_recv)

    counts = {}

    def fresh(way):
        counts[way] = counts.get(way, -1) + 1
        return counts[way]

    for part in (1, 0):
        slot, height = piece(part)
        src = narrow.at[slot, pl.ds(0, height)]
        start("up", dp, slot, height, fresh("up"), z < NZ - 1, src)
        start("down", dp, slot, height, fresh("down"), z > 0, src)
        start("y", dp, slot, height, fresh("y"), None, src)
    for item in own:
        item.start()

    def from_z(sign, far, part):
        origin = z + sign * far
        inside = (origin >= 0) if sign < 0 else (origin <= NZ - 1)
        holder = origin * 2 + y
        slot, height = piece(part)
        arrive(holder, slot, height, inside)
        if far < NZ - 1:
            if sign < 0:
                start("up", holder, slot, height, fresh("up"), inside & (z < NZ - 1))
            else:
                start("down", holder, slot, height, fresh("down"), inside & (z > 0))
        start("y", holder, slot, height, fresh("y"), inside)
        if part == 1:
            start("x", holder, slot, height, fresh("x"), inside)
        start("core", holder, slot, height, fresh("core"), inside)

    def signs(far):
        return (0,) if far == 0 else (-1, 1)

    def valid_of(sign, far):
        origin = z + sign * far
        if far == 0:
            return origin, None
        return origin, ((origin >= 0) if sign < 0 else (origin <= NZ - 1))

    def from_y(sign, far, part):
        origin, inside = valid_of(sign, far)
        holder = origin * 2 + 1 - y
        slot, height = piece(part)
        arrive(holder, slot, height, inside)
        if part == 1:
            start("x", holder, slot, height, fresh("x"), inside)
        start("core", holder, slot, height, fresh("core"), inside)

    def from_x(sign, far, side):
        origin, inside = valid_of(sign, far)
        holder = origin * 2 + (y if side == 0 else 1 - y)
        slot = 2 + 2 * (1 - x) + c
        arrive(holder, slot, BLK, inside)
        start("core", holder, slot, BLK, fresh("core"), inside)

    for far in range(1, NZ):
        for part in (1, 0):
            for sign in (-1, 1):
                from_z(sign, far, part)
            for sign in signs(far - 1):
                from_y(sign, far - 1, part)
        if far == 1:
            for step in (2, 3, 1):
                rows_copy(1, grads, grad_row, step).start()
        if far >= 2:
            for sign in signs(far - 1):
                from_x(sign, far - 1, 0)
            for sign in signs(far - 2):
                from_x(sign, far - 2, 1)
    for part in (1, 0):
        for sign in (-1, 1):
            from_y(sign, NZ - 1, part)
    for sign in (-1, 1):
        from_x(sign, NZ - 1, 0)
    for far in (NZ - 2, NZ - 1):
        for sign in signs(far):
            from_x(sign, far, 1)

    for far in range(NZ):
        for sign in signs(far):
            origin, inside = valid_of(sign, far)
            for side in (0, 1):
                if far == 0 and side == 0:
                    continue
                holder = origin * 2 + (y if side == 0 else 1 - y)
                for slot, height in ((1 - c, BLK + 16), (3 - c, BLK), (5 - c, BLK)):
                    arrive(holder, slot, height, inside)
    for step in (2, 3, 1):
        rows_arrival(0, tokens, token_row, step).wait_recv()
        rows_arrival(1, grads, grad_row, step).wait_recv()
        rows_copy(0, tokens, token_row, step).wait_send()
        rows_copy(1, grads, grad_row, step).wait_send()
    for item, valid in started:
        if valid is None:
            item.wait_send()
        else:
            pl.when(valid)(item.wait_send)
    for item in own + keeps:
        item.wait()


def gather_all(weights, vector, tokens, grads):
    anywhere = pl.BlockSpec(memory_space=pltpu.HBM)
    return pl.pallas_call(
        gather_kernel,
        name="gather_all",
        out_shape=[
            pltpu.HBM((48, PITCH, BLK), jnp.bfloat16),
            pltpu.HBM(tokens.shape, jnp.bfloat16),
            pltpu.HBM(grads.shape, jnp.bfloat16),
        ],
        in_specs=[anywhere, pl.BlockSpec(memory_space=pltpu.VMEM), anywhere, anywhere],
        out_specs=[anywhere, anywhere, anywhere],
        scratch_shapes=[
            pltpu.VMEM((6, BLK, BLK), jnp.float32),
            pltpu.VMEM((6, PITCH, BLK), jnp.bfloat16),
            pltpu.SemaphoreType.DMA((6,)),
            pltpu.SemaphoreType.DMA((6,)),
            pltpu.SemaphoreType.DMA((5, 40)),
            pltpu.SemaphoreType.DMA((48,)),
            pltpu.SemaphoreType.DMA((2, 3)),
            pltpu.SemaphoreType.DMA((2, 4)),
            pltpu.SemaphoreType.DMA((2,)),
        ],
        compiler_params=pltpu.CompilerParams(
            collective_id=0, has_side_effects=True, vmem_limit_bytes=24 << 20
        ),
    )(in_hbm(weights), vector.reshape(1, BLK), in_hbm(tokens), in_hbm(grads))


ROW = 512
PAIR = 128
SPAN = 384
EPS = 1e-06


def erf_of(x):
    x = jnp.clip(x, -3.832506856900711, 3.832506856900711)
    s = x * x
    top = 0.00022905065861350646
    for term in (0.0034082910107109506, 0.050955695062380861, 0.18520832239976145, 1.128379143519084):
        top = top * s + term
    bottom = -1.1791602954361697e-7
    for term in (0.000023547966471313185, 0.0010179625278914885, 0.014070470171167667,
                 0.11098505178285362, 0.49746925110067538, 1.0):
        bottom = bottom * s + term
    return x * top / bottom


def dot_nn(a, b):
    return lax.dot_general(a, b, (((1,), (0,)), ((), ())), preferred_element_type=jnp.float32)


def dot_nt(a, b):
    return lax.dot_general(a, b, (((1,), (1,)), ((), ())), preferred_element_type=jnp.float32)


def dot_tn(a, b):
    return lax.dot_general(a, b, (((0,), (0,)), ((), ())), preferred_element_type=jnp.float32)


def layer_kernel(
    owner, weights, tokens, dy_ref, segments, grads, block_out, input_half,
    wqkv, wo, w1, w2, gains, qkv, probs, context, hidden, hidden16, norm1, act, slope, acc, dz, dz16,
    dqkv, dup, stage, vecs, spread, w_sem, g_sem, v_sem,
):
    half = jnp.bfloat16
    sp = lax.axis_index("sp")

    def weight_copies():
        copies = []
        for which, ref in enumerate((wqkv.at[0], wqkv.at[1], wqkv.at[2], wo)):
            for r in range(2):
                for q in range(2):
                    copies.append((which * 4 + r * 2 + q, ref, r, q))
        for r in range(2):
            for q in range(8):
                copies.append((16 + r * 8 + q, w1.at[q // 2], r, q % 2))
        for r in range(8):
            for q in range(2):
                copies.append((32 + r * 2 + q, w2.at[r // 2], r % 2, q))
        return [
            pltpu.make_async_copy(
                weights.at[owner[b], pl.ds(0, BLK)],
                ref.at[pl.ds(r * BLK, BLK), pl.ds(q * BLK, BLK)],
                w_sem.at[b],
            )
            for b, ref, r, q in copies
        ]

    copies = weight_copies()
    gain_copies = [
        pltpu.make_async_copy(
            weights.at[6 * d, pl.ds(BLK, 16)], gains.at[d // 2, :, pl.ds((d % 2) * BLK, BLK)], g_sem.at[d]
        )
        for d in range(8)
    ]
    for item in copies[:16] + gain_copies + copies[16:]:
        item.start()

    seg_row = segments[pl.ds(sp, 1), :].astype(jnp.float32)
    spread[...] = jnp.transpose(jnp.broadcast_to(seg_row, (PAIR, ROW)))

    for item in copies[:12]:
        item.wait()
    x = tokens[...]
    for part in range(3):
        block = dot_nn(x, wqkv[part])
        if part == 0:
            block = block * 0.125
        block = block.astype(half)
        for p in range(6):
            qkv[part * 6 + p] = block[:, p * PAIR : (p + 1) * PAIR]

    lane = lax.broadcasted_iota(jnp.int32, (1, PAIR), 1)
    lows = (lane < 64, lane >= 64)

    def visible(part):
        keys = segments[pl.ds(sp, 1), pl.ds(part * PAIR, SPAN)].astype(jnp.float32)
        own = spread[pl.ds(part * 256, 256), pl.ds(0, 1)]
        return own == keys

    def attend(p, carry):
        q2, k2, v2 = qkv[p], qkv[6 + p], qkv[12 + p]
        for part in range(2):
            mask = visible(part)
            qs = q2[part * 256 : part * 256 + 256]
            ks = k2[part * PAIR : part * PAIR + SPAN]
            vs = v2[part * PAIR : part * PAIR + SPAN]
            outs = []
            for h in range(2):
                scores = dot_nt(jnp.where(lows[h], qs, jnp.zeros_like(qs)), ks)
                scores = jnp.where(mask, scores, -1e30)
                top = jnp.max(scores, axis=1, keepdims=True)
                raised = jnp.exp(scores - top)
                prob = raised * (1.0 / jnp.sum(raised, axis=1, keepdims=True))
                probs[p, 2 * part + h] = prob
                outs.append(dot_nn(prob.astype(half), vs))
            context[p, pl.ds(part * 256, 256)] = jnp.where(lows[0], outs[0], outs[1]).astype(half)
        return carry

    lax.fori_loop(0, 6, attend, 0)

    for item in copies[12:16] + gain_copies:
        item.wait()
    joined = jnp.concatenate([context[p] for p in range(6)], axis=1)

    def gain(k):
        return gains[k, pl.ds(0, 1), :].astype(jnp.float32)

    def normalise(z):
        centre = jnp.mean(z, axis=1, keepdims=True)
        z = z - centre
        inverse = lax.rsqrt(jnp.mean(z * z, axis=1, keepdims=True) + EPS)
        return z * inverse, inverse

    acc[...] = dot_nn(joined, wo[...])

    def norm_one(t, carry):
        rows = pl.ds(pl.multiple_of(t * 64, 64), 64)
        hat, inverse = normalise(tokens[rows, :].astype(jnp.float32) + acc[rows, :])
        norm1[rows, :] = hat
        spread[rows, :] = jnp.where(lane == 1, inverse, spread[rows, :])
        value = hat * gain(0) + gain(1)
        hidden[rows, :] = value
        hidden16[rows, :] = value.astype(half)
        return carry

    lax.fori_loop(0, 8, norm_one, 0)
    for item in copies[16:]:
        item.wait()

    def forward(j, carry):
        up = dot_nn(hidden16[...], w1[j])
        phi_big = 0.5 + 0.5 * erf_of(up * (1.0 / math.sqrt(2.0)))
        value = (up * phi_big).astype(half)
        slope[j] = phi_big + up * (jnp.exp(-0.5 * up * up) * (1.0 / math.sqrt(2.0 * math.pi)))
        act[j] = value
        part = dot_nn(value, w2[j])
        hidden[...] += part
        return carry

    lax.fori_loop(0, 4, forward, 0)

    vecs[...] = jnp.zeros_like(vecs)

    def fold(value):
        return jnp.sum(value.reshape(-1, 8, D), axis=0)

    def norm_back(hat, inverse, delta, gain_row):
        e = delta * gain_row
        return (
            e - jnp.mean(e, axis=1, keepdims=True) - hat * jnp.mean(e * hat, axis=1, keepdims=True)
        ) * inverse

    def norm_two(t, carry):
        rows = pl.ds(pl.multiple_of(t * 64, 64), 64)
        hat, inverse = normalise(hidden[rows, :])
        block_out[rows, :] = (hat * gain(2) + gain(3)).astype(half)
        delta = dy_ref[rows, :].astype(jnp.float32)
        vecs[2] += fold(delta * hat)
        vecs[3] += fold(delta)
        back = norm_back(hat, inverse, delta, gain(2))
        dz[rows, :] = back
        dz16[rows, :] = back.astype(half)
        return carry

    lax.fori_loop(0, 8, norm_two, 0)

    def out_copy(slot, b, r, q):
        return pltpu.make_async_copy(
            stage.at[slot, pl.ds(r * BLK, BLK), pl.ds(q * BLK, BLK)],
            grads.at[owner[b], pl.ds(0, BLK)],
            v_sem.at[slot, r * 2 + q],
        )

    def flush(slot, blocks):
        for r in range(2):
            for q in range(2):
                out_copy(slot, blocks(r, q), r, q).start()

    def drain(slot):
        for r in range(2):
            for q in range(2):
                out_copy(slot, 0, r, q).wait()

    def backward(j, carry):
        ddown = dz16[...]
        delta = (dot_nt(ddown, w2[j]) * slope[j]).astype(half)

        @pl.when(j >= 2)
        def _():
            drain(2 * (j % 2))
            drain(2 * (j % 2) + 1)

        stage[2 * (j % 2)] = dot_tn(act[j], ddown).astype(half)
        flush(2 * (j % 2), lambda r, q: 32 + (2 * j + r) * 2 + q)
        stage[2 * (j % 2) + 1] = dot_tn(hidden16[...], delta).astype(half)
        flush(2 * (j % 2) + 1, lambda r, q: 16 + r * 8 + 2 * j + q)
        dz[...] += dot_nt(delta, w1[j])
        return carry

    lax.fori_loop(0, 4, backward, 0)

    def norm_one_back(t, carry):
        rows = pl.ds(pl.multiple_of(t * 64, 64), 64)
        hat = norm1[rows, :]
        delta = dz[rows, :]
        vecs[0] += fold(delta * hat)
        vecs[1] += fold(delta)
        back = norm_back(hat, spread[rows, pl.ds(1, 1)], delta, gain(0))
        dz[rows, :] = back
        dz16[rows, :] = back.astype(half)
        return carry

    lax.fori_loop(0, 8, norm_one_back, 0)

    for slot in range(4):
        drain(slot)
    dattn = dz16[...]
    stage[0] = dot_tn(joined, dattn).astype(half)
    flush(0, lambda r, q: 12 + r * 2 + q)
    dcontext = dot_nt(dattn, wo[...]).astype(half)
    for p in range(6):
        context[p] = dcontext[:, p * PAIR : (p + 1) * PAIR]

    def attend_back(p, carry):
        q2, k2, v2, d2 = qkv[p], qkv[6 + p], qkv[12 + p], context[p]
        dup[...] = jnp.zeros_like(dup)
        for part in range(2):
            window = pl.ds(part * PAIR, SPAN)
            qs = q2[part * 256 : part * 256 + 256]
            ds = d2[part * 256 : part * 256 + 256]
            ks = k2[part * PAIR : part * PAIR + SPAN]
            vs = v2[part * PAIR : part * PAIR + SPAN]
            dvs, dqs, dks = [], [], []
            for h in range(2):
                prob = probs[p, 2 * part + h]
                dprob = dot_nt(jnp.where(lows[h], ds, jnp.zeros_like(ds)), vs)
                product = prob * dprob
                dscore = (product - prob * jnp.sum(product, axis=1, keepdims=True)).astype(half)
                dvs.append(dot_tn(prob.astype(half), ds))
                dqs.append(dot_nn(dscore, ks))
                dks.append(dot_tn(dscore, qs))
            dqkv[p, pl.ds(part * 256, 256)] = (
                jnp.where(lows[0], dqs[0], dqs[1]) * 0.125
            ).astype(half)
            dup[0, window] += jnp.where(lows[0], dks[0], dks[1])
            dup[1, window] += jnp.where(lows[0], dvs[0], dvs[1])
        dqkv[6 + p] = dup[0].astype(half)
        dqkv[12 + p] = dup[1].astype(half)
        return carry

    lax.fori_loop(0, 6, attend_back, 0)

    for part in range(3):
        delta = jnp.concatenate([dqkv[part * 6 + p] for p in range(6)], axis=1)
        stage[1 + part] = dot_tn(x, delta).astype(half)
        flush(1 + part, lambda r, q: part * 4 + r * 2 + q)
        dz[...] += dot_nt(delta, wqkv[part])

    input_half[...] = dz[...].astype(half)
    for k in range(4):
        row = jnp.sum(vecs[k], axis=0, keepdims=True)
        vecs16 = jnp.broadcast_to(row, (16, D)).astype(half)
        gains[k] = vecs16
    for k in range(4):
        for q in range(2):
            for s in range(2):
                pltpu.make_async_copy(
                    gains.at[k, :, pl.ds(q * BLK, BLK)],
                    grads.at[6 * (2 * k + q) + s, pl.ds(BLK, 16)],
                    w_sem.at[(2 * k + q) * 2 + s],
                ).start()
    for k in range(4):
        for q in range(2):
            for s in range(2):
                pltpu.make_async_copy(
                    gains.at[k, :, pl.ds(q * BLK, BLK)],
                    grads.at[6 * (2 * k + q) + s, pl.ds(BLK, 16)],
                    w_sem.at[(2 * k + q) * 2 + s],
                ).wait()
    for slot in range(4):
        drain(slot)


def run_layer(owner_slot, gathered, token_row, grad_row, segment_ids):
    half, full = jnp.bfloat16, jnp.float32
    anywhere = pl.BlockSpec(memory_space=pltpu.HBM)
    vmem = pl.BlockSpec(memory_space=pltpu.VMEM)
    dma = pltpu.SemaphoreType.DMA
    return pl.pallas_call(
        layer_kernel,
        name="run_layer",
        out_shape=[
            jax.ShapeDtypeStruct((48, PITCH, BLK), half),
            jax.ShapeDtypeStruct((ROW, D), half),
            jax.ShapeDtypeStruct((ROW, D), half),
        ],
        in_specs=[pl.BlockSpec(memory_space=pltpu.SMEM), anywhere, vmem, vmem, vmem],
        out_specs=[anywhere, vmem, vmem],
        scratch_shapes=[
            pltpu.VMEM((3, D, D), half),
            pltpu.VMEM((D, D), half),
            pltpu.VMEM((4, D, D), half),
            pltpu.VMEM((4, D, D), half),
            pltpu.VMEM((4, 16, D), half),
            pltpu.VMEM((18, ROW, PAIR), half),
            pltpu.VMEM((6, 4, 256, SPAN), full),
            pltpu.VMEM((6, ROW, PAIR), half),
            pltpu.VMEM((ROW, D), full),
            pltpu.VMEM((ROW, D), half),
            pltpu.VMEM((ROW, D), full),
            pltpu.VMEM((4, ROW, D), half),
            pltpu.VMEM((4, ROW, D), full),
            pltpu.VMEM((ROW, D), full),
            pltpu.VMEM((ROW, D), full),
            pltpu.VMEM((ROW, D), half),
            pltpu.VMEM((18, ROW, PAIR), half),
            pltpu.VMEM((2, ROW, PAIR), full),
            pltpu.VMEM((4, D, D), half),
            pltpu.VMEM((4, 8, D), full),
            pltpu.VMEM((ROW, PAIR), full),
            dma((48,)),
            dma((8,)),
            dma((4, 4)),
        ],
        compiler_params=pltpu.CompilerParams(vmem_limit_bytes=62 << 20),
    )(owner_slot, gathered, token_row, grad_row, segment_ids)


BLANK = BLK + 16
HALF = BLK // 2


def reduce_kernel(
    grads, rows_a, rows_b, total, land_a, land_b,
    mine0, mine1, mine2, mine3, core0, core1, core2, core3, cross, side0, side1, side2,
    line0, line1, line2, last0, last1,
    load_sem, core_send, core_recv, x_send, x_recv, y_send, y_recv, z_send, z_recv,
    last_send, last_recv, give_send, give_recv, keep_sem, row_send, row_recv, row_keep,
):
    z, y, x, c = place()
    dp = z * 2 + y
    sp = x * 2 + c
    mine = (mine0, mine1, mine2, mine3)
    core = (core0, core1, core2, core3)
    side = (side0, side1, side2)
    line = (line0, line1, line2)
    last = (last0, last1)
    high = z // 2
    order = (3 - 3 * high, 2 - high, 1 - z + 4 * high, z)
    twin = (dp, (1 - x) * 2 + c)
    mate = (dp, x * 2 + 1 - c)
    beside = (z * 2 + 1 - y, sp)
    inner = (z > 0) & (z < NZ - 1)

    def view(ref, stream, dest, core_of):
        base = dest * 6
        if stream == 0:
            return ref.at[base + core_of, pl.ds(0, BLANK)]
        if stream == 1:
            return ref.at[base + 2 + core_of, pl.ds(0, BLK)]
        slot = base + (4 + x if stream == 2 else 5 - x)
        return ref.at[slot, pl.ds(pl.multiple_of(core_of * HALF, HALF), HALF)]

    def remote(src, dst, send, recv, target):
        return pltpu.make_async_remote_copy(
            src_ref=src, dst_ref=dst, send_sem=send, recv_sem=recv,
            device_id=target, device_id_type=MESH,
        )

    def load(stream, dest):
        return pltpu.make_async_copy(
            view(grads, stream, dest, c), mine[stream].at[dest], load_sem.at[stream, dest]
        )

    def to_mate(stream, dest):
        return remote(
            view(grads, stream, dest, 1 - c), core[stream].at[dest],
            core_send.at[stream, dest], core_recv.at[stream, dest], mate,
        )

    def to_twin(dest):
        return remote(mine3.at[dest], cross.at[dest], x_send.at[dest], x_recv.at[dest], twin)

    def to_side(stream, goal):
        dest = goal * 2 + 1 - y
        return remote(
            mine[stream].at[dest], side[stream].at[goal],
            y_send.at[stream, goal], y_recv.at[stream, goal], beside,
        )

    def row_copy(which, source, landing, step, arrival):
        peer = (sp + step) % 4
        at = peer if arrival else sp
        return remote(
            source.at[peer], landing.at[at],
            row_send.at[which, step - 1], row_recv.at[which, at], (dp, peer),
        )

    sequence = []
    for i in range(4):
        away = order[i] * 2 + 1 - y
        sequence += [(3, away), (0, away), (1, away)]
    for i in range(4):
        sequence += [(3, order[i] * 2 + y)]
    for i in range(4):
        sequence += [(2, order[i] * 2 + 1 - y)]
    for i in range(4):
        home = order[i] * 2 + y
        sequence += [(0, home), (1, home)]
    for i in range(4):
        sequence += [(2, order[i] * 2 + y)]
    for stream, dest in sequence:
        load(stream, dest).start()
    keeps = [
        pltpu.make_async_copy(rows_a.at[sp], land_a.at[sp], row_keep.at[0]),
        pltpu.make_async_copy(rows_b.at[sp], land_b.at[sp], row_keep.at[1]),
    ]
    for keep in keeps:
        keep.start()
    greet(z, y, x, c)
    for stream, dest in sequence:
        to_mate(stream, dest).start()

    def merge(stream, dest):
        load(stream, dest).wait()
        to_mate(stream, dest).wait_recv()
        mine[stream][dest] = mine[stream][dest] + core[stream][dest]

    def along(stream, goal):
        dest = goal * 2 + y
        upward = (goal > z).astype(jnp.int32)
        step = 2 * upward - 1
        way = 1 - upward
        item = remote(
            mine[stream].at[dest], line[stream].at[way, goal],
            z_send.at[stream, goal], z_recv.at[stream, way, goal], (dp + 2 * step, sp),
        )

        @pl.when(inner)
        def _():
            item.wait_recv()
            mine[stream][dest] = mine[stream][dest] + line[stream][way, goal]

        item.start()

    def settle(stream):
        for way, valid, step in ((0, z > 0, 1), (1, z < NZ - 1, -1)):
            @pl.when(valid)
            def _():
                remote(
                    mine[stream].at[dp], line[stream].at[way, z],
                    z_send.at[stream, z], z_recv.at[stream, way, z], (dp - 2 * step, sp),
                ).wait_recv()
                mine[stream][dp] = mine[stream][dp] + line[stream][way, z]

    for i in range(4):
        away = order[i] * 2 + 1 - y
        merge(3, away)
        to_twin(away).start()
        for stream in (0, 1):
            merge(stream, away)
            to_side(stream, order[i]).start()
    for i in range(4):
        home = order[i] * 2 + y
        merge(3, home)
        to_twin(home).start()
    for step in (2, 3, 1):
        row_copy(0, rows_a, land_a, step, False).start()
    for i in range(4):
        away = order[i] * 2 + 1 - y
        merge(2, away)
        to_twin(away).wait_recv()
        mine2[away] = mine2[away] + cross[away]
        to_side(2, order[i]).start()
        home = order[i] * 2 + y
        for stream in (0, 1):
            merge(stream, home)
            to_side(stream, order[i]).wait_recv()
            mine[stream][home] = mine[stream][home] + side[stream][order[i]]
            if i < 3:
                along(stream, order[i])
    for step in (2, 3, 1):
        row_copy(1, rows_b, land_b, step, False).start()
    for i in range(4):
        home = order[i] * 2 + y
        merge(2, home)
        to_twin(home).wait_recv()
        mine2[home] = mine2[home] + cross[home]
        to_side(2, order[i]).wait_recv()
        mine2[home] = mine2[home] + side2[order[i]]
        if i < 3:
            along(2, order[i])

    def swap_last(stream):
        return remote(
            mine[stream].at[dp], last[stream], last_send.at[stream], last_recv.at[stream], twin
        )

    for stream in (0, 1):
        settle(stream)
        swap_last(stream).start()
    settle(2)

    def place_of(stream, core_of):
        return view(total, stream, 0, core_of)

    def give(stream, index, target, source, core_of):
        return remote(
            source, place_of(stream, core_of), give_send.at[index], give_recv.at[index], target
        )

    own_twin = give(2, 0, twin, mine2.at[dp], c)
    own_twin.start()
    own_mate = give(2, 1, mate, mine2.at[dp], c)
    own_mate.start()
    kept = [pltpu.make_async_copy(mine2.at[dp], place_of(2, c), keep_sem.at[2])]
    kept[0].start()
    gifts = [own_twin, own_mate]
    for stream in (0, 1):
        swap_last(stream).wait_recv()
        core[stream][dp] = mine[stream][dp] + last[stream][...]
        gift = give(stream, 2 + stream, mate, core[stream].at[dp], c)
        gift.start()
        gifts.append(gift)
        keep = pltpu.make_async_copy(core[stream].at[dp], place_of(stream, c), keep_sem.at[stream])
        keep.start()
        kept.append(keep)
    give(3, 0, twin, place_of(3, c), c).wait_recv()
    passed = give(3, 4, mate, place_of(3, c), c)
    passed.start()
    gifts.append(passed)
    for stream, index in ((2, 1), (0, 2), (1, 3), (3, 4)):
        give(stream, index, mate, place_of(stream, 1 - c), 1 - c).wait_recv()
    for step in (2, 3, 1):
        for which, source, landing in ((0, rows_a, land_a), (1, rows_b, land_b)):
            row_copy(which, source, landing, step, True).wait_recv()
            row_copy(which, source, landing, step, False).wait_send()
    for stream, dest in sequence:
        to_mate(stream, dest).wait_send()
    for i in range(4):
        for side_of in (0, 1):
            to_twin(order[i] * 2 + side_of).wait_send()
        for stream in range(3):
            to_side(stream, order[i]).wait_send()
            if i < 3:
                remote(
                    mine[stream].at[order[i] * 2 + y], line[stream].at[0, order[i]],
                    z_send.at[stream, order[i]], z_recv.at[stream, 0, order[i]], twin,
                ).wait_send()
    for stream in (0, 1):
        swap_last(stream).wait_send()
    for item in gifts:
        item.wait_send()
    for item in kept + keeps:
        item.wait()


def reduce_all(grads, rows_a, rows_b):
    anywhere = pl.BlockSpec(memory_space=pltpu.HBM)
    half = jnp.bfloat16
    heights = (BLANK, BLK, HALF, HALF)
    dma = pltpu.SemaphoreType.DMA
    return pl.pallas_call(
        reduce_kernel,
        name="reduce_all",
        out_shape=[
            jax.ShapeDtypeStruct((6, PITCH, BLK), half),
            pltpu.HBM(rows_a.shape, half),
            pltpu.HBM(rows_b.shape, half),
        ],
        in_specs=[anywhere] * 3,
        out_specs=[anywhere] * 3,
        scratch_shapes=[pltpu.VMEM((8, h, BLK), half) for h in heights]
        + [pltpu.VMEM((8, h, BLK), half) for h in heights]
        + [pltpu.VMEM((8, HALF, BLK), half)]
        + [pltpu.VMEM((4, h, BLK), half) for h in heights[:3]]
        + [pltpu.VMEM((2, 4, h, BLK), half) for h in heights[:3]]
        + [pltpu.VMEM((h, BLK), half) for h in heights[:2]]
        + [
            dma((4, 8)), dma((4, 8)), dma((4, 8)), dma((8,)), dma((8,)), dma((3, 4)), dma((3, 4)),
            dma((3, 4)), dma((3, 2, 4)), dma((2,)), dma((2,)), dma((5,)), dma((5,)), dma((3,)),
            dma((2, 3)), dma((2, 4)), dma((2,)),
        ],
        compiler_params=pltpu.CompilerParams(
            collective_id=1, has_side_effects=True, vmem_limit_bytes=30 << 20
        ),
    )(in_hbm(grads), in_hbm(rows_a), in_hbm(rows_b))


CORRECT = 1.0 - 0.5**STEP


def update_kernel(
    total, weights, first, second, left, right, left_rot, right_rot, vec_grad, vec, vec_first, vec_second,
    moment_one, moment_two, left_new, right_new, weights_new, weights_half, vector_one, vector_two, vector_new,
):
    half = jnp.bfloat16
    grad = total[0, :BLK, :]
    left_new[0] = 0.95 * left[0] + 0.05 * dot_nt(grad, grad)
    right_new[0] = 0.95 * right[0] + 0.05 * dot_tn(grad, grad)
    rot_l = left_rot[0].astype(half)
    rot_r = right_rot[0].astype(half)
    turned = dot_nn(dot_tn(rot_l, grad).astype(half), rot_r)
    one = 0.5 * first[0] + 0.5 * turned
    two = 0.5 * second[0] + 0.5 * turned * turned
    moment_one[0] = one
    moment_two[0] = two
    ratio = (one / CORRECT) / (jnp.sqrt(two / CORRECT) + 1e-08)
    stepped = dot_nt(dot_nn(rot_l, ratio.astype(half)).astype(half), rot_r)
    fresh = weights[0] - rate_matrix * stepped
    weights_new[0] = fresh
    weights_half[0] = fresh.astype(half)

    @pl.when(pl.program_id(0) == 0)
    def _():
        slope = vec_grad[0, :1, :].astype(jnp.float32)
        vec_one = 0.5 * vec_first[...] + 0.5 * slope
        vec_two = 0.5 * vec_second[...] + 0.5 * slope * slope
        vector_one[...] = vec_one
        vector_two[...] = vec_two
        vector_new[...] = vec[...] - rate_vector * (
            (vec_one / CORRECT) / (jnp.sqrt(vec_two / CORRECT) + 1e-08)
        )


def update_all(total, weights, first, second, left, right, left_rot, right_rot, vec, vec_first, vec_second):
    full = jnp.float32
    holding = weights.shape[0]
    block = pl.BlockSpec((1, BLK, BLK), lambda i: (i, 0, 0))
    row = pl.BlockSpec((1, BLK), lambda i: (0, 0))
    vector = jax.ShapeDtypeStruct((1, BLK), full)
    matrix = jax.ShapeDtypeStruct(weights.shape, full)
    return pl.pallas_call(
        update_kernel,
        name="update_all",
        grid=(holding,),
        out_shape=[matrix] * 5 + [jax.ShapeDtypeStruct(weights.shape, jnp.bfloat16)] + [vector] * 3,
        in_specs=[pl.BlockSpec((1, PITCH, BLK), lambda i: (i, 0, 0))]
        + [block] * 7
        + [pl.BlockSpec((1, 16, BLK), lambda i: (0, BLK // 16, 0)), row, row, row],
        out_specs=[block] * 6 + [row] * 3,
        compiler_params=pltpu.CompilerParams(vmem_limit_bytes=30 << 20),
    )(
        total, weights, first, second, left, right, left_rot, right_rot, total,
        vec.reshape(1, BLK), vec_first.reshape(1, BLK), vec_second.reshape(1, BLK),
    )


def fast_device(
    tokens, output_grad, segment_ids, lengths, owner_slot, slot_weights, first_moment, second_moment,
    left_stats, right_stats, left_basis, right_basis, vector_values, vector_first, vector_second,
):
    gathered, token_row, grad_row = gather_all(slot_weights, vector_values, tokens, output_grad)
    placed, block_row, input_row = run_layer(
        owner_slot, gathered, token_row.reshape(-1, D), grad_row.reshape(-1, D), segment_ids
    )
    total, block_out, input_half = reduce_all(
        placed, block_row.reshape(tokens.shape), input_row.reshape(tokens.shape)
    )
    updated = update_all(
        total, slot_weights, first_moment, second_moment, left_stats, right_stats, left_basis, right_basis,
        vector_values, vector_first, vector_second,
    )
    vectors = [value.reshape(-1) for value in updated[6:]]
    return (block_out, input_half.astype(jnp.float32), *updated[:6], *vectors)


def solution(mesh):
    in_specs = (
        P("dp", "sp", None),
        P("dp", "sp", None),
        P("dp", None),
        P("dp", None),
        P(),
        P("dp", None, None),
        P("dp", None, None),
        P("dp", None, None),
        P("dp", None, None),
        P("dp", None, None),
        P("dp", None, None),
        P("dp", None, None),
        P("dp"),
        P("dp"),
        P("dp"),
    )
    out_specs = (
        P("dp", "sp", None),
        P("dp", "sp", None),
        P("dp", None, None),
        P("dp", None, None),
        P("dp", None, None),
        P("dp", None, None),
        P("dp", None, None),
        P("dp", None, None),
        P("dp"),
        P("dp"),
        P("dp"),
    )
    chosen = fast_device if dict(mesh.shape) == {"dp": 8, "sp": 4} else per_device
    return jax.shard_map(
        chosen, mesh=mesh, in_specs=in_specs, out_specs=out_specs, check_vma=False
    )
```

```python
import math

import jax
import jax.numpy as jnp
from jax import lax
from jax.experimental import pallas as pl
from jax.experimental.pallas import tpu as pltpu
from jax.sharding import PartitionSpec as P

D = 768
HD = 64
FF = 3072
BLK = 384
STEP = 4


highest = lax.Precision.HIGHEST
rate_matrix = 0.04
rate_vector = 0.2


def layer_norm(summed, gain, shift):
    centre = jnp.mean(summed, axis=-1, keepdims=True)
    centred = summed - centre
    spread = jnp.mean(centred * centred, axis=-1, keepdims=True)
    return centred * lax.rsqrt(spread + 1e-06) * gain + shift


def exact_gelu(values):
    return jax.nn.gelu(values, approximate=False)


def passage_mask(segment_row, length_row):
    starts = jnp.cumsum(length_row) - length_row
    number = length_row.shape[0]
    onehot = (segment_row[:, None] == jnp.arange(number, dtype=jnp.int32)[None, :]).astype(
        jnp.int32
    )
    opening = jnp.sum(onehot * starts[None, :], axis=1)
    closing = opening + jnp.sum(onehot * length_row[None, :], axis=1)
    places = jnp.arange(segment_row.shape[0], dtype=jnp.int32)
    return (places[None, :] >= opening[:, None]) & (places[None, :] < closing[:, None])


def into_blocks(matrix):
    height, breadth = matrix.shape
    return (
        matrix.reshape(height // BLK, BLK, breadth // BLK, BLK)
        .transpose(0, 2, 1, 3)
        .reshape(-1, BLK, BLK)
    )


def from_blocks(blocks, height, breadth):
    return (
        blocks.reshape(height // BLK, breadth // BLK, BLK, BLK)
        .transpose(0, 2, 1, 3)
        .reshape(height, breadth)
    )


def split_blocks(blocks):
    square = (D // BLK) ** 2
    broad = D * FF // (BLK * BLK)
    w_query = from_blocks(blocks[0:square], D, D)
    w_key = from_blocks(blocks[square : 2 * square], D, D)
    w_value = from_blocks(blocks[2 * square : 3 * square], D, D)
    w_output = from_blocks(blocks[3 * square : 4 * square], D, D)
    w_upward = from_blocks(blocks[4 * square : 4 * square + broad], D, FF)
    w_downward = from_blocks(blocks[4 * square + broad : 4 * square + 2 * broad], FF, D)
    return (w_query, w_key, w_value, w_output, w_upward, w_downward)


def contract_rows(left_mat, right_mat):
    return lax.dot_general(
        left_mat, right_mat, (((0,), (0,)), ((), ())), preferred_element_type=jnp.float32
    )


def contract_cols(left_mat, right_mat):
    return lax.dot_general(
        left_mat, right_mat, (((1,), (1,)), ((), ())), preferred_element_type=jnp.float32
    )


def soap_update(
    gradient, weights, moment_old, second_old, left_old, right_old, left_rot, right_rot
):
    left_next = 0.95 * left_old + 0.05 * jnp.einsum(
        "nij,nkj->nik", gradient, gradient, precision=highest
    )
    right_next = 0.95 * right_old + 0.05 * jnp.einsum(
        "nji,njk->nik", gradient, gradient, precision=highest
    )
    turned = jnp.einsum("nji,njk->nik", left_rot, gradient, precision=highest)
    turned = jnp.einsum("nij,njk->nik", turned, right_rot, precision=highest)
    moment_next = 0.5 * moment_old + 0.5 * turned
    second_next = 0.5 * second_old + 0.5 * turned * turned
    correct = 1.0 - 0.5**STEP
    ratio = moment_next / correct / (jnp.sqrt(second_next / correct) + 1e-08)
    stepped = jnp.einsum("nij,njk->nik", left_rot, ratio, precision=highest)
    stepped = jnp.einsum("nij,nkj->nik", stepped, right_rot, precision=highest)
    return (moment_next, second_next, left_next, right_next, weights - rate_matrix * stepped)


def adam_update(gradient, values, moment_old, second_old):
    moment_next = 0.5 * moment_old + 0.5 * gradient
    second_next = 0.5 * second_old + 0.5 * gradient * gradient
    correct = 1.0 - 0.5**STEP
    ratio = moment_next / correct / (jnp.sqrt(second_next / correct) + 1e-08)
    return (moment_next, second_next, values - rate_vector * ratio)


def masked_scores(joint_row, segment_row, length_row):
    positions = joint_row.shape[0]
    query = joint_row[:, 0].reshape(positions, -1, HD)
    keyed = joint_row[:, 1].reshape(positions, -1, HD)
    valued = joint_row[:, 2].reshape(positions, -1, HD)
    scores = jnp.einsum("qhd,khd->hqk", query, keyed, preferred_element_type=jnp.float32) * 0.125
    visible = passage_mask(segment_row, length_row)
    return (jnp.where(visible[None], scores, -1e30), query, keyed, valued)


def attend_rows(item):
    joint_row, segment_row, length_row = item
    scores, query, keyed, valued = masked_scores(joint_row, segment_row, length_row)
    largest = jnp.max(scores, axis=-1, keepdims=True)
    raised = jnp.exp(scores - largest)
    totals = jnp.sum(raised, axis=-1, keepdims=True)
    probs = raised / totals
    logsum = (largest + jnp.log(totals))[..., 0]
    context = jnp.einsum(
        "hqk,khd->qhd", probs.astype(jnp.bfloat16), valued, preferred_element_type=jnp.float32
    )
    return (context.reshape(joint_row.shape[0], -1).astype(jnp.bfloat16), logsum)


def back_rows(item):
    joint_row, logsum, delta_context, segment_row, length_row = item
    positions = joint_row.shape[0]
    scores, query, keyed, valued = masked_scores(joint_row, segment_row, length_row)
    probs = jnp.exp(scores - logsum[..., None])
    delta_ctx = delta_context.reshape(positions, -1, HD)
    delta_value = jnp.einsum(
        "hqk,qhd->khd", probs.astype(jnp.bfloat16), delta_ctx, preferred_element_type=jnp.float32
    )
    delta_prob = jnp.einsum("qhd,khd->hqk", delta_ctx, valued, preferred_element_type=jnp.float32)
    weighted = jnp.sum(probs * delta_prob, axis=-1, keepdims=True)
    delta_score = (probs * (delta_prob - weighted)).astype(jnp.bfloat16)
    delta_query = (
        jnp.einsum("hqk,khd->qhd", delta_score, keyed, preferred_element_type=jnp.float32) * 0.125
    )
    delta_key = (
        jnp.einsum("hqk,qhd->khd", delta_score, query, preferred_element_type=jnp.float32) * 0.125
    )
    stacked = jnp.stack(
        [
            delta_query.reshape(positions, -1),
            delta_key.reshape(positions, -1),
            delta_value.reshape(positions, -1),
        ],
        axis=1,
    )
    return stacked.astype(jnp.bfloat16)


def pick_blocks(source, slot_index, owner_slot, fanout, part_index):
    matches = owner_slot[None, :] == slot_index[:, None]
    present = jnp.any(matches, axis=1).astype(jnp.float32)
    chosen = jnp.sum(
        matches.astype(jnp.int32) * jnp.arange(owner_slot.shape[0], dtype=jnp.int32)[None, :],
        axis=1,
    )
    picked = jnp.take(source, chosen * fanout + part_index, axis=0)
    return picked * present[:, None, None]


def per_device(
    tokens,
    output_grad,
    segment_ids,
    lengths,
    owner_slot,
    slot_weights,
    first_moment,
    second_moment,
    left_stats,
    right_stats,
    left_basis,
    right_basis,
    vector_values,
    vector_first,
    vector_second,
):
    holding = slot_weights.shape[0]
    row_count = tokens.shape[0]
    token_count = tokens.shape[1]
    gathered, vector_half = (
        lax.all_gather(slot_weights.astype(jnp.bfloat16), "dp", axis=0, tiled=True),
        lax.all_gather(vector_values.astype(jnp.bfloat16), "dp", axis=0, tiled=True),
    )
    blocks = jnp.take(gathered, owner_slot, axis=0)
    w_query, w_key, w_value, w_output, w_upward, w_downward = split_blocks(blocks)
    w_joint = jnp.concatenate([w_query, w_key, w_value], axis=1)
    gains = vector_half.astype(jnp.float32).reshape(4, D)
    flat_tokens = tokens.reshape(-1, D)
    projected = jnp.dot(flat_tokens, w_joint, preferred_element_type=jnp.float32).astype(
        jnp.bfloat16
    )
    projected = projected.reshape(row_count, token_count, 3, D)
    heads = lax.all_to_all(projected, "sp", split_axis=3, concat_axis=1, tiled=True)
    context, logsum = lax.map(attend_rows, (heads, segment_ids, lengths))
    context_tok = lax.all_to_all(context, "sp", split_axis=1, concat_axis=2, tiled=True).reshape(
        -1, D
    )
    attended = jnp.dot(context_tok, w_output, preferred_element_type=jnp.float32)
    summed_one = flat_tokens.astype(jnp.float32) + attended
    hidden, norm_one_pull = jax.vjp(layer_norm, summed_one, gains[0], gains[1])
    hidden_half = hidden.astype(jnp.bfloat16)
    upward = jnp.dot(hidden_half, w_upward, preferred_element_type=jnp.float32)
    activated, gelu_pull = jax.vjp(exact_gelu, upward)
    active_half = activated.astype(jnp.bfloat16)
    downward = jnp.dot(active_half, w_downward, preferred_element_type=jnp.float32)
    result, norm_two_pull = jax.vjp(layer_norm, hidden + downward, gains[2], gains[3])
    block_out = result.astype(jnp.bfloat16).reshape(row_count, token_count, D)
    cotangent = output_grad.reshape(-1, D).astype(jnp.float32)
    delta_two, delta_gain_two, delta_shift_two = norm_two_pull(cotangent)
    delta_down = delta_two.astype(jnp.bfloat16)
    grad_down = contract_rows(active_half, delta_down)
    delta_active = contract_cols(delta_down, w_downward)
    (delta_upward,) = gelu_pull(delta_active)
    delta_up = delta_upward.astype(jnp.bfloat16)
    grad_up = contract_rows(hidden_half, delta_up)
    delta_hidden = delta_two + contract_cols(delta_up, w_upward)
    delta_one, delta_gain_one, delta_shift_one = norm_one_pull(delta_hidden)
    delta_attn = delta_one.astype(jnp.bfloat16)
    grad_output = contract_rows(context_tok, delta_attn)
    delta_context = (
        contract_cols(delta_attn, w_output).astype(jnp.bfloat16).reshape(row_count, token_count, D)
    )
    delta_heads = lax.all_to_all(delta_context, "sp", split_axis=2, concat_axis=1, tiled=True)
    delta_projected = lax.map(back_rows, (heads, logsum, delta_heads, segment_ids, lengths))
    delta_joint = lax.all_to_all(
        delta_projected, "sp", split_axis=1, concat_axis=3, tiled=True
    ).reshape(-1, 3 * D)
    grad_joint = contract_rows(flat_tokens, delta_joint)
    input_grad = (delta_one + contract_cols(delta_joint, w_joint)).reshape(
        row_count, token_count, D
    )
    grad_blocks = jnp.concatenate(
        [
            into_blocks(grad_joint[:, :D]),
            into_blocks(grad_joint[:, D : 2 * D]),
            into_blocks(grad_joint[:, 2 * D :]),
            into_blocks(grad_output),
            into_blocks(grad_up),
            into_blocks(grad_down),
        ],
        axis=0,
    )
    vector_grad = jnp.concatenate(
        [delta_gain_one, delta_shift_one, delta_gain_two, delta_shift_two]
    )
    vector_total = lax.psum(vector_grad, ("dp", "sp"))
    piece_len = vector_values.shape[0]
    vector_piece = lax.dynamic_slice_in_dim(
        vector_total, lax.axis_index("dp") * piece_len, piece_len
    )
    slot_index = jnp.arange(holding * lax.axis_size("dp"), dtype=jnp.int32)
    owned = lax.psum_scatter(
        pick_blocks(grad_blocks, slot_index, owner_slot, 1, 0),
        "dp",
        scatter_dimension=0,
        tiled=True,
    )
    owned = lax.psum(owned.astype(jnp.bfloat16), "sp").astype(jnp.float32)
    moment_one, moment_two, left_new, right_new, weights_new = soap_update(
        owned,
        slot_weights,
        first_moment,
        second_moment,
        left_stats,
        right_stats,
        left_basis,
        right_basis,
    )
    vector_one, vector_two, vector_new = adam_update(
        vector_piece, vector_values, vector_first, vector_second
    )
    return (
        block_out,
        input_grad,
        moment_one,
        moment_two,
        left_new,
        right_new,
        weights_new,
        weights_new.astype(jnp.bfloat16),
        vector_one,
        vector_two,
        vector_new,
    )


PITCH = BLK + 16
MESH = pl.DeviceIdType.MESH
NZ = 4


def in_hbm(value):
    return pltpu.with_memory_space_constraint(value, pltpu.HBM)


def place():
    dp = lax.axis_index("dp")
    sp = lax.axis_index("sp")
    return dp // 2, dp % 2, sp // 2, sp % 2


def greet(z, y, x, c):
    barrier = pltpu.get_barrier_semaphore()
    dp = z * 2 + y
    sp = x * 2 + c

    def signal(target):
        pl.semaphore_signal(barrier, 1, device_id=target, device_id_type=MESH)

    for step in range(1, 4):
        signal((dp, (sp + step) % 4))
    signal((z * 2 + 1 - y, sp))

    @pl.when(z < NZ - 1)
    def _():
        signal((dp + 2, sp))

    @pl.when(z > 0)
    def _():
        signal((dp - 2, sp))

    pl.semaphore_wait(barrier, 4 + (z < NZ - 1).astype(jnp.int32) + (z > 0).astype(jnp.int32))


def gather_kernel(
    weights, vector, tokens, grads, out, token_row, grad_row,
    wide, narrow, load_sem, keep_sem, send_sem, recv_sem, row_send, row_recv, row_keep,
):
    z, y, x, c = place()
    dp = z * 2 + y
    sp = x * 2 + c
    loads = [pltpu.make_async_copy(weights.at[i], wide.at[i], load_sem.at[i]) for i in range(6)]
    for load in loads:
        load.start()
    keeps = [
        pltpu.make_async_copy(tokens.at[sp], token_row.at[sp], row_keep.at[0]),
        pltpu.make_async_copy(grads.at[sp], grad_row.at[sp], row_keep.at[1]),
    ]
    for keep in keeps:
        keep.start()
    gains = jnp.broadcast_to(vector[...], (16, BLK)).astype(jnp.bfloat16)
    greet(z, y, x, c)

    def rows_copy(which, source, landing, step):
        peer = (sp + step) % 4
        return pltpu.make_async_remote_copy(
            src_ref=source.at[peer], dst_ref=landing.at[sp],
            send_sem=row_send.at[which, step - 1], recv_sem=row_recv.at[which, sp],
            device_id=(dp, peer), device_id_type=MESH,
        )

    def rows_arrival(which, source, landing, step):
        peer = (sp + step) % 4
        return pltpu.make_async_remote_copy(
            src_ref=source.at[peer], dst_ref=landing.at[peer],
            send_sem=row_send.at[which, step - 1], recv_sem=row_recv.at[which, peer],
            device_id=(dp, peer), device_id_type=MESH,
        )

    for step in (2, 3, 1):
        rows_copy(0, tokens, token_row, step).start()

    for i in range(6):
        loads[i].wait()
        narrow[i, :BLK, :] = wide[i].astype(jnp.bfloat16)
        narrow[i, BLK:, :] = gains
    own = [pltpu.make_async_copy(narrow.at[i], out.at[dp * 6 + i], keep_sem.at[i]) for i in range(6)]

    def piece(part):
        return (c, BLK + 16) if part == 0 else (2 + 2 * x + c, BLK)

    targets = {
        "up": (dp + 2, sp), "down": (dp - 2, sp), "y": (z * 2 + 1 - y, sp),
        "x": (dp, (1 - x) * 2 + c), "core": (dp, x * 2 + 1 - c),
    }
    number = {"up": 0, "down": 1, "y": 2, "x": 3, "core": 4}

    def copy(way, holder, slot, height, index, source=None):
        at = holder * 6 + slot
        src = out.at[at, pl.ds(0, height)] if source is None else source
        return pltpu.make_async_remote_copy(
            src_ref=src, dst_ref=out.at[at, pl.ds(0, height)],
            send_sem=send_sem.at[number[way], index], recv_sem=recv_sem.at[at],
            device_id=targets[way], device_id_type=MESH,
        )

    started = []

    def start(way, holder, slot, height, index, valid=None, source=None):
        item = copy(way, holder, slot, height, index, source)
        if valid is None:
            item.start()
        else:
            pl.when(valid)(item.start)
        started.append((item, valid))

    def arrive(holder, slot, height, valid=None):
        item = copy("core", holder, slot, height, 0)
        if valid is None:
            item.wait_recv()
        else:
            pl.when(valid)(item.wait_recv)

    counts = {}

    def fresh(way):
        counts[way] = counts.get(way, -1) + 1
        return counts[way]

    for part in (1, 0):
        slot, height = piece(part)
        src = narrow.at[slot, pl.ds(0, height)]
        start("up", dp, slot, height, fresh("up"), z < NZ - 1, src)
        start("down", dp, slot, height, fresh("down"), z > 0, src)
        start("y", dp, slot, height, fresh("y"), None, src)
    for item in own:
        item.start()

    def from_z(sign, far, part):
        origin = z + sign * far
        inside = (origin >= 0) if sign < 0 else (origin <= NZ - 1)
        holder = origin * 2 + y
        slot, height = piece(part)
        arrive(holder, slot, height, inside)
        if far < NZ - 1:
            if sign < 0:
                start("up", holder, slot, height, fresh("up"), inside & (z < NZ - 1))
            else:
                start("down", holder, slot, height, fresh("down"), inside & (z > 0))
        start("y", holder, slot, height, fresh("y"), inside)
        if part == 1:
            start("x", holder, slot, height, fresh("x"), inside)
        start("core", holder, slot, height, fresh("core"), inside)

    def signs(far):
        return (0,) if far == 0 else (-1, 1)

    def valid_of(sign, far):
        origin = z + sign * far
        if far == 0:
            return origin, None
        return origin, ((origin >= 0) if sign < 0 else (origin <= NZ - 1))

    def from_y(sign, far, part):
        origin, inside = valid_of(sign, far)
        holder = origin * 2 + 1 - y
        slot, height = piece(part)
        arrive(holder, slot, height, inside)
        if part == 1:
            start("x", holder, slot, height, fresh("x"), inside)
        start("core", holder, slot, height, fresh("core"), inside)

    def from_x(sign, far, side):
        origin, inside = valid_of(sign, far)
        holder = origin * 2 + (y if side == 0 else 1 - y)
        slot = 2 + 2 * (1 - x) + c
        arrive(holder, slot, BLK, inside)
        start("core", holder, slot, BLK, fresh("core"), inside)

    for far in range(1, NZ):
        for part in (1, 0):
            for sign in (-1, 1):
                from_z(sign, far, part)
            for sign in signs(far - 1):
                from_y(sign, far - 1, part)
        if far == 1:
            for step in (2, 3, 1):
                rows_copy(1, grads, grad_row, step).start()
        if far >= 2:
            for sign in signs(far - 1):
                from_x(sign, far - 1, 0)
            for sign in signs(far - 2):
                from_x(sign, far - 2, 1)
    for part in (1, 0):
        for sign in (-1, 1):
            from_y(sign, NZ - 1, part)
    for sign in (-1, 1):
        from_x(sign, NZ - 1, 0)
    for far in (NZ - 2, NZ - 1):
        for sign in signs(far):
            from_x(sign, far, 1)

    for far in range(NZ):
        for sign in signs(far):
            origin, inside = valid_of(sign, far)
            for side in (0, 1):
                if far == 0 and side == 0:
                    continue
                holder = origin * 2 + (y if side == 0 else 1 - y)
                for slot, height in ((1 - c, BLK + 16), (3 - c, BLK), (5 - c, BLK)):
                    arrive(holder, slot, height, inside)
    for step in (2, 3, 1):
        rows_arrival(0, tokens, token_row, step).wait_recv()
        rows_arrival(1, grads, grad_row, step).wait_recv()
        rows_copy(0, tokens, token_row, step).wait_send()
        rows_copy(1, grads, grad_row, step).wait_send()
    for item, valid in started:
        if valid is None:
            item.wait_send()
        else:
            pl.when(valid)(item.wait_send)
    for item in own + keeps:
        item.wait()


def gather_all(weights, vector, tokens, grads):
    anywhere = pl.BlockSpec(memory_space=pltpu.HBM)
    return pl.pallas_call(
        gather_kernel,
        name="gather_all",
        out_shape=[
            pltpu.HBM((48, PITCH, BLK), jnp.bfloat16),
            pltpu.HBM(tokens.shape, jnp.bfloat16),
            pltpu.HBM(grads.shape, jnp.bfloat16),
        ],
        in_specs=[anywhere, pl.BlockSpec(memory_space=pltpu.VMEM), anywhere, anywhere],
        out_specs=[anywhere, anywhere, anywhere],
        scratch_shapes=[
            pltpu.VMEM((6, BLK, BLK), jnp.float32),
            pltpu.VMEM((6, PITCH, BLK), jnp.bfloat16),
            pltpu.SemaphoreType.DMA((6,)),
            pltpu.SemaphoreType.DMA((6,)),
            pltpu.SemaphoreType.DMA((5, 40)),
            pltpu.SemaphoreType.DMA((48,)),
            pltpu.SemaphoreType.DMA((2, 3)),
            pltpu.SemaphoreType.DMA((2, 4)),
            pltpu.SemaphoreType.DMA((2,)),
        ],
        compiler_params=pltpu.CompilerParams(
            collective_id=0, has_side_effects=True, vmem_limit_bytes=24 << 20
        ),
    )(in_hbm(weights), vector.reshape(1, BLK), in_hbm(tokens), in_hbm(grads))


ROW = 512
PAIR = 128
SPAN = 384
EPS = 1e-06


def gelu_of(u):
    bell = jnp.exp(-0.5 * u * u)
    t = 1.0 / (1.0 + (0.3275911 / math.sqrt(2.0)) * jnp.abs(u))
    tail = 0.5 * 1.061405429
    for term in (-1.453152027, 1.421413741, -0.284496736, 0.254829592):
        tail = tail * t + 0.5 * term
    tail = tail * t * bell
    below = jnp.where(u >= 0.0, 1.0 - tail, tail)
    return (u * below).astype(jnp.bfloat16), below + u * (bell * (1.0 / math.sqrt(2.0 * math.pi)))


def dot_nn(a, b):
    return lax.dot_general(a, b, (((1,), (0,)), ((), ())), preferred_element_type=jnp.float32)


def dot_nt(a, b):
    return lax.dot_general(a, b, (((1,), (1,)), ((), ())), preferred_element_type=jnp.float32)


def dot_tn(a, b):
    return lax.dot_general(a, b, (((0,), (0,)), ((), ())), preferred_element_type=jnp.float32)


def layer_kernel(
    owner, weights, tokens, dy_ref, segments, grads, block_out, input_half,
    wqkv, wo, w1, w2, gains, qkv, probs, shares, held, context, hidden, hidden16, norm1, act, slope, acc, dz, dz16,
    dqkv, dup, stage, flipped, flipped_hidden, ups, vecs, spread, w_sem, g_sem, v_sem,
):
    half = jnp.bfloat16
    sp = lax.axis_index("sp")

    def weight_copies():
        copies = []
        for which, ref in enumerate((wqkv.at[0], wqkv.at[1], wqkv.at[2], wo)):
            for r in range(2):
                for q in range(2):
                    copies.append((which * 4 + r * 2 + q, ref, r, q))
        for r in range(2):
            for q in range(8):
                copies.append((16 + r * 8 + q, w1.at[q // 2], r, q % 2))
        for r in range(8):
            for q in range(2):
                copies.append((32 + r * 2 + q, w2.at[r // 2], r % 2, q))
        return [
            pltpu.make_async_copy(
                weights.at[owner[b], pl.ds(0, BLK)],
                ref.at[pl.ds(r * BLK, BLK), pl.ds(q * BLK, BLK)],
                w_sem.at[b],
            )
            for b, ref, r, q in copies
        ]

    copies = weight_copies()
    gain_copies = [
        pltpu.make_async_copy(
            weights.at[6 * d, pl.ds(BLK, 16)], gains.at[d // 2, :, pl.ds((d % 2) * BLK, BLK)], g_sem.at[d]
        )
        for d in range(8)
    ]
    for item in copies[:16] + gain_copies + copies[16:]:
        item.start()

    seg_row = segments[pl.ds(sp, 1), :].astype(jnp.float32)
    spread[...] = jnp.transpose(jnp.broadcast_to(seg_row, (PAIR, ROW)))

    for item in copies[:12]:
        item.wait()
    x = tokens[...]
    flipped[...] = jnp.transpose(x)
    for part in range(3):
        block = dot_nn(x, wqkv[part])
        if part == 0:
            block = block * 0.125
        block = block.astype(half)
        for p in range(6):
            qkv[part * 6 + p] = block[:, p * PAIR : (p + 1) * PAIR]

    lane = lax.broadcasted_iota(jnp.int32, (1, PAIR), 1)
    lows = (lane < 64, lane >= 64)

    def visible(part):
        keys = segments[pl.ds(sp, 1), pl.ds(part * PAIR, SPAN)].astype(jnp.float32)
        own = spread[pl.ds(part * 256, 256), pl.ds(0, 1)]
        return own == keys

    def attend(p, carry):
        q2, k2, v2 = qkv[p], qkv[6 + p], qkv[12 + p]
        for part in range(2):
            mask = visible(part)
            qs = q2[part * 256 : part * 256 + 256]
            ks = k2[part * PAIR : part * PAIR + SPAN]
            vs = v2[part * PAIR : part * PAIR + SPAN]
            outs = []
            for h in range(2):
                scores = dot_nt(jnp.where(lows[h], qs, jnp.zeros_like(qs)), ks)
                scores = jnp.where(mask, scores, -1e30)
                raised = jnp.exp(scores - jnp.max(scores, axis=1, keepdims=True)).astype(half)
                probs[p, 2 * part + h] = raised
                outs.append(dot_nn(raised, jnp.where(lows[h], vs, jnp.ones_like(vs))))
            inverse = 1.0 / pltpu.roll(jnp.where(lows[0], outs[1], outs[0]), 64, 1)
            shares[p, pl.ds(part * 256, 256)] = inverse
            context[p, pl.ds(part * 256, 256)] = (jnp.where(lows[0], outs[0], outs[1]) * inverse).astype(half)
        return carry

    lax.fori_loop(0, 6, attend, 0)

    for item in copies[12:16] + gain_copies:
        item.wait()
    joined = jnp.concatenate([context[p] for p in range(6)], axis=1)

    def gain(k):
        return gains[k, pl.ds(0, 1), :].astype(jnp.float32)

    def normalise(z):
        centre = jnp.mean(z, axis=1, keepdims=True)
        z = z - centre
        inverse = lax.rsqrt(jnp.mean(z * z, axis=1, keepdims=True) + EPS)
        return z * inverse, inverse

    acc[...] = dot_nn(joined, wo[...])

    def norm_one(t, carry):
        rows = pl.ds(pl.multiple_of(t * 64, 64), 64)
        hat, inverse = normalise(tokens[rows, :].astype(jnp.float32) + acc[rows, :])
        norm1[rows, :] = hat
        spread[rows, :] = jnp.where(lane == 1, inverse, spread[rows, :])
        value = hat * gain(0) + gain(1)
        hidden[rows, :] = value
        hidden16[rows, :] = value.astype(half)
        return carry

    lax.fori_loop(0, 8, norm_one, 0)
    for item in copies[16:]:
        item.wait()

    flipped_hidden[...] = jnp.transpose(hidden16[...])
    ups[0] = dot_nn(hidden16[...], w1[0])
    for j in range(5):
        if j < 3:
            ups[(j + 1) % 2] = dot_nn(hidden16[...], w1[j + 1])
        if j < 4:
            act[j], slope[j] = gelu_of(ups[j % 2])
        if j > 0:
            hidden[...] += dot_nn(act[j - 1], w2[j - 1])

    vecs[...] = jnp.zeros_like(vecs)

    def fold(value):
        return jnp.sum(value.reshape(-1, 8, D), axis=0)

    def norm_back(hat, inverse, delta, gain_row):
        e = delta * gain_row
        return (
            e - jnp.mean(e, axis=1, keepdims=True) - hat * jnp.mean(e * hat, axis=1, keepdims=True)
        ) * inverse

    def norm_two(t, carry):
        rows = pl.ds(pl.multiple_of(t * 64, 64), 64)
        hat, inverse = normalise(hidden[rows, :])
        block_out[rows, :] = (hat * gain(2) + gain(3)).astype(half)
        delta = dy_ref[rows, :].astype(jnp.float32)
        vecs[2] += fold(delta * hat)
        vecs[3] += fold(delta)
        back = norm_back(hat, inverse, delta, gain(2))
        dz[rows, :] = back
        dz16[rows, :] = back.astype(half)
        return carry

    lax.fori_loop(0, 8, norm_two, 0)

    def out_copy(slot, b, r, q):
        return pltpu.make_async_copy(
            stage.at[slot, pl.ds(r * BLK, BLK), pl.ds(q * BLK, BLK)],
            grads.at[owner[b], pl.ds(0, BLK)],
            v_sem.at[slot, r * 2 + q],
        )

    def flush(slot, blocks):
        for r in range(2):
            for q in range(2):
                out_copy(slot, blocks(r, q), r, q).start()

    def drain(slot):
        for r in range(2):
            for q in range(2):
                out_copy(slot, 0, r, q).wait()

    def backward(j, carry):
        ddown = dz16[...]
        delta = (dot_nt(ddown, w2[j]) * slope[j]).astype(half)

        @pl.when(j >= 2)
        def _():
            drain(2 * (j % 2))
            drain(2 * (j % 2) + 1)

        stage[2 * (j % 2)] = dot_tn(act[j], ddown).astype(half)
        flush(2 * (j % 2), lambda r, q: 32 + (2 * j + r) * 2 + q)
        stage[2 * (j % 2) + 1] = dot_nn(flipped_hidden[...], delta).astype(half)
        flush(2 * (j % 2) + 1, lambda r, q: 16 + r * 8 + 2 * j + q)
        dz[...] += dot_nt(delta, w1[j])
        return carry

    lax.fori_loop(0, 4, backward, 0)

    def norm_one_back(t, carry):
        rows = pl.ds(pl.multiple_of(t * 64, 64), 64)
        hat = norm1[rows, :]
        delta = dz[rows, :]
        vecs[0] += fold(delta * hat)
        vecs[1] += fold(delta)
        back = norm_back(hat, spread[rows, pl.ds(1, 1)], delta, gain(0))
        dz[rows, :] = back
        dz16[rows, :] = back.astype(half)
        return carry

    lax.fori_loop(0, 8, norm_one_back, 0)

    for slot in range(4):
        drain(slot)
    dattn = dz16[...]
    stage[0] = dot_tn(joined, dattn).astype(half)
    flush(0, lambda r, q: 12 + r * 2 + q)
    dcontext = dot_nt(dattn, wo[...]).astype(half)
    for p in range(6):
        held[p] = context[p]
        context[p] = dcontext[:, p * PAIR : (p + 1) * PAIR]

    def attend_back(p, carry):
        q2, k2, v2, d2 = qkv[p], qkv[6 + p], qkv[12 + p], context[p]
        dup[...] = jnp.zeros_like(dup)
        for part in range(2):
            window = pl.ds(part * PAIR, SPAN)
            qs = q2[part * 256 : part * 256 + 256]
            ds = d2[part * 256 : part * 256 + 256]
            ks = k2[part * PAIR : part * PAIR + SPAN]
            vs = v2[part * PAIR : part * PAIR + SPAN]
            dvs, dqs, dks = [], [], []
            share = shares[p, pl.ds(part * 256, 256)]
            scaled = (ds.astype(jnp.float32) * share).astype(half)
            weight = scaled.astype(jnp.float32) * held[p, pl.ds(part * 256, 256)].astype(jnp.float32)
            for h in range(2):
                raised = probs[p, 2 * part + h]
                dprob = dot_nt(jnp.where(lows[h], scaled, jnp.zeros_like(scaled)), vs)
                centre = jnp.sum(jnp.where(lows[h], weight, 0.0), axis=1, keepdims=True)
                dscore = (raised.astype(jnp.float32) * (dprob - centre)).astype(half)
                dvs.append(dot_tn(raised, scaled))
                dqs.append(dot_nn(dscore, ks))
                dks.append(dot_tn(dscore, qs))
            dqkv[p, pl.ds(part * 256, 256)] = (
                jnp.where(lows[0], dqs[0], dqs[1]) * 0.125
            ).astype(half)
            dup[0, window] += jnp.where(lows[0], dks[0], dks[1])
            dup[1, window] += jnp.where(lows[0], dvs[0], dvs[1])
        dqkv[6 + p] = dup[0].astype(half)
        dqkv[12 + p] = dup[1].astype(half)
        return carry

    lax.fori_loop(0, 6, attend_back, 0)

    for part in range(3):
        delta = jnp.concatenate([dqkv[part * 6 + p] for p in range(6)], axis=1)
        stage[1 + part] = dot_nn(flipped[...], delta).astype(half)
        flush(1 + part, lambda r, q: part * 4 + r * 2 + q)
        dz[...] += dot_nt(delta, wqkv[part])

    input_half[...] = dz[...].astype(half)
    for k in range(4):
        row = jnp.sum(vecs[k], axis=0, keepdims=True)
        vecs16 = jnp.broadcast_to(row, (16, D)).astype(half)
        gains[k] = vecs16
    for k in range(4):
        for q in range(2):
            for s in range(2):
                pltpu.make_async_copy(
                    gains.at[k, :, pl.ds(q * BLK, BLK)],
                    grads.at[6 * (2 * k + q) + s, pl.ds(BLK, 16)],
                    w_sem.at[(2 * k + q) * 2 + s],
                ).start()
    for k in range(4):
        for q in range(2):
            for s in range(2):
                pltpu.make_async_copy(
                    gains.at[k, :, pl.ds(q * BLK, BLK)],
                    grads.at[6 * (2 * k + q) + s, pl.ds(BLK, 16)],
                    w_sem.at[(2 * k + q) * 2 + s],
                ).wait()
    for slot in range(4):
        drain(slot)


def run_layer(owner_slot, gathered, token_row, grad_row, segment_ids):
    half, full = jnp.bfloat16, jnp.float32
    anywhere = pl.BlockSpec(memory_space=pltpu.HBM)
    vmem = pl.BlockSpec(memory_space=pltpu.VMEM)
    dma = pltpu.SemaphoreType.DMA
    return pl.pallas_call(
        layer_kernel,
        name="run_layer",
        out_shape=[
            jax.ShapeDtypeStruct((48, PITCH, BLK), half),
            jax.ShapeDtypeStruct((ROW, D), half),
            jax.ShapeDtypeStruct((ROW, D), half),
        ],
        in_specs=[pl.BlockSpec(memory_space=pltpu.SMEM), anywhere, vmem, vmem, vmem],
        out_specs=[anywhere, vmem, vmem],
        scratch_shapes=[
            pltpu.VMEM((3, D, D), half),
            pltpu.VMEM((D, D), half),
            pltpu.VMEM((4, D, D), half),
            pltpu.VMEM((4, D, D), half),
            pltpu.VMEM((4, 16, D), half),
            pltpu.VMEM((18, ROW, PAIR), half),
            pltpu.VMEM((6, 4, 256, SPAN), half),
            pltpu.VMEM((6, ROW, PAIR), full),
            pltpu.VMEM((6, ROW, PAIR), half),
            pltpu.VMEM((6, ROW, PAIR), half),
            pltpu.VMEM((ROW, D), full),
            pltpu.VMEM((ROW, D), half),
            pltpu.VMEM((ROW, D), full),
            pltpu.VMEM((4, ROW, D), half),
            pltpu.VMEM((4, ROW, D), full),
            pltpu.VMEM((ROW, D), full),
            pltpu.VMEM((ROW, D), full),
            pltpu.VMEM((ROW, D), half),
            pltpu.VMEM((18, ROW, PAIR), half),
            pltpu.VMEM((2, ROW, PAIR), full),
            pltpu.VMEM((4, D, D), half),
            pltpu.VMEM((D, ROW), half),
            pltpu.VMEM((D, ROW), half),
            pltpu.VMEM((2, ROW, D), full),
            pltpu.VMEM((4, 8, D), full),
            pltpu.VMEM((ROW, PAIR), full),
            dma((48,)),
            dma((8,)),
            dma((4, 4)),
        ],
        compiler_params=pltpu.CompilerParams(vmem_limit_bytes=62 << 20),
    )(owner_slot, gathered, token_row, grad_row, segment_ids)


BLANK = BLK + 16
HALF = BLK // 2
STREAMS = {
    "A0": (BLANK, 0, True, True),
    "A1": (HALF, 0, True, True),
    "A2": (HALF, HALF, True, False),
    "O": (HALF, 0, False, True),
    "XO": (HALF, 0, False, True),
}
TASKS = (
    ("Y", "A1", 1), ("Y", "A1", 0), ("Z", "A2", 0, 0), ("Y", "A0", 0), ("X", "O", 0, 1), ("X", "O", 0, 0),
    ("Z", "A2", 1, 1), ("X", "O", 1, 1), ("Y", "A0", 2), ("X", "O", 1, 0), ("R", 1), ("Z", "A2", 0, 1),
    ("Z", "A2", 2, 1), ("Z", "A2", 3, 0), ("X", "O", 2, 1), ("R", 0), ("Z", "A2", 1, 0), ("Z", "A2", 2, 0),
    ("Z", "A2", 3, 1), ("Y", "A0", 1), ("X", "O", 3, 1), ("X", "O", 2, 0), ("Y", "O", 0), ("C", "A0", 0),
    ("Y", "O", 1), ("X", "O", 3, 0), ("C", "A1", 0), ("F1", "A2"), ("Y", "A1", 2), ("Y", "A0", 3), ("C", "A0", 1),
    ("C", "A0", 2), ("Y", "A1", 3), ("C", "O", 0), ("Y", "O", 2), ("F", "A2"), ("Y", "O", 3), ("C", "A1", 1),
    ("C", "A0", 3), ("F", "A0"), ("C", "O", 1), ("C", "O", 2), ("C", "A1", 2), ("C", "O", 3), ("C", "A1", 3),
    ("F", "O"), ("L", "A2"), ("L", "A0"), ("F", "A1"), ("L", "O"), ("L", "A1"),
)


def reduce_kernel(grads, rows_a, rows_b, total, land_a, land_b, *scratch):
    z, y, x, c = place()
    dp = z * 2 + y
    sp = x * 2 + c
    names = list(STREAMS)
    moving = [name for name in names if name != "XO"]
    planes = [name for name in moving if STREAMS[name][2]]
    scratch = list(scratch)

    def take(keys):
        return {key: scratch.pop(0) for key in keys}

    mine, core, side, line, last = take(names), take(names), take(moving), take(moving), take(planes)
    cross, = take(["cross"]).values()
    load_sem, core_send, core_recv = take(names), take(names), take(names)
    y_send, y_recv, z_send, z_recv = take(moving), take(moving), take(moving), take(moving)
    x_send, x_recv, last_send, last_recv, give_send, give_recv, keep_sem, row_send, row_recv, row_keep = scratch
    high = z // 2
    order = (3 - 3 * high, 2 - high, 1 - z + 4 * high, z)
    twin = (dp, (1 - x) * 2 + c)
    mate = (dp, x * 2 + 1 - c)
    beside = (z * 2 + 1 - y, sp)
    inner = (z > 0) & (z < NZ - 1)

    def view(ref, name, dest, core_of):
        base = dest * 6
        if name == "A0":
            return ref.at[base + core_of, pl.ds(0, BLANK)]
        if name in ("A1", "A2"):
            return ref.at[base + 2 + core_of, pl.ds(STREAMS[name][1], HALF)]
        slot = base + (4 + x if name == "O" else 5 - x)
        return ref.at[slot, pl.ds(pl.multiple_of(core_of * HALF, HALF), HALF)]

    def remote(src, dst, send, recv, target):
        return pltpu.make_async_remote_copy(
            src_ref=src, dst_ref=dst, send_sem=send, recv_sem=recv,
            device_id=target, device_id_type=MESH,
        )

    def load(name, dest):
        return pltpu.make_async_copy(view(grads, name, dest, c), mine[name].at[dest], load_sem[name].at[dest])

    def to_mate(name, dest):
        return remote(
            view(grads, name, dest, 1 - c), core[name].at[dest],
            core_send[name].at[dest], core_recv[name].at[dest], mate,
        )

    def to_twin(dest):
        return remote(mine["XO"].at[dest], cross.at[dest], x_send.at[dest], x_recv.at[dest], twin)

    def to_side(name, goal):
        at = goal if STREAMS[name][3] else 0
        return remote(
            mine[name].at[goal * 2 + 1 - y], side[name].at[at],
            y_send[name].at[at], y_recv[name].at[at], beside,
        )

    def row_copy(which, source, landing, step, arrival):
        peer = (sp + step) % 4
        at = peer if arrival else sp
        return remote(
            source.at[peer], landing.at[at],
            row_send.at[which, step - 1], row_recv.at[which, at], (dp, peer),
        )

    def column_of(flag):
        return y if flag == 0 else 1 - y

    def dest_of(task):
        if task[0] in ("X", "Z"):
            return order[task[2]] * 2 + column_of(task[3])
        return order[task[2]] * 2 + (1 - y if task[0] == "Y" else y)

    sequence = [
        ("XO" if task[0] == "X" else task[1], dest_of(task)) for task in TASKS if task[0] in ("X", "Y", "C", "Z")
    ]
    for name, dest in sequence:
        load(name, dest).start()
    keeps = [
        pltpu.make_async_copy(rows_a.at[sp], land_a.at[sp], row_keep.at[0]),
        pltpu.make_async_copy(rows_b.at[sp], land_b.at[sp], row_keep.at[1]),
    ]
    for keep in keeps:
        keep.start()
    greet(z, y, x, c)
    for name, dest in sequence:
        to_mate(name, dest).start()

    def merge(name, dest):
        load(name, dest).wait()
        to_mate(name, dest).wait_recv()
        value = mine[name][dest] + core[name][dest]
        if name == "O":
            to_twin(dest).wait_recv()
            value = value + cross[dest]
        mine[name][dest] = value

    def hop(name, goal, column, way, target):
        lane = goal if STREAMS[name][3] else goal * 2 + column
        return remote(
            mine[name].at[goal * 2 + column], line[name].at[way, lane],
            z_send[name].at[lane], z_recv[name].at[way, lane], target,
        )

    def along(name, goal, column):
        dest = goal * 2 + column
        upward = (goal > z).astype(jnp.int32)
        step = 2 * upward - 1
        way = 1 - upward
        item = hop(name, goal, column, way, (dp + 2 * step, sp))
        lane = goal if STREAMS[name][3] else dest

        @pl.when(inner)
        def _():
            item.wait_recv()
            mine[name][dest] = mine[name][dest] + line[name][way, lane]

        item.start()

    def settle(name, column):
        dest = z * 2 + column
        lane = z if STREAMS[name][3] else dest
        for way, valid, step in ((0, z > 0, 1), (1, z < NZ - 1, -1)):
            @pl.when(valid)
            def _():
                hop(name, z, column, way, (dp - 2 * step, sp)).wait_recv()
                mine[name][dest] = mine[name][dest] + line[name][way, lane]

    def swap_last(name):
        at = planes.index(name)
        return remote(mine[name].at[dp], last[name], last_send.at[at], last_recv.at[at], twin)

    def place_of(name, core_of):
        return view(total, name, 0, core_of)

    gift_at = {name: at for at, name in enumerate(planes + ["O", "twin", "XO"])}

    def give(name, key, target, source, core_of):
        at = gift_at[key]
        return remote(source, place_of(name, core_of), give_send.at[at], give_recv.at[at], target)

    gifts, kept = [], []

    def hand_on(name, key, target, source):
        item = give(name, key, target, source, c)
        item.start()
        gifts.append(item)

    def keep_here(name, source):
        item = pltpu.make_async_copy(source, place_of(name, c), keep_sem.at[gift_at[name]])
        item.start()
        kept.append(item)

    for task in TASKS:
        kind, name = task[0], task[1]
        if kind == "R":
            source, landing = ((rows_a, land_a), (rows_b, land_b))[name]
            for step in (2, 3, 1):
                row_copy(name, source, landing, step, False).start()
        elif kind == "X":
            merge("XO", dest_of(task))
            to_twin(dest_of(task)).start()
        elif kind == "Y":
            merge(name, dest_of(task))
            to_side(name, order[task[2]]).start()
        elif kind == "C":
            dest = dest_of(task)
            merge(name, dest)
            to_side(name, order[task[2]]).wait_recv()
            mine[name][dest] = mine[name][dest] + side[name][order[task[2]]]
            if task[2] < 3:
                along(name, order[task[2]], y)
        elif kind == "Z":
            merge(name, dest_of(task))
            if task[2] < 3:
                along(name, order[task[2]], column_of(task[3]))
        elif kind == "F1":
            settle(name, 1 - y)
            to_side(name, z).start()
        elif kind == "F":
            settle(name, y)
            if not STREAMS[name][3]:
                to_side(name, z).wait_recv()
                mine[name][dp] = mine[name][dp] + side[name][0]
            if name in planes:
                swap_last(name).start()
            else:
                hand_on(name, "twin", twin, mine[name].at[dp])
                hand_on(name, "O", mate, mine[name].at[dp])
                keep_here(name, mine[name].at[dp])
        elif kind == "L":
            if name in planes:
                swap_last(name).wait_recv()
                core[name][dp] = mine[name][dp] + last[name][...]
                hand_on(name, name, mate, core[name].at[dp])
                keep_here(name, core[name].at[dp])
            else:
                give("XO", "twin", twin, place_of("XO", c), c).wait_recv()
                hand_on("XO", "XO", mate, place_of("XO", c))

    for name in planes + ["O", "XO"]:
        give(name, name, mate, place_of(name, 1 - c), 1 - c).wait_recv()
    for step in (2, 3, 1):
        for which, source, landing in ((0, rows_a, land_a), (1, rows_b, land_b)):
            row_copy(which, source, landing, step, True).wait_recv()
            row_copy(which, source, landing, step, False).wait_send()
    for name, dest in sequence:
        to_mate(name, dest).wait_send()
    for i in range(4):
        for column in (0, 1):
            to_twin(order[i] * 2 + column).wait_send()
        for name in moving:
            if STREAMS[name][3]:
                to_side(name, order[i]).wait_send()
                if i < 3:
                    hop(name, order[i], y, 0, twin).wait_send()
            elif i < 3:
                for column in (0, 1):
                    hop(name, order[i], column, 0, twin).wait_send()
            else:
                to_side(name, z).wait_send()
    for name in planes:
        swap_last(name).wait_send()
    for item in gifts:
        item.wait_send()
    for item in kept + keeps:
        item.wait()


def reduce_all(grads, rows_a, rows_b):
    anywhere = pl.BlockSpec(memory_space=pl.ANY)
    half = jnp.bfloat16
    dma = pltpu.SemaphoreType.DMA
    moving = [name for name in STREAMS if name != "XO"]
    planes = [name for name in moving if STREAMS[name][2]]

    def buffers(shapes):
        return [pltpu.VMEM((*lead, STREAMS[name][0], BLK), half) for name, lead in shapes]

    first = {name: STREAMS[name][3] for name in moving}
    return pl.pallas_call(
        reduce_kernel,
        name="reduce_all",
        out_shape=[
            jax.ShapeDtypeStruct((6, PITCH, BLK), half),
            pltpu.HBM(rows_a.shape, half),
            pltpu.HBM(rows_b.shape, half),
        ],
        in_specs=[anywhere] * 3,
        out_specs=[anywhere] * 3,
        scratch_shapes=buffers([(name, (8,)) for name in STREAMS] * 2)
        + buffers([(name, (4 if first[name] else 1,)) for name in moving])
        + buffers([(name, (2, 4 if first[name] else 8)) for name in moving])
        + buffers([(name, ()) for name in planes])
        + buffers([("O", (8,))])
        + [dma((8,))] * (3 * len(STREAMS))
        + [dma((4 if first[name] else 1,)) for name in moving] * 2
        + [dma((4 if first[name] else 8,)) for name in moving]
        + [dma((2, 4 if first[name] else 8)) for name in moving]
        + [
            dma((8,)), dma((8,)), dma((len(planes),)), dma((len(planes),)), dma((len(planes) + 3,)),
            dma((len(planes) + 3,)), dma((len(planes) + 1,)), dma((2, 3)), dma((2, 4)), dma((2,)),
        ],
        compiler_params=pltpu.CompilerParams(
            collective_id=1, has_side_effects=True, vmem_limit_bytes=28 << 20
        ),
    )(in_hbm(grads), in_hbm(rows_a), in_hbm(rows_b))


CORRECT = 1.0 - 0.5**STEP
GROUP = 2


def update_kernel(
    total, weights, first, second, left, right, left_rot, right_rot, vec, vec_first, vec_second, land_a, land_b,
    moment_one, moment_two, left_new, right_new, weights_new, weights_half, vector_one, vector_two, vector_new,
    rows_a, rows_b, held, narrow, wide, stage, stage_half, out_sem, sems,
):
    half = jnp.bfloat16
    take_a = pltpu.make_async_copy(land_a, held, sems.at[0])
    give_a = pltpu.make_async_copy(held, rows_a, sems.at[3])
    take_b = pltpu.make_async_copy(land_b, narrow, sems.at[1])
    give_b = pltpu.make_async_copy(wide, rows_b, sems.at[2])
    take_b.start()
    take_a.start()
    slope = total[0, pl.ds(BLK, 1), :].astype(jnp.float32)
    vec_one = 0.5 * vec_first[...] + 0.5 * slope
    vec_two = 0.5 * vec_second[...] + 0.5 * slope * slope
    vector_one[...] = vec_one
    vector_two[...] = vec_two
    vector_new[...] = vec[...] - rate_vector * (
        (vec_one / CORRECT) / (jnp.sqrt(vec_two / CORRECT) + 1e-08)
    )
    targets = (left_new, right_new, moment_one, moment_two, weights_new)

    def outputs(i):
        copies = [
            pltpu.make_async_copy(stage.at[k, i], target.at[i], out_sem.at[i, k])
            for k, target in enumerate(targets)
        ]
        return copies + [pltpu.make_async_copy(stage_half.at[i], weights_half.at[i], out_sem.at[i, 5])]

    def blocks(pair, carry):
        for i in [pair * GROUP + k for k in range(GROUP)]:
            grad = total[i, :BLK, :]
            rot_l = left_rot[i].astype(half)
            rot_r = right_rot[i].astype(half)
            turned = dot_nn(dot_tn(rot_l, grad).astype(half), rot_r)
            stage[0, i] = 0.95 * left[i] + 0.05 * dot_nt(grad, grad)
            one = 0.5 * first[i] + 0.5 * turned
            two = 0.5 * second[i] + 0.5 * turned * turned
            stage[2, i] = one
            stage[3, i] = two
            ratio = (one / CORRECT) / (jnp.sqrt(two / CORRECT) + 1e-08)
            stage[1, i] = 0.95 * right[i] + 0.05 * dot_tn(grad, grad)
            stepped = dot_nt(dot_nn(rot_l, ratio.astype(half)).astype(half), rot_r)
            fresh = weights[i] - rate_matrix * stepped
            stage[4, i] = fresh
            stage_half[i] = fresh.astype(half)
        for i in [pair * GROUP + k for k in range(GROUP)]:
            for item in outputs(i):
                item.start()

        @pl.when(pair == 0)
        def _():
            take_a.wait()
            give_a.start()
            take_b.wait()
            for r in range(narrow.shape[0]):
                wide[r] = narrow[r].astype(jnp.float32)
            give_b.start()

        return carry

    lax.fori_loop(0, weights.shape[0] // GROUP, blocks, 0)
    for i in range(weights.shape[0]):
        for item in outputs(i):
            item.wait()
    give_a.wait()
    give_b.wait()


def update_all(
    total, weights, first, second, left, right, left_rot, right_rot, vec, vec_first, vec_second, land_a, land_b
):
    full = jnp.float32
    vmem = pl.BlockSpec(memory_space=pltpu.VMEM)
    anywhere = pl.BlockSpec(memory_space=pl.ANY)
    vector = jax.ShapeDtypeStruct((1, BLK), full)
    matrix = pltpu.HBM(weights.shape, full)
    return pl.pallas_call(
        update_kernel,
        name="update_all",
        out_shape=[matrix] * 5 + [pltpu.HBM(weights.shape, jnp.bfloat16)] + [vector] * 3
        + [pltpu.HBM(land_a.shape, jnp.bfloat16), pltpu.HBM(land_b.shape, full)],
        in_specs=[vmem] * 11 + [anywhere] * 2,
        out_specs=[anywhere] * 6 + [vmem] * 3 + [anywhere] * 2,
        scratch_shapes=[
            pltpu.VMEM(land_a.shape, jnp.bfloat16),
            pltpu.VMEM(land_b.shape, jnp.bfloat16),
            pltpu.VMEM(land_b.shape, full),
            pltpu.VMEM((5, *weights.shape), full),
            pltpu.VMEM(weights.shape, jnp.bfloat16),
            pltpu.SemaphoreType.DMA((weights.shape[0], 6)),
            pltpu.SemaphoreType.DMA((4,)),
        ],
        compiler_params=pltpu.CompilerParams(vmem_limit_bytes=30 << 20),
    )(
        total, weights, first, second, left, right, left_rot, right_rot,
        vec.reshape(1, BLK), vec_first.reshape(1, BLK), vec_second.reshape(1, BLK), in_hbm(land_a), in_hbm(land_b),
    )


def fast_device(
    tokens, output_grad, segment_ids, lengths, owner_slot, slot_weights, first_moment, second_moment,
    left_stats, right_stats, left_basis, right_basis, vector_values, vector_first, vector_second,
):
    gathered, token_row, grad_row = gather_all(slot_weights, vector_values, tokens, output_grad)
    placed, block_row, input_row = run_layer(
        owner_slot, gathered, token_row.reshape(-1, D), grad_row.reshape(-1, D), segment_ids
    )
    total, block_land, input_land = reduce_all(
        placed, block_row.reshape(tokens.shape), input_row.reshape(tokens.shape)
    )
    updated = update_all(
        total, slot_weights, first_moment, second_moment, left_stats, right_stats, left_basis, right_basis,
        vector_values, vector_first, vector_second, block_land, input_land,
    )
    vectors = [value.reshape(-1) for value in updated[6:9]]
    return (updated[9], updated[10], *updated[:6], *vectors)


def solution(mesh):
    in_specs = (
        P("dp", "sp", None),
        P("dp", "sp", None),
        P("dp", None),
        P("dp", None),
        P(),
        P("dp", None, None),
        P("dp", None, None),
        P("dp", None, None),
        P("dp", None, None),
        P("dp", None, None),
        P("dp", None, None),
        P("dp", None, None),
        P("dp"),
        P("dp"),
        P("dp"),
    )
    out_specs = (
        P("dp", "sp", None),
        P("dp", "sp", None),
        P("dp", None, None),
        P("dp", None, None),
        P("dp", None, None),
        P("dp", None, None),
        P("dp", None, None),
        P("dp", None, None),
        P("dp"),
        P("dp"),
        P("dp"),
    )
    chosen = fast_device if dict(mesh.shape) == {"dp": 8, "sp": 4} else per_device
    return jax.shard_map(
        chosen, mesh=mesh, in_specs=in_specs, out_specs=out_specs, check_vma=False
    )
```

```python
import math

import jax
import jax.numpy as jnp
from jax import lax
from jax.experimental import pallas as pl
from jax.experimental.pallas import tpu as pltpu
from jax.sharding import PartitionSpec as P

D = 768
HD = 64
FF = 3072
BLK = 384
STEP = 4


highest = lax.Precision.HIGHEST
rate_matrix = 0.04
rate_vector = 0.2


def layer_norm(summed, gain, shift):
    centre = jnp.mean(summed, axis=-1, keepdims=True)
    centred = summed - centre
    spread = jnp.mean(centred * centred, axis=-1, keepdims=True)
    return centred * lax.rsqrt(spread + 1e-06) * gain + shift


def exact_gelu(values):
    return jax.nn.gelu(values, approximate=False)


def passage_mask(segment_row, length_row):
    starts = jnp.cumsum(length_row) - length_row
    number = length_row.shape[0]
    onehot = (segment_row[:, None] == jnp.arange(number, dtype=jnp.int32)[None, :]).astype(
        jnp.int32
    )
    opening = jnp.sum(onehot * starts[None, :], axis=1)
    closing = opening + jnp.sum(onehot * length_row[None, :], axis=1)
    places = jnp.arange(segment_row.shape[0], dtype=jnp.int32)
    return (places[None, :] >= opening[:, None]) & (places[None, :] < closing[:, None])


def into_blocks(matrix):
    height, breadth = matrix.shape
    return (
        matrix.reshape(height // BLK, BLK, breadth // BLK, BLK)
        .transpose(0, 2, 1, 3)
        .reshape(-1, BLK, BLK)
    )


def from_blocks(blocks, height, breadth):
    return (
        blocks.reshape(height // BLK, breadth // BLK, BLK, BLK)
        .transpose(0, 2, 1, 3)
        .reshape(height, breadth)
    )


def split_blocks(blocks):
    square = (D // BLK) ** 2
    broad = D * FF // (BLK * BLK)
    w_query = from_blocks(blocks[0:square], D, D)
    w_key = from_blocks(blocks[square : 2 * square], D, D)
    w_value = from_blocks(blocks[2 * square : 3 * square], D, D)
    w_output = from_blocks(blocks[3 * square : 4 * square], D, D)
    w_upward = from_blocks(blocks[4 * square : 4 * square + broad], D, FF)
    w_downward = from_blocks(blocks[4 * square + broad : 4 * square + 2 * broad], FF, D)
    return (w_query, w_key, w_value, w_output, w_upward, w_downward)


def contract_rows(left_mat, right_mat):
    return lax.dot_general(
        left_mat, right_mat, (((0,), (0,)), ((), ())), preferred_element_type=jnp.float32
    )


def contract_cols(left_mat, right_mat):
    return lax.dot_general(
        left_mat, right_mat, (((1,), (1,)), ((), ())), preferred_element_type=jnp.float32
    )


def soap_update(
    gradient, weights, moment_old, second_old, left_old, right_old, left_rot, right_rot
):
    left_next = 0.95 * left_old + 0.05 * jnp.einsum(
        "nij,nkj->nik", gradient, gradient, precision=highest
    )
    right_next = 0.95 * right_old + 0.05 * jnp.einsum(
        "nji,njk->nik", gradient, gradient, precision=highest
    )
    turned = jnp.einsum("nji,njk->nik", left_rot, gradient, precision=highest)
    turned = jnp.einsum("nij,njk->nik", turned, right_rot, precision=highest)
    moment_next = 0.5 * moment_old + 0.5 * turned
    second_next = 0.5 * second_old + 0.5 * turned * turned
    correct = 1.0 - 0.5**STEP
    ratio = moment_next / correct / (jnp.sqrt(second_next / correct) + 1e-08)
    stepped = jnp.einsum("nij,njk->nik", left_rot, ratio, precision=highest)
    stepped = jnp.einsum("nij,nkj->nik", stepped, right_rot, precision=highest)
    return (moment_next, second_next, left_next, right_next, weights - rate_matrix * stepped)


def adam_update(gradient, values, moment_old, second_old):
    moment_next = 0.5 * moment_old + 0.5 * gradient
    second_next = 0.5 * second_old + 0.5 * gradient * gradient
    correct = 1.0 - 0.5**STEP
    ratio = moment_next / correct / (jnp.sqrt(second_next / correct) + 1e-08)
    return (moment_next, second_next, values - rate_vector * ratio)


def masked_scores(joint_row, segment_row, length_row):
    positions = joint_row.shape[0]
    query = joint_row[:, 0].reshape(positions, -1, HD)
    keyed = joint_row[:, 1].reshape(positions, -1, HD)
    valued = joint_row[:, 2].reshape(positions, -1, HD)
    scores = jnp.einsum("qhd,khd->hqk", query, keyed, preferred_element_type=jnp.float32) * 0.125
    visible = passage_mask(segment_row, length_row)
    return (jnp.where(visible[None], scores, -1e30), query, keyed, valued)


def attend_rows(item):
    joint_row, segment_row, length_row = item
    scores, query, keyed, valued = masked_scores(joint_row, segment_row, length_row)
    largest = jnp.max(scores, axis=-1, keepdims=True)
    raised = jnp.exp(scores - largest)
    totals = jnp.sum(raised, axis=-1, keepdims=True)
    probs = raised / totals
    logsum = (largest + jnp.log(totals))[..., 0]
    context = jnp.einsum(
        "hqk,khd->qhd", probs.astype(jnp.bfloat16), valued, preferred_element_type=jnp.float32
    )
    return (context.reshape(joint_row.shape[0], -1).astype(jnp.bfloat16), logsum)


def back_rows(item):
    joint_row, logsum, delta_context, segment_row, length_row = item
    positions = joint_row.shape[0]
    scores, query, keyed, valued = masked_scores(joint_row, segment_row, length_row)
    probs = jnp.exp(scores - logsum[..., None])
    delta_ctx = delta_context.reshape(positions, -1, HD)
    delta_value = jnp.einsum(
        "hqk,qhd->khd", probs.astype(jnp.bfloat16), delta_ctx, preferred_element_type=jnp.float32
    )
    delta_prob = jnp.einsum("qhd,khd->hqk", delta_ctx, valued, preferred_element_type=jnp.float32)
    weighted = jnp.sum(probs * delta_prob, axis=-1, keepdims=True)
    delta_score = (probs * (delta_prob - weighted)).astype(jnp.bfloat16)
    delta_query = (
        jnp.einsum("hqk,khd->qhd", delta_score, keyed, preferred_element_type=jnp.float32) * 0.125
    )
    delta_key = (
        jnp.einsum("hqk,qhd->khd", delta_score, query, preferred_element_type=jnp.float32) * 0.125
    )
    stacked = jnp.stack(
        [
            delta_query.reshape(positions, -1),
            delta_key.reshape(positions, -1),
            delta_value.reshape(positions, -1),
        ],
        axis=1,
    )
    return stacked.astype(jnp.bfloat16)


def pick_blocks(source, slot_index, owner_slot, fanout, part_index):
    matches = owner_slot[None, :] == slot_index[:, None]
    present = jnp.any(matches, axis=1).astype(jnp.float32)
    chosen = jnp.sum(
        matches.astype(jnp.int32) * jnp.arange(owner_slot.shape[0], dtype=jnp.int32)[None, :],
        axis=1,
    )
    picked = jnp.take(source, chosen * fanout + part_index, axis=0)
    return picked * present[:, None, None]


def per_device(
    tokens,
    output_grad,
    segment_ids,
    lengths,
    owner_slot,
    slot_weights,
    first_moment,
    second_moment,
    left_stats,
    right_stats,
    left_basis,
    right_basis,
    vector_values,
    vector_first,
    vector_second,
):
    holding = slot_weights.shape[0]
    row_count = tokens.shape[0]
    token_count = tokens.shape[1]
    gathered, vector_half = (
        lax.all_gather(slot_weights.astype(jnp.bfloat16), "dp", axis=0, tiled=True),
        lax.all_gather(vector_values.astype(jnp.bfloat16), "dp", axis=0, tiled=True),
    )
    blocks = jnp.take(gathered, owner_slot, axis=0)
    w_query, w_key, w_value, w_output, w_upward, w_downward = split_blocks(blocks)
    w_joint = jnp.concatenate([w_query, w_key, w_value], axis=1)
    gains = vector_half.astype(jnp.float32).reshape(4, D)
    flat_tokens = tokens.reshape(-1, D)
    projected = jnp.dot(flat_tokens, w_joint, preferred_element_type=jnp.float32).astype(
        jnp.bfloat16
    )
    projected = projected.reshape(row_count, token_count, 3, D)
    heads = lax.all_to_all(projected, "sp", split_axis=3, concat_axis=1, tiled=True)
    context, logsum = lax.map(attend_rows, (heads, segment_ids, lengths))
    context_tok = lax.all_to_all(context, "sp", split_axis=1, concat_axis=2, tiled=True).reshape(
        -1, D
    )
    attended = jnp.dot(context_tok, w_output, preferred_element_type=jnp.float32)
    summed_one = flat_tokens.astype(jnp.float32) + attended
    hidden, norm_one_pull = jax.vjp(layer_norm, summed_one, gains[0], gains[1])
    hidden_half = hidden.astype(jnp.bfloat16)
    upward = jnp.dot(hidden_half, w_upward, preferred_element_type=jnp.float32)
    activated, gelu_pull = jax.vjp(exact_gelu, upward)
    active_half = activated.astype(jnp.bfloat16)
    downward = jnp.dot(active_half, w_downward, preferred_element_type=jnp.float32)
    result, norm_two_pull = jax.vjp(layer_norm, hidden + downward, gains[2], gains[3])
    block_out = result.astype(jnp.bfloat16).reshape(row_count, token_count, D)
    cotangent = output_grad.reshape(-1, D).astype(jnp.float32)
    delta_two, delta_gain_two, delta_shift_two = norm_two_pull(cotangent)
    delta_down = delta_two.astype(jnp.bfloat16)
    grad_down = contract_rows(active_half, delta_down)
    delta_active = contract_cols(delta_down, w_downward)
    (delta_upward,) = gelu_pull(delta_active)
    delta_up = delta_upward.astype(jnp.bfloat16)
    grad_up = contract_rows(hidden_half, delta_up)
    delta_hidden = delta_two + contract_cols(delta_up, w_upward)
    delta_one, delta_gain_one, delta_shift_one = norm_one_pull(delta_hidden)
    delta_attn = delta_one.astype(jnp.bfloat16)
    grad_output = contract_rows(context_tok, delta_attn)
    delta_context = (
        contract_cols(delta_attn, w_output).astype(jnp.bfloat16).reshape(row_count, token_count, D)
    )
    delta_heads = lax.all_to_all(delta_context, "sp", split_axis=2, concat_axis=1, tiled=True)
    delta_projected = lax.map(back_rows, (heads, logsum, delta_heads, segment_ids, lengths))
    delta_joint = lax.all_to_all(
        delta_projected, "sp", split_axis=1, concat_axis=3, tiled=True
    ).reshape(-1, 3 * D)
    grad_joint = contract_rows(flat_tokens, delta_joint)
    input_grad = (delta_one + contract_cols(delta_joint, w_joint)).reshape(
        row_count, token_count, D
    )
    grad_blocks = jnp.concatenate(
        [
            into_blocks(grad_joint[:, :D]),
            into_blocks(grad_joint[:, D : 2 * D]),
            into_blocks(grad_joint[:, 2 * D :]),
            into_blocks(grad_output),
            into_blocks(grad_up),
            into_blocks(grad_down),
        ],
        axis=0,
    )
    vector_grad = jnp.concatenate(
        [delta_gain_one, delta_shift_one, delta_gain_two, delta_shift_two]
    )
    vector_total = lax.psum(vector_grad, ("dp", "sp"))
    piece_len = vector_values.shape[0]
    vector_piece = lax.dynamic_slice_in_dim(
        vector_total, lax.axis_index("dp") * piece_len, piece_len
    )
    slot_index = jnp.arange(holding * lax.axis_size("dp"), dtype=jnp.int32)
    owned = lax.psum_scatter(
        pick_blocks(grad_blocks, slot_index, owner_slot, 1, 0),
        "dp",
        scatter_dimension=0,
        tiled=True,
    )
    owned = lax.psum(owned.astype(jnp.bfloat16), "sp").astype(jnp.float32)
    moment_one, moment_two, left_new, right_new, weights_new = soap_update(
        owned,
        slot_weights,
        first_moment,
        second_moment,
        left_stats,
        right_stats,
        left_basis,
        right_basis,
    )
    vector_one, vector_two, vector_new = adam_update(
        vector_piece, vector_values, vector_first, vector_second
    )
    return (
        block_out,
        input_grad,
        moment_one,
        moment_two,
        left_new,
        right_new,
        weights_new,
        weights_new.astype(jnp.bfloat16),
        vector_one,
        vector_two,
        vector_new,
    )


PITCH = BLK + 16
MESH = pl.DeviceIdType.MESH
NZ = 4


def in_hbm(value):
    return pltpu.with_memory_space_constraint(value, pltpu.HBM)


def place():
    dp = lax.axis_index("dp")
    sp = lax.axis_index("sp")
    return dp // 2, dp % 2, sp // 2, sp % 2


def greet(z, y, x, c):
    barrier = pltpu.get_barrier_semaphore()
    dp = z * 2 + y
    sp = x * 2 + c

    def signal(target):
        pl.semaphore_signal(barrier, 1, device_id=target, device_id_type=MESH)

    for step in range(1, 4):
        signal((dp, (sp + step) % 4))
    signal((z * 2 + 1 - y, sp))

    @pl.when(z < NZ - 1)
    def _():
        signal((dp + 2, sp))

    @pl.when(z > 0)
    def _():
        signal((dp - 2, sp))

    pl.semaphore_wait(barrier, 4 + (z < NZ - 1).astype(jnp.int32) + (z > 0).astype(jnp.int32))


PIECES = {
    "A0": (BLK + 16, False, True),
    "A1": (BLK // 2, False, False),
    "O0": (BLK // 2, True, True),
    "O1": (BLK // 4, True, True),
}
STEPS = (
    ("own", "O1"), ("rows", 1), ("own", "O0"), ("own", "A1"), ("z", "O1", 1, 1, 0), ("z", "O1", 1, -1, 0),
    ("y", "O1", 0, 0), ("z", "O0", 1, 1, 0), ("own", "A0"), ("z", "O0", 2, 1, 0), ("y", "O0", 0, 0),
    ("z", "O0", 1, -1, 0), ("z", "O1", 2, -1, 0), ("y", "O1", 1, -1), ("z", "O1", 3, -1, 0), ("z", "A1", 1, 1, 0),
    ("z", "O1", 2, 1, 0), ("y", "O1", 1, 1), ("z", "O0", 3, 1, 0), ("z", "A0", 1, -1, 0), ("y", "O1", 2, -1),
    ("y", "O0", 1, 1), ("z", "O1", 3, 1, 0), ("y", "O0", 2, 1), ("x", "O0", 3, 1, 0), ("x", "O1", 3, -1, 0),
    ("x", "O1", 1, 1, 0), ("z", "A1", 1, -1, 0), ("x", "O0", 1, -1, 0), ("z", "A0", 1, 1, 0),
    ("x", "O1", 1, -1, 1), ("y", "O1", 3, -1), ("y", "A1", 0, 0), ("z", "A0", 2, 1, 0), ("x", "O0", 2, 1, 0),
    ("y", "O1", 2, 1), ("rows", 0), ("z", "O0", 2, -1, 0), ("x", "O0", 2, 1, 1), ("z", "A0", 2, -1, 0),
    ("x", "O1", 0, 0, 1), ("z", "A1", 1, 1, 1), ("x", "O0", 1, 1, 1), ("z", "O0", 3, -1, 0), ("z", "A1", 1, -1, 1),
    ("y", "O0", 2, -1), ("y", "O0", 3, 1), ("y", "A0", 1, -1), ("x", "O1", 2, 1, 1), ("x", "O1", 3, 1, 0),
    ("x", "O0", 0, 0, 1), ("y", "O0", 3, -1), ("z", "A0", 3, 1, 0), ("y", "O1", 3, 1), ("z", "A0", 3, -1, 0),
    ("x", "O0", 1, 1, 0), ("x", "O1", 3, -1, 1), ("y", "O0", 1, -1), ("z", "A1", 2, -1, 0), ("y", "A0", 0, 0),
    ("x", "O1", 2, -1, 1), ("y", "A0", 2, -1), ("z", "A1", 2, -1, 1), ("x", "O0", 2, -1, 0), ("z", "A1", 3, -1, 0),
    ("x", "O0", 3, -1, 0), ("x", "O0", 3, -1, 1), ("z", "A1", 2, 1, 1), ("y", "A0", 2, 1), ("z", "A1", 2, 1, 0),
    ("x", "O0", 3, 1, 1), ("x", "O1", 2, -1, 0), ("z", "A1", 3, 1, 1), ("x", "O1", 2, 1, 0), ("x", "O0", 2, -1, 1),
    ("y", "A0", 3, -1), ("y", "A0", 1, 1), ("y", "A0", 3, 1), ("x", "O1", 3, 1, 1), ("x", "O1", 1, -1, 0),
    ("x", "O1", 1, 1, 1), ("x", "O0", 1, -1, 1), ("z", "A1", 3, -1, 1), ("z", "A1", 3, 1, 0),
)


def piece_view(ref, name, x_of, c_of, base):
    height = PIECES[name][0]
    if name == "A0":
        return ref.at[base + c_of, pl.ds(0, height)]
    if name == "A1":
        slot, row = base + 2, height * c_of
    elif name == "O0":
        slot, row = base + 4 + x_of, height * c_of
    else:
        slot, row = base + 3, 2 * height * x_of + height * c_of
    return ref.at[slot, pl.ds(pl.multiple_of(row, height), height)]


def gather_kernel(weights, vector, tokens, grads, out, token_row, grad_row, wide, narrow, *sems):
    z, y, x, c = place()
    dp = z * 2 + y
    sp = x * 2 + c
    sems = list(sems)
    load_sem, keep_sem, row_send, row_recv, row_keep = [sems.pop(0) for _ in range(5)]
    ways = ("up", "down", "y", "mate", "x", "pass")
    send_sem = {(way, name): sems.pop(0) for way in ways for name in PIECES if PIECES[name][1] or way not in ways[4:]}
    recv_sem = {(way, name): sems.pop(0) for way in ways[2:] for name in PIECES if PIECES[name][1] or way not in ways[4:]}
    targets = {
        "up": (dp + 2, sp), "down": (dp - 2, sp), "y": (z * 2 + 1 - y, sp),
        "x": (dp, (1 - x) * 2 + c), "mate": (dp, x * 2 + 1 - c), "pass": (dp, x * 2 + 1 - c),
    }
    def load_of(i):
        return pltpu.make_async_copy(weights.at[i], wide.at[i], load_sem.at[i])

    for i in (c, 2, 3, 4 + x, 1 - c, 5 - x):
        load_of(i).start()
    keeps = [
        pltpu.make_async_copy(tokens.at[sp], token_row.at[sp], row_keep.at[0]),
        pltpu.make_async_copy(grads.at[sp], grad_row.at[sp], row_keep.at[1]),
    ]
    for keep in keeps:
        keep.start()
    gains = jnp.broadcast_to(vector[...], (16, BLK)).astype(jnp.bfloat16)
    greet(z, y, x, c)

    def row_copy(which, source, landing, step, arrival):
        peer = (sp + step) % 4
        at = peer if arrival else sp
        return pltpu.make_async_remote_copy(
            src_ref=source.at[peer], dst_ref=landing.at[at],
            send_sem=row_send.at[which, step - 1], recv_sem=row_recv.at[which, at],
            device_id=(dp, peer), device_id_type=MESH,
        )

    def round_block(i):
        load_of(i).wait()
        narrow[i, :BLK, :] = wide[i].astype(jnp.bfloat16)
        narrow[i, BLK:, :] = gains

    for i in (c, 2, 3, 4 + x):
        round_block(i)
    own = [pltpu.make_async_copy(narrow.at[i], out.at[dp * 6 + i], keep_sem.at[i]) for i in range(6)]
    started = []

    def item_of(way, name, holder, x_of, c_of, fresh=False):
        landing = piece_view(out, name, x_of, c_of, holder * 6)
        arrives = way if way in ("mate", "x", "pass") else "y"
        return pltpu.make_async_remote_copy(
            src_ref=piece_view(narrow, name, x_of, c_of, 0) if fresh else landing, dst_ref=landing,
            send_sem=send_sem[way, name].at[holder], recv_sem=recv_sem[arrives, name].at[holder],
            device_id=targets[way], device_id_type=MESH,
        )

    def send(way, name, holder, valid, x_of=x, fresh=False):
        if way in ("up", "down"):
            room = z < NZ - 1 if way == "up" else z > 0
            valid = room if valid is None else valid & room
        item = item_of(way, name, holder, x_of, c, fresh)
        if valid is None:
            item.start()
        else:
            pl.when(valid)(item.start)
        started.append((item, valid))

    def arrive(way, name, holder, valid, x_of, c_of):
        item = item_of(way, name, holder, x_of, c_of)
        if valid is None:
            item.wait_recv()
        else:
            pl.when(valid)(item.wait_recv)

    def origin_of(sign, far):
        origin = z + sign * far
        if far == 0:
            return origin, None
        return origin, ((origin >= 0) if sign < 0 else (origin <= NZ - 1))

    for step in STEPS:
        kind, name = step[0], step[1]
        if kind == "own":
            for way in ("up", "down", "y"):
                send(way, name, dp, None, fresh=True)
        elif kind == "rows":
            source, landing = ((tokens, token_row), (grads, grad_row))[name]
            for hop in (2, 3, 1):
                row_copy(name, source, landing, hop, False).start()
        else:
            origin, inside = origin_of(step[3], step[2])
            if kind == "x":
                holder = origin * 2 + (y if step[4] == 0 else 1 - y)
                arrive("x", name, holder, inside, 1 - x, c)
                send("pass", name, holder, inside, 1 - x)
                continue
            holder = origin * 2 + (y if kind == "z" and step[4] == 0 else 1 - y)
            arrive("y", name, holder, inside, x, c)
            if kind == "z":
                if step[2] < NZ - 1:
                    send("up" if step[3] < 0 else "down", name, holder, inside)
                if PIECES[name][2] and step[4] == 0:
                    send("y", name, holder, inside)
            elif not PIECES[name][2]:
                send("up", name, holder, inside)
                send("down", name, holder, inside)
            if PIECES[name][1]:
                send("x", name, holder, inside)
            send("mate", name, holder, inside)
        if kind == "own" and name == "A0":
            for i in (1 - c, 5 - x):
                round_block(i)
            for item in own:
                item.start()

    for far in range(NZ):
        for sign in (0,) if far == 0 else (-1, 1):
            origin, inside = origin_of(sign, far)
            for column in (1,) if far == 0 else (0, 1):
                holder = origin * 2 + (y if column == 0 else 1 - y)
                for name in PIECES:
                    arrive("mate", name, holder, inside, x, 1 - c)
                    if PIECES[name][1]:
                        arrive("pass", name, holder, inside, 1 - x, 1 - c)
    for hop in (2, 3, 1):
        for which, source, landing in ((0, tokens, token_row), (1, grads, grad_row)):
            row_copy(which, source, landing, hop, True).wait_recv()
            row_copy(which, source, landing, hop, False).wait_send()
    for item, valid in started:
        if valid is None:
            item.wait_send()
        else:
            pl.when(valid)(item.wait_send)
    for item in own + keeps:
        item.wait()


def gather_all(weights, vector, tokens, grads):
    anywhere = pl.BlockSpec(memory_space=pl.ANY)
    dma = pltpu.SemaphoreType.DMA
    carried = sum(1 for name in PIECES if PIECES[name][1])
    flows = (4 * len(PIECES) + 2 * carried) + (2 * len(PIECES) + 2 * carried)
    return pl.pallas_call(
        gather_kernel,
        name="gather_all",
        out_shape=[
            pltpu.HBM((48, PITCH, BLK), jnp.bfloat16),
            pltpu.HBM(tokens.shape, jnp.bfloat16),
            pltpu.HBM(grads.shape, jnp.bfloat16),
        ],
        in_specs=[anywhere, pl.BlockSpec(memory_space=pltpu.VMEM), anywhere, anywhere],
        out_specs=[anywhere, anywhere, anywhere],
        scratch_shapes=[
            pltpu.VMEM((6, BLK, BLK), jnp.float32),
            pltpu.VMEM((6, PITCH, BLK), jnp.bfloat16),
            dma((6,)), dma((6,)), dma((2, 3)), dma((2, 4)), dma((2,)),
        ]
        + [dma((8,))] * flows,
        compiler_params=pltpu.CompilerParams(
            collective_id=0, has_side_effects=True, vmem_limit_bytes=24 << 20
        ),
    )(in_hbm(weights), vector.reshape(1, BLK), in_hbm(tokens), in_hbm(grads))


ROW = 512
PAIR = 128
SPAN = 384
EPS = 1e-06


def gelu_of(u):
    bell = jnp.exp(-0.5 * u * u)
    t = 1.0 / (1.0 + (0.3275911 / math.sqrt(2.0)) * jnp.abs(u))
    tail = 0.5 * 1.061405429
    for term in (-1.453152027, 1.421413741, -0.284496736, 0.254829592):
        tail = tail * t + 0.5 * term
    tail = tail * t * bell
    below = jnp.where(u >= 0.0, 1.0 - tail, tail)
    return (u * below).astype(jnp.bfloat16), below + u * (bell * (1.0 / math.sqrt(2.0 * math.pi)))


def dot_nn(a, b):
    return lax.dot_general(a, b, (((1,), (0,)), ((), ())), preferred_element_type=jnp.float32)


def dot_nt(a, b):
    return lax.dot_general(a, b, (((1,), (1,)), ((), ())), preferred_element_type=jnp.float32)


def dot_tn(a, b):
    return lax.dot_general(a, b, (((0,), (0,)), ((), ())), preferred_element_type=jnp.float32)


def layer_kernel(
    owner, weights, tokens, dy_ref, segments, grads, block_out, input_half,
    wqkv, wo, w1, w2, gains, qkv, probs, shares, held, context, hidden, hidden16, norm1, act, slope, acc, dz, dz16,
    dqkv, dup, stage, flipped, flipped_hidden, ups, vecs, spread, w_sem, g_sem, v_sem,
):
    half = jnp.bfloat16
    sp = lax.axis_index("sp")

    def weight_copies():
        copies = []
        for which, ref in enumerate((wqkv.at[0], wqkv.at[1], wqkv.at[2], wo)):
            for r in range(2):
                for q in range(2):
                    copies.append((which * 4 + r * 2 + q, ref, r, q))
        for r in range(2):
            for q in range(8):
                copies.append((16 + r * 8 + q, w1.at[q // 2], r, q % 2))
        for r in range(8):
            for q in range(2):
                copies.append((32 + r * 2 + q, w2.at[r // 2], r % 2, q))
        return [
            pltpu.make_async_copy(
                weights.at[owner[b], pl.ds(0, BLK)],
                ref.at[pl.ds(r * BLK, BLK), pl.ds(q * BLK, BLK)],
                w_sem.at[b],
            )
            for b, ref, r, q in copies
        ]

    copies = weight_copies()
    gain_copies = [
        pltpu.make_async_copy(
            weights.at[6 * d, pl.ds(BLK, 16)], gains.at[d // 2, :, pl.ds((d % 2) * BLK, BLK)], g_sem.at[d]
        )
        for d in range(8)
    ]
    for item in copies[:16] + gain_copies + copies[16:]:
        item.start()

    seg_row = segments[pl.ds(sp, 1), :].astype(jnp.float32)
    spread[...] = jnp.transpose(jnp.broadcast_to(seg_row, (PAIR, ROW)))

    for item in copies[:12]:
        item.wait()
    x = tokens[...]
    flipped[...] = jnp.transpose(x)
    for part in range(3):
        block = dot_nn(x, wqkv[part])
        if part == 0:
            block = block * 0.125
        block = block.astype(half)
        for p in range(6):
            qkv[part * 6 + p] = block[:, p * PAIR : (p + 1) * PAIR]

    lane = lax.broadcasted_iota(jnp.int32, (1, PAIR), 1)
    lows = (lane < 64, lane >= 64)

    def visible(part):
        keys = segments[pl.ds(sp, 1), pl.ds(part * PAIR, SPAN)].astype(jnp.float32)
        own = spread[pl.ds(part * 256, 256), pl.ds(0, 1)]
        return own == keys

    def attend(p, carry):
        q2, k2, v2 = qkv[p], qkv[6 + p], qkv[12 + p]
        for part in range(2):
            mask = visible(part)
            qs = q2[part * 256 : part * 256 + 256]
            ks = k2[part * PAIR : part * PAIR + SPAN]
            vs = v2[part * PAIR : part * PAIR + SPAN]
            outs = []
            for h in range(2):
                scores = dot_nt(jnp.where(lows[h], qs, jnp.zeros_like(qs)), ks)
                scores = jnp.where(mask, scores, -1e30)
                raised = jnp.exp(scores - jnp.max(scores, axis=1, keepdims=True)).astype(half)
                probs[p, 2 * part + h] = raised
                outs.append(dot_nn(raised, jnp.where(lows[h], vs, jnp.ones_like(vs))))
            inverse = 1.0 / pltpu.roll(jnp.where(lows[0], outs[1], outs[0]), 64, 1)
            shares[p, pl.ds(part * 256, 256)] = inverse
            context[p, pl.ds(part * 256, 256)] = (jnp.where(lows[0], outs[0], outs[1]) * inverse).astype(half)
        return carry

    lax.fori_loop(0, 6, attend, 0)

    for item in copies[12:16] + gain_copies:
        item.wait()
    joined = jnp.concatenate([context[p] for p in range(6)], axis=1)

    def gain(k):
        return gains[k, pl.ds(0, 1), :].astype(jnp.float32)

    def normalise(z):
        centre = jnp.mean(z, axis=1, keepdims=True)
        z = z - centre
        inverse = lax.rsqrt(jnp.mean(z * z, axis=1, keepdims=True) + EPS)
        return z * inverse, inverse

    acc[...] = dot_nn(joined, wo[...])

    def norm_one(t, carry):
        rows = pl.ds(pl.multiple_of(t * 128, 128), 128)
        hat, inverse = normalise(tokens[rows, :].astype(jnp.float32) + acc[rows, :])
        norm1[rows, :] = hat
        spread[rows, :] = jnp.where(lane == 1, inverse, spread[rows, :])
        value = hat * gain(0) + gain(1)
        hidden[rows, :] = value
        hidden16[rows, :] = value.astype(half)
        return carry

    lax.fori_loop(0, 4, norm_one, 0)
    for item in copies[16:]:
        item.wait()

    flipped_hidden[...] = jnp.transpose(hidden16[...])
    ups[0] = dot_nn(hidden16[...], w1[0])
    for j in range(5):
        if j < 3:
            ups[(j + 1) % 2] = dot_nn(hidden16[...], w1[j + 1])
        if j < 4:
            act[j], slope[j] = gelu_of(ups[j % 2])
        if j > 0:
            hidden[...] += dot_nn(act[j - 1], w2[j - 1])

    vecs[...] = jnp.zeros_like(vecs)

    def fold(value):
        return jnp.sum(value.reshape(-1, 8, D), axis=0)

    def norm_back(hat, inverse, delta, gain_row):
        e = delta * gain_row
        return (
            e - jnp.mean(e, axis=1, keepdims=True) - hat * jnp.mean(e * hat, axis=1, keepdims=True)
        ) * inverse

    def norm_two(t, carry):
        rows = pl.ds(pl.multiple_of(t * 128, 128), 128)
        hat, inverse = normalise(hidden[rows, :])
        block_out[rows, :] = (hat * gain(2) + gain(3)).astype(half)
        delta = dy_ref[rows, :].astype(jnp.float32)
        vecs[2] += fold(delta * hat)
        vecs[3] += fold(delta)
        back = norm_back(hat, inverse, delta, gain(2))
        dz[rows, :] = back
        dz16[rows, :] = back.astype(half)
        return carry

    lax.fori_loop(0, 4, norm_two, 0)

    def out_copy(slot, b, r, q):
        return pltpu.make_async_copy(
            stage.at[slot, pl.ds(r * BLK, BLK), pl.ds(q * BLK, BLK)],
            grads.at[owner[b], pl.ds(0, BLK)],
            v_sem.at[slot, r * 2 + q],
        )

    def flush(slot, blocks):
        for r in range(2):
            for q in range(2):
                out_copy(slot, blocks(r, q), r, q).start()

    def drain(slot):
        for r in range(2):
            for q in range(2):
                out_copy(slot, 0, r, q).wait()

    def backward(j, carry):
        ddown = dz16[...]
        delta = (dot_nt(ddown, w2[j]) * slope[j]).astype(half)

        @pl.when(j >= 2)
        def _():
            drain(2 * (j % 2))
            drain(2 * (j % 2) + 1)

        stage[2 * (j % 2)] = dot_tn(act[j], ddown).astype(half)
        flush(2 * (j % 2), lambda r, q: 32 + (2 * j + r) * 2 + q)
        stage[2 * (j % 2) + 1] = dot_nn(flipped_hidden[...], delta).astype(half)
        flush(2 * (j % 2) + 1, lambda r, q: 16 + r * 8 + 2 * j + q)
        dz[...] += dot_nt(delta, w1[j])
        return carry

    lax.fori_loop(0, 4, backward, 0)

    def norm_one_back(t, carry):
        rows = pl.ds(pl.multiple_of(t * 128, 128), 128)
        hat = norm1[rows, :]
        delta = dz[rows, :]
        vecs[0] += fold(delta * hat)
        vecs[1] += fold(delta)
        back = norm_back(hat, spread[rows, pl.ds(1, 1)], delta, gain(0))
        dz[rows, :] = back
        dz16[rows, :] = back.astype(half)
        return carry

    lax.fori_loop(0, 4, norm_one_back, 0)

    for slot in range(4):
        drain(slot)
    dattn = dz16[...]
    stage[0] = dot_tn(joined, dattn).astype(half)
    flush(0, lambda r, q: 12 + r * 2 + q)
    dcontext = dot_nt(dattn, wo[...]).astype(half)
    for p in range(6):
        held[p] = context[p]
        context[p] = dcontext[:, p * PAIR : (p + 1) * PAIR]

    def attend_back(p, carry):
        q2, k2, v2, d2 = qkv[p], qkv[6 + p], qkv[12 + p], context[p]
        dup[...] = jnp.zeros_like(dup)
        for part in range(2):
            window = pl.ds(part * PAIR, SPAN)
            qs = q2[part * 256 : part * 256 + 256]
            ds = d2[part * 256 : part * 256 + 256]
            ks = k2[part * PAIR : part * PAIR + SPAN]
            vs = v2[part * PAIR : part * PAIR + SPAN]
            dvs, dqs, dks = [], [], []
            share = shares[p, pl.ds(part * 256, 256)]
            scaled = (ds.astype(jnp.float32) * share).astype(half)
            weight = scaled.astype(jnp.float32) * held[p, pl.ds(part * 256, 256)].astype(jnp.float32)
            for h in range(2):
                raised = probs[p, 2 * part + h]
                dprob = dot_nt(jnp.where(lows[h], scaled, jnp.zeros_like(scaled)), vs)
                centre = jnp.sum(jnp.where(lows[h], weight, 0.0), axis=1, keepdims=True)
                dscore = (raised.astype(jnp.float32) * (dprob - centre)).astype(half)
                dvs.append(dot_tn(raised, scaled))
                dqs.append(dot_nn(dscore, ks))
                dks.append(dot_tn(dscore, qs))
            dqkv[p, pl.ds(part * 256, 256)] = (
                jnp.where(lows[0], dqs[0], dqs[1]) * 0.125
            ).astype(half)
            dup[0, window] += jnp.where(lows[0], dks[0], dks[1])
            dup[1, window] += jnp.where(lows[0], dvs[0], dvs[1])
        dqkv[6 + p] = dup[0].astype(half)
        dqkv[12 + p] = dup[1].astype(half)
        return carry

    lax.fori_loop(0, 6, attend_back, 0)

    for part in range(3):
        delta = jnp.concatenate([dqkv[part * 6 + p] for p in range(6)], axis=1)
        stage[1 + part] = dot_nn(flipped[...], delta).astype(half)
        flush(1 + part, lambda r, q: part * 4 + r * 2 + q)
        dz[...] += dot_nt(delta, wqkv[part])

    input_half[...] = dz[...].astype(half)
    for k in range(4):
        row = jnp.sum(vecs[k], axis=0, keepdims=True)
        vecs16 = jnp.broadcast_to(row, (16, D)).astype(half)
        gains[k] = vecs16
    for k in range(4):
        for q in range(2):
            for s in range(2):
                pltpu.make_async_copy(
                    gains.at[k, :, pl.ds(q * BLK, BLK)],
                    grads.at[6 * (2 * k + q) + s, pl.ds(BLK, 16)],
                    w_sem.at[(2 * k + q) * 2 + s],
                ).start()
    for k in range(4):
        for q in range(2):
            for s in range(2):
                pltpu.make_async_copy(
                    gains.at[k, :, pl.ds(q * BLK, BLK)],
                    grads.at[6 * (2 * k + q) + s, pl.ds(BLK, 16)],
                    w_sem.at[(2 * k + q) * 2 + s],
                ).wait()
    for slot in range(4):
        drain(slot)


def run_layer(owner_slot, gathered, token_row, grad_row, segment_ids):
    half, full = jnp.bfloat16, jnp.float32
    anywhere = pl.BlockSpec(memory_space=pltpu.HBM)
    vmem = pl.BlockSpec(memory_space=pltpu.VMEM)
    dma = pltpu.SemaphoreType.DMA
    return pl.pallas_call(
        layer_kernel,
        name="run_layer",
        out_shape=[
            jax.ShapeDtypeStruct((48, PITCH, BLK), half),
            jax.ShapeDtypeStruct((ROW, D), half),
            jax.ShapeDtypeStruct((ROW, D), half),
        ],
        in_specs=[pl.BlockSpec(memory_space=pltpu.SMEM), anywhere, vmem, vmem, vmem],
        out_specs=[anywhere, vmem, vmem],
        scratch_shapes=[
            pltpu.VMEM((3, D, D), half),
            pltpu.VMEM((D, D), half),
            pltpu.VMEM((4, D, D), half),
            pltpu.VMEM((4, D, D), half),
            pltpu.VMEM((4, 16, D), half),
            pltpu.VMEM((18, ROW, PAIR), half),
            pltpu.VMEM((6, 4, 256, SPAN), half),
            pltpu.VMEM((6, ROW, PAIR), full),
            pltpu.VMEM((6, ROW, PAIR), half),
            pltpu.VMEM((6, ROW, PAIR), half),
            pltpu.VMEM((ROW, D), full),
            pltpu.VMEM((ROW, D), half),
            pltpu.VMEM((ROW, D), full),
            pltpu.VMEM((4, ROW, D), half),
            pltpu.VMEM((4, ROW, D), full),
            pltpu.VMEM((ROW, D), full),
            pltpu.VMEM((ROW, D), full),
            pltpu.VMEM((ROW, D), half),
            pltpu.VMEM((18, ROW, PAIR), half),
            pltpu.VMEM((2, ROW, PAIR), full),
            pltpu.VMEM((4, D, D), half),
            pltpu.VMEM((D, ROW), half),
            pltpu.VMEM((D, ROW), half),
            pltpu.VMEM((2, ROW, D), full),
            pltpu.VMEM((4, 8, D), full),
            pltpu.VMEM((ROW, PAIR), full),
            dma((48,)),
            dma((8,)),
            dma((4, 4)),
        ],
        compiler_params=pltpu.CompilerParams(vmem_limit_bytes=62 << 20),
    )(owner_slot, gathered, token_row, grad_row, segment_ids)


BLANK = BLK + 16
HALF = BLK // 2
STREAMS = {
    "A0": (BLANK, 0, True, True),
    "A1": (HALF, 0, True, True),
    "A2": (HALF, HALF, True, False),
    "O": (HALF, 0, False, True),
    "XO": (HALF, 0, False, True),
}
TASKS = (
    ("Y", "A1", 1), ("Y", "A1", 0), ("Z", "A2", 0, 0), ("Y", "A0", 0), ("X", "O", 0, 1), ("X", "O", 0, 0),
    ("Z", "A2", 1, 1), ("X", "O", 1, 1), ("Y", "A0", 2), ("X", "O", 1, 0), ("R", 1), ("Z", "A2", 0, 1),
    ("Z", "A2", 2, 1), ("Z", "A2", 3, 0), ("X", "O", 2, 1), ("R", 0), ("Z", "A2", 1, 0), ("Z", "A2", 2, 0),
    ("Z", "A2", 3, 1), ("Y", "A0", 1), ("X", "O", 3, 1), ("X", "O", 2, 0), ("Y", "O", 0), ("C", "A0", 0),
    ("Y", "O", 1), ("X", "O", 3, 0), ("C", "A1", 0), ("F1", "A2"), ("Y", "A1", 2), ("Y", "A0", 3), ("C", "A0", 1),
    ("C", "A0", 2), ("Y", "A1", 3), ("C", "O", 0), ("Y", "O", 2), ("F", "A2"), ("Y", "O", 3), ("C", "A1", 1),
    ("C", "A0", 3), ("F", "A0"), ("C", "O", 1), ("C", "O", 2), ("C", "A1", 2), ("C", "O", 3), ("C", "A1", 3),
    ("F", "O"), ("L", "A2"), ("L", "A0"), ("F", "A1"), ("L", "O"), ("L", "A1"),
)


def reduce_kernel(grads, rows_a, rows_b, total, land_a, land_b, *scratch):
    z, y, x, c = place()
    dp = z * 2 + y
    sp = x * 2 + c
    names = list(STREAMS)
    moving = [name for name in names if name != "XO"]
    planes = [name for name in moving if STREAMS[name][2]]
    scratch = list(scratch)

    def take(keys):
        return {key: scratch.pop(0) for key in keys}

    mine, core, side, line, last = take(names), take(names), take(moving), take(moving), take(planes)
    cross, = take(["cross"]).values()
    load_sem, core_send, core_recv = take(names), take(names), take(names)
    y_send, y_recv, z_send, z_recv = take(moving), take(moving), take(moving), take(moving)
    x_send, x_recv, last_send, last_recv, give_send, give_recv, keep_sem, row_send, row_recv, row_keep = scratch
    high = z // 2
    order = (3 - 3 * high, 2 - high, 1 - z + 4 * high, z)
    twin = (dp, (1 - x) * 2 + c)
    mate = (dp, x * 2 + 1 - c)
    beside = (z * 2 + 1 - y, sp)
    inner = (z > 0) & (z < NZ - 1)

    def view(ref, name, dest, core_of):
        base = dest * 6
        if name == "A0":
            return ref.at[base + core_of, pl.ds(0, BLANK)]
        if name in ("A1", "A2"):
            return ref.at[base + 2 + core_of, pl.ds(STREAMS[name][1], HALF)]
        slot = base + (4 + x if name == "O" else 5 - x)
        return ref.at[slot, pl.ds(pl.multiple_of(core_of * HALF, HALF), HALF)]

    def remote(src, dst, send, recv, target):
        return pltpu.make_async_remote_copy(
            src_ref=src, dst_ref=dst, send_sem=send, recv_sem=recv,
            device_id=target, device_id_type=MESH,
        )

    def load(name, dest):
        return pltpu.make_async_copy(view(grads, name, dest, c), mine[name].at[dest], load_sem[name].at[dest])

    def to_mate(name, dest):
        return remote(
            view(grads, name, dest, 1 - c), core[name].at[dest],
            core_send[name].at[dest], core_recv[name].at[dest], mate,
        )

    def to_twin(dest):
        return remote(mine["XO"].at[dest], cross.at[dest], x_send.at[dest], x_recv.at[dest], twin)

    def to_side(name, goal):
        at = goal if STREAMS[name][3] else 0
        return remote(
            mine[name].at[goal * 2 + 1 - y], side[name].at[at],
            y_send[name].at[at], y_recv[name].at[at], beside,
        )

    def row_copy(which, source, landing, step, arrival):
        peer = (sp + step) % 4
        at = peer if arrival else sp
        return remote(
            source.at[peer], landing.at[at],
            row_send.at[which, step - 1], row_recv.at[which, at], (dp, peer),
        )

    def column_of(flag):
        return y if flag == 0 else 1 - y

    def dest_of(task):
        if task[0] in ("X", "Z"):
            return order[task[2]] * 2 + column_of(task[3])
        return order[task[2]] * 2 + (1 - y if task[0] == "Y" else y)

    sequence = [
        ("XO" if task[0] == "X" else task[1], dest_of(task)) for task in TASKS if task[0] in ("X", "Y", "C", "Z")
    ]
    for name, dest in sequence:
        load(name, dest).start()
    keeps = [
        pltpu.make_async_copy(rows_a.at[sp], land_a.at[sp], row_keep.at[0]),
        pltpu.make_async_copy(rows_b.at[sp], land_b.at[sp], row_keep.at[1]),
    ]
    for keep in keeps:
        keep.start()
    greet(z, y, x, c)
    for name, dest in sequence:
        to_mate(name, dest).start()

    def merge(name, dest):
        load(name, dest).wait()
        to_mate(name, dest).wait_recv()
        value = mine[name][dest] + core[name][dest]
        if name == "O":
            to_twin(dest).wait_recv()
            value = value + cross[dest]
        mine[name][dest] = value

    def hop(name, goal, column, way, target):
        lane = goal if STREAMS[name][3] else goal * 2 + column
        return remote(
            mine[name].at[goal * 2 + column], line[name].at[way, lane],
            z_send[name].at[lane], z_recv[name].at[way, lane], target,
        )

    def along(name, goal, column):
        dest = goal * 2 + column
        upward = (goal > z).astype(jnp.int32)
        step = 2 * upward - 1
        way = 1 - upward
        item = hop(name, goal, column, way, (dp + 2 * step, sp))
        lane = goal if STREAMS[name][3] else dest

        @pl.when(inner)
        def _():
            item.wait_recv()
            mine[name][dest] = mine[name][dest] + line[name][way, lane]

        item.start()

    def settle(name, column):
        dest = z * 2 + column
        lane = z if STREAMS[name][3] else dest
        for way, valid, step in ((0, z > 0, 1), (1, z < NZ - 1, -1)):
            @pl.when(valid)
            def _():
                hop(name, z, column, way, (dp - 2 * step, sp)).wait_recv()
                mine[name][dest] = mine[name][dest] + line[name][way, lane]

    def swap_last(name):
        at = planes.index(name)
        return remote(mine[name].at[dp], last[name], last_send.at[at], last_recv.at[at], twin)

    def place_of(name, core_of):
        return view(total, name, 0, core_of)

    gift_at = {name: at for at, name in enumerate(planes + ["O", "twin", "XO"])}

    def give(name, key, target, source, core_of):
        at = gift_at[key]
        return remote(source, place_of(name, core_of), give_send.at[at], give_recv.at[at], target)

    gifts, kept = [], []

    def hand_on(name, key, target, source):
        item = give(name, key, target, source, c)
        item.start()
        gifts.append(item)

    def keep_here(name, source):
        item = pltpu.make_async_copy(source, place_of(name, c), keep_sem.at[gift_at[name]])
        item.start()
        kept.append(item)

    for task in TASKS:
        kind, name = task[0], task[1]
        if kind == "R":
            source, landing = ((rows_a, land_a), (rows_b, land_b))[name]
            for step in (2, 3, 1):
                row_copy(name, source, landing, step, False).start()
        elif kind == "X":
            merge("XO", dest_of(task))
            to_twin(dest_of(task)).start()
        elif kind == "Y":
            merge(name, dest_of(task))
            to_side(name, order[task[2]]).start()
        elif kind == "C":
            dest = dest_of(task)
            merge(name, dest)
            to_side(name, order[task[2]]).wait_recv()
            mine[name][dest] = mine[name][dest] + side[name][order[task[2]]]
            if task[2] < 3:
                along(name, order[task[2]], y)
        elif kind == "Z":
            merge(name, dest_of(task))
            if task[2] < 3:
                along(name, order[task[2]], column_of(task[3]))
        elif kind == "F1":
            settle(name, 1 - y)
            to_side(name, z).start()
        elif kind == "F":
            settle(name, y)
            if not STREAMS[name][3]:
                to_side(name, z).wait_recv()
                mine[name][dp] = mine[name][dp] + side[name][0]
            if name in planes:
                swap_last(name).start()
            else:
                hand_on(name, "twin", twin, mine[name].at[dp])
                hand_on(name, "O", mate, mine[name].at[dp])
                keep_here(name, mine[name].at[dp])
        elif kind == "L":
            if name in planes:
                swap_last(name).wait_recv()
                core[name][dp] = mine[name][dp] + last[name][...]
                hand_on(name, name, mate, core[name].at[dp])
                keep_here(name, core[name].at[dp])
            else:
                give("XO", "twin", twin, place_of("XO", c), c).wait_recv()
                hand_on("XO", "XO", mate, place_of("XO", c))

    for name in planes + ["O", "XO"]:
        give(name, name, mate, place_of(name, 1 - c), 1 - c).wait_recv()
    for step in (2, 3, 1):
        for which, source, landing in ((0, rows_a, land_a), (1, rows_b, land_b)):
            row_copy(which, source, landing, step, True).wait_recv()
            row_copy(which, source, landing, step, False).wait_send()
    for name, dest in sequence:
        to_mate(name, dest).wait_send()
    for i in range(4):
        for column in (0, 1):
            to_twin(order[i] * 2 + column).wait_send()
        for name in moving:
            if STREAMS[name][3]:
                to_side(name, order[i]).wait_send()
                if i < 3:
                    hop(name, order[i], y, 0, twin).wait_send()
            elif i < 3:
                for column in (0, 1):
                    hop(name, order[i], column, 0, twin).wait_send()
            else:
                to_side(name, z).wait_send()
    for name in planes:
        swap_last(name).wait_send()
    for item in gifts:
        item.wait_send()
    for item in kept + keeps:
        item.wait()


def reduce_all(grads, rows_a, rows_b):
    anywhere = pl.BlockSpec(memory_space=pl.ANY)
    half = jnp.bfloat16
    dma = pltpu.SemaphoreType.DMA
    moving = [name for name in STREAMS if name != "XO"]
    planes = [name for name in moving if STREAMS[name][2]]

    def buffers(shapes):
        return [pltpu.VMEM((*lead, STREAMS[name][0], BLK), half) for name, lead in shapes]

    first = {name: STREAMS[name][3] for name in moving}
    return pl.pallas_call(
        reduce_kernel,
        name="reduce_all",
        out_shape=[
            jax.ShapeDtypeStruct((6, PITCH, BLK), half),
            pltpu.HBM(rows_a.shape, half),
            pltpu.HBM(rows_b.shape, half),
        ],
        in_specs=[anywhere] * 3,
        out_specs=[anywhere] * 3,
        scratch_shapes=buffers([(name, (8,)) for name in STREAMS] * 2)
        + buffers([(name, (4 if first[name] else 1,)) for name in moving])
        + buffers([(name, (2, 4 if first[name] else 8)) for name in moving])
        + buffers([(name, ()) for name in planes])
        + buffers([("O", (8,))])
        + [dma((8,))] * (3 * len(STREAMS))
        + [dma((4 if first[name] else 1,)) for name in moving] * 2
        + [dma((4 if first[name] else 8,)) for name in moving]
        + [dma((2, 4 if first[name] else 8)) for name in moving]
        + [
            dma((8,)), dma((8,)), dma((len(planes),)), dma((len(planes),)), dma((len(planes) + 3,)),
            dma((len(planes) + 3,)), dma((len(planes) + 1,)), dma((2, 3)), dma((2, 4)), dma((2,)),
        ],
        compiler_params=pltpu.CompilerParams(
            collective_id=1, has_side_effects=True, vmem_limit_bytes=28 << 20
        ),
    )(in_hbm(grads), in_hbm(rows_a), in_hbm(rows_b))


CORRECT = 1.0 - 0.5**STEP
GROUP = 2


def update_kernel(
    total, weights, first, second, left_old, right_old, left_rot, right_rot, vec, vec_first, vec_second, land_a,
    land_b, moment_one, moment_two, left_new, right_new, weights_new, weights_half, vector_one, vector_two, vector_new,
    rows_a, rows_b, held, narrow, wide, stage, stage_half, left, right, out_sem, in_sem, sems,
):
    half = jnp.bfloat16
    take_a = pltpu.make_async_copy(land_a, held, sems.at[0])
    give_a = pltpu.make_async_copy(held, rows_a, sems.at[3])
    take_b = pltpu.make_async_copy(land_b, narrow, sems.at[1])
    give_b = pltpu.make_async_copy(wide, rows_b, sems.at[2])
    count = weights.shape[0]

    def state_of(i):
        return [
            pltpu.make_async_copy(old.at[i], now.at[i], in_sem.at[i, k])
            for k, (old, now) in enumerate(((left_old, left), (right_old, right)))
        ]

    for i in range(count):
        for item in state_of(i):
            item.start()
    take_b.start()
    take_a.start()
    slope = total[0, pl.ds(BLK, 1), :].astype(jnp.float32)
    vec_one = 0.5 * vec_first[...] + 0.5 * slope
    vec_two = 0.5 * vec_second[...] + 0.5 * slope * slope
    vector_one[...] = vec_one
    vector_two[...] = vec_two
    vector_new[...] = vec[...] - rate_vector * (
        (vec_one / CORRECT) / (jnp.sqrt(vec_two / CORRECT) + 1e-08)
    )
    targets = (left_new, right_new, moment_one, moment_two, weights_new)

    def outputs(i):
        copies = [
            pltpu.make_async_copy(stage.at[k, i], target.at[i], out_sem.at[i, k])
            for k, target in enumerate(targets)
        ]
        return copies + [pltpu.make_async_copy(stage_half.at[i], weights_half.at[i], out_sem.at[i, 5])]

    def blocks(pair, carry):
        for i in [pair * GROUP + k for k in range(GROUP)]:
            for item in state_of(i):
                item.wait()
        for i in [pair * GROUP + k for k in range(GROUP)]:
            grad = total[i, :BLK, :]
            rot_l = left_rot[i].astype(half)
            rot_r = right_rot[i].astype(half)
            turned = dot_nn(dot_tn(rot_l, grad).astype(half), rot_r)
            stage[0, i] = 0.95 * left[i] + 0.05 * dot_nt(grad, grad)
            one = 0.5 * first[i] + 0.5 * turned
            two = 0.5 * second[i] + 0.5 * turned * turned
            stage[2, i] = one
            stage[3, i] = two
            ratio = (one / CORRECT) / (jnp.sqrt(two / CORRECT) + 1e-08)
            stage[1, i] = 0.95 * right[i] + 0.05 * dot_tn(grad, grad)
            stepped = dot_nt(dot_nn(rot_l, ratio.astype(half)).astype(half), rot_r)
            fresh = weights[i] - rate_matrix * stepped
            stage[4, i] = fresh
            stage_half[i] = fresh.astype(half)
        for i in [pair * GROUP + k for k in range(GROUP)]:
            for item in outputs(i):
                item.start()

        @pl.when(pair == 0)
        def _():
            take_a.wait()
            give_a.start()
            take_b.wait()
            for r in range(narrow.shape[0]):
                wide[r] = narrow[r].astype(jnp.float32)
            give_b.start()

        return carry

    lax.fori_loop(0, weights.shape[0] // GROUP, blocks, 0)
    for i in range(weights.shape[0]):
        for item in outputs(i):
            item.wait()
    give_a.wait()
    give_b.wait()


def update_all(
    total, weights, first, second, left, right, left_rot, right_rot, vec, vec_first, vec_second, land_a, land_b
):
    full = jnp.float32
    vmem = pl.BlockSpec(memory_space=pltpu.VMEM)
    anywhere = pl.BlockSpec(memory_space=pl.ANY)
    vector = jax.ShapeDtypeStruct((1, BLK), full)
    matrix = pltpu.HBM(weights.shape, full)
    return pl.pallas_call(
        update_kernel,
        name="update_all",
        out_shape=[matrix] * 5 + [pltpu.HBM(weights.shape, jnp.bfloat16)] + [vector] * 3
        + [pltpu.HBM(land_a.shape, jnp.bfloat16), pltpu.HBM(land_b.shape, full)],
        in_specs=[vmem] * 4 + [anywhere] * 2 + [vmem] * 5 + [anywhere] * 2,
        out_specs=[anywhere] * 6 + [vmem] * 3 + [anywhere] * 2,
        scratch_shapes=[
            pltpu.VMEM(land_a.shape, jnp.bfloat16),
            pltpu.VMEM(land_b.shape, jnp.bfloat16),
            pltpu.VMEM(land_b.shape, full),
            pltpu.VMEM((5, *weights.shape), full),
            pltpu.VMEM(weights.shape, jnp.bfloat16),
            pltpu.VMEM(weights.shape, full),
            pltpu.VMEM(weights.shape, full),
            pltpu.SemaphoreType.DMA((weights.shape[0], 6)),
            pltpu.SemaphoreType.DMA((weights.shape[0], 2)),
            pltpu.SemaphoreType.DMA((4,)),
        ],
        compiler_params=pltpu.CompilerParams(vmem_limit_bytes=38 << 20),
    )(
        total, weights, first, second, in_hbm(left), in_hbm(right), left_rot, right_rot,
        vec.reshape(1, BLK), vec_first.reshape(1, BLK), vec_second.reshape(1, BLK), in_hbm(land_a), in_hbm(land_b),
    )


def fast_device(
    tokens, output_grad, segment_ids, lengths, owner_slot, slot_weights, first_moment, second_moment,
    left_stats, right_stats, left_basis, right_basis, vector_values, vector_first, vector_second,
):
    gathered, token_row, grad_row = gather_all(slot_weights, vector_values, tokens, output_grad)
    placed, block_row, input_row = run_layer(
        owner_slot, gathered, token_row.reshape(-1, D), grad_row.reshape(-1, D), segment_ids
    )
    total, block_land, input_land = reduce_all(
        placed, block_row.reshape(tokens.shape), input_row.reshape(tokens.shape)
    )
    updated = update_all(
        total, slot_weights, first_moment, second_moment, left_stats, right_stats, left_basis, right_basis,
        vector_values, vector_first, vector_second, block_land, input_land,
    )
    vectors = [value.reshape(-1) for value in updated[6:9]]
    return (updated[9], updated[10], *updated[:6], *vectors)


def solution(mesh):
    in_specs = (
        P("dp", "sp", None),
        P("dp", "sp", None),
        P("dp", None),
        P("dp", None),
        P(),
        P("dp", None, None),
        P("dp", None, None),
        P("dp", None, None),
        P("dp", None, None),
        P("dp", None, None),
        P("dp", None, None),
        P("dp", None, None),
        P("dp"),
        P("dp"),
        P("dp"),
    )
    out_specs = (
        P("dp", "sp", None),
        P("dp", "sp", None),
        P("dp", None, None),
        P("dp", None, None),
        P("dp", None, None),
        P("dp", None, None),
        P("dp", None, None),
        P("dp", None, None),
        P("dp"),
        P("dp"),
        P("dp"),
    )
    chosen = fast_device if dict(mesh.shape) == {"dp": 8, "sp": 4} else per_device
    return jax.shard_map(
        chosen, mesh=mesh, in_specs=in_specs, out_specs=out_specs, check_vma=False
    )
```

```python
import math

import jax
import jax.numpy as jnp
from jax import lax
from jax.experimental import pallas as pl
from jax.experimental.pallas import tpu as pltpu
from jax.sharding import PartitionSpec as P

D = 768
HD = 64
FF = 3072
BLK = 384
STEP = 4


highest = lax.Precision.HIGHEST
rate_matrix = 0.04
rate_vector = 0.2


def layer_norm(summed, gain, shift):
    centre = jnp.mean(summed, axis=-1, keepdims=True)
    centred = summed - centre
    spread = jnp.mean(centred * centred, axis=-1, keepdims=True)
    return centred * lax.rsqrt(spread + 1e-06) * gain + shift


def exact_gelu(values):
    return jax.nn.gelu(values, approximate=False)


def passage_mask(segment_row, length_row):
    starts = jnp.cumsum(length_row) - length_row
    number = length_row.shape[0]
    onehot = (segment_row[:, None] == jnp.arange(number, dtype=jnp.int32)[None, :]).astype(
        jnp.int32
    )
    opening = jnp.sum(onehot * starts[None, :], axis=1)
    closing = opening + jnp.sum(onehot * length_row[None, :], axis=1)
    places = jnp.arange(segment_row.shape[0], dtype=jnp.int32)
    return (places[None, :] >= opening[:, None]) & (places[None, :] < closing[:, None])


def into_blocks(matrix):
    height, breadth = matrix.shape
    return (
        matrix.reshape(height // BLK, BLK, breadth // BLK, BLK)
        .transpose(0, 2, 1, 3)
        .reshape(-1, BLK, BLK)
    )


def from_blocks(blocks, height, breadth):
    return (
        blocks.reshape(height // BLK, breadth // BLK, BLK, BLK)
        .transpose(0, 2, 1, 3)
        .reshape(height, breadth)
    )


def split_blocks(blocks):
    square = (D // BLK) ** 2
    broad = D * FF // (BLK * BLK)
    w_query = from_blocks(blocks[0:square], D, D)
    w_key = from_blocks(blocks[square : 2 * square], D, D)
    w_value = from_blocks(blocks[2 * square : 3 * square], D, D)
    w_output = from_blocks(blocks[3 * square : 4 * square], D, D)
    w_upward = from_blocks(blocks[4 * square : 4 * square + broad], D, FF)
    w_downward = from_blocks(blocks[4 * square + broad : 4 * square + 2 * broad], FF, D)
    return (w_query, w_key, w_value, w_output, w_upward, w_downward)


def contract_rows(left_mat, right_mat):
    return lax.dot_general(
        left_mat, right_mat, (((0,), (0,)), ((), ())), preferred_element_type=jnp.float32
    )


def contract_cols(left_mat, right_mat):
    return lax.dot_general(
        left_mat, right_mat, (((1,), (1,)), ((), ())), preferred_element_type=jnp.float32
    )


def soap_update(
    gradient, weights, moment_old, second_old, left_old, right_old, left_rot, right_rot
):
    left_next = 0.95 * left_old + 0.05 * jnp.einsum(
        "nij,nkj->nik", gradient, gradient, precision=highest
    )
    right_next = 0.95 * right_old + 0.05 * jnp.einsum(
        "nji,njk->nik", gradient, gradient, precision=highest
    )
    turned = jnp.einsum("nji,njk->nik", left_rot, gradient, precision=highest)
    turned = jnp.einsum("nij,njk->nik", turned, right_rot, precision=highest)
    moment_next = 0.5 * moment_old + 0.5 * turned
    second_next = 0.5 * second_old + 0.5 * turned * turned
    correct = 1.0 - 0.5**STEP
    ratio = moment_next / correct / (jnp.sqrt(second_next / correct) + 1e-08)
    stepped = jnp.einsum("nij,njk->nik", left_rot, ratio, precision=highest)
    stepped = jnp.einsum("nij,nkj->nik", stepped, right_rot, precision=highest)
    return (moment_next, second_next, left_next, right_next, weights - rate_matrix * stepped)


def adam_update(gradient, values, moment_old, second_old):
    moment_next = 0.5 * moment_old + 0.5 * gradient
    second_next = 0.5 * second_old + 0.5 * gradient * gradient
    correct = 1.0 - 0.5**STEP
    ratio = moment_next / correct / (jnp.sqrt(second_next / correct) + 1e-08)
    return (moment_next, second_next, values - rate_vector * ratio)


def masked_scores(joint_row, segment_row, length_row):
    positions = joint_row.shape[0]
    query = joint_row[:, 0].reshape(positions, -1, HD)
    keyed = joint_row[:, 1].reshape(positions, -1, HD)
    valued = joint_row[:, 2].reshape(positions, -1, HD)
    scores = jnp.einsum("qhd,khd->hqk", query, keyed, preferred_element_type=jnp.float32) * 0.125
    visible = passage_mask(segment_row, length_row)
    return (jnp.where(visible[None], scores, -1e30), query, keyed, valued)


def attend_rows(item):
    joint_row, segment_row, length_row = item
    scores, query, keyed, valued = masked_scores(joint_row, segment_row, length_row)
    largest = jnp.max(scores, axis=-1, keepdims=True)
    raised = jnp.exp(scores - largest)
    totals = jnp.sum(raised, axis=-1, keepdims=True)
    probs = raised / totals
    logsum = (largest + jnp.log(totals))[..., 0]
    context = jnp.einsum(
        "hqk,khd->qhd", probs.astype(jnp.bfloat16), valued, preferred_element_type=jnp.float32
    )
    return (context.reshape(joint_row.shape[0], -1).astype(jnp.bfloat16), logsum)


def back_rows(item):
    joint_row, logsum, delta_context, segment_row, length_row = item
    positions = joint_row.shape[0]
    scores, query, keyed, valued = masked_scores(joint_row, segment_row, length_row)
    probs = jnp.exp(scores - logsum[..., None])
    delta_ctx = delta_context.reshape(positions, -1, HD)
    delta_value = jnp.einsum(
        "hqk,qhd->khd", probs.astype(jnp.bfloat16), delta_ctx, preferred_element_type=jnp.float32
    )
    delta_prob = jnp.einsum("qhd,khd->hqk", delta_ctx, valued, preferred_element_type=jnp.float32)
    weighted = jnp.sum(probs * delta_prob, axis=-1, keepdims=True)
    delta_score = (probs * (delta_prob - weighted)).astype(jnp.bfloat16)
    delta_query = (
        jnp.einsum("hqk,khd->qhd", delta_score, keyed, preferred_element_type=jnp.float32) * 0.125
    )
    delta_key = (
        jnp.einsum("hqk,qhd->khd", delta_score, query, preferred_element_type=jnp.float32) * 0.125
    )
    stacked = jnp.stack(
        [
            delta_query.reshape(positions, -1),
            delta_key.reshape(positions, -1),
            delta_value.reshape(positions, -1),
        ],
        axis=1,
    )
    return stacked.astype(jnp.bfloat16)


def pick_blocks(source, slot_index, owner_slot, fanout, part_index):
    matches = owner_slot[None, :] == slot_index[:, None]
    present = jnp.any(matches, axis=1).astype(jnp.float32)
    chosen = jnp.sum(
        matches.astype(jnp.int32) * jnp.arange(owner_slot.shape[0], dtype=jnp.int32)[None, :],
        axis=1,
    )
    picked = jnp.take(source, chosen * fanout + part_index, axis=0)
    return picked * present[:, None, None]


def per_device(
    tokens,
    output_grad,
    segment_ids,
    lengths,
    owner_slot,
    slot_weights,
    first_moment,
    second_moment,
    left_stats,
    right_stats,
    left_basis,
    right_basis,
    vector_values,
    vector_first,
    vector_second,
):
    holding = slot_weights.shape[0]
    row_count = tokens.shape[0]
    token_count = tokens.shape[1]
    gathered, vector_half = (
        lax.all_gather(slot_weights.astype(jnp.bfloat16), "dp", axis=0, tiled=True),
        lax.all_gather(vector_values.astype(jnp.bfloat16), "dp", axis=0, tiled=True),
    )
    blocks = jnp.take(gathered, owner_slot, axis=0)
    w_query, w_key, w_value, w_output, w_upward, w_downward = split_blocks(blocks)
    w_joint = jnp.concatenate([w_query, w_key, w_value], axis=1)
    gains = vector_half.astype(jnp.float32).reshape(4, D)
    flat_tokens = tokens.reshape(-1, D)
    projected = jnp.dot(flat_tokens, w_joint, preferred_element_type=jnp.float32).astype(
        jnp.bfloat16
    )
    projected = projected.reshape(row_count, token_count, 3, D)
    heads = lax.all_to_all(projected, "sp", split_axis=3, concat_axis=1, tiled=True)
    context, logsum = lax.map(attend_rows, (heads, segment_ids, lengths))
    context_tok = lax.all_to_all(context, "sp", split_axis=1, concat_axis=2, tiled=True).reshape(
        -1, D
    )
    attended = jnp.dot(context_tok, w_output, preferred_element_type=jnp.float32)
    summed_one = flat_tokens.astype(jnp.float32) + attended
    hidden, norm_one_pull = jax.vjp(layer_norm, summed_one, gains[0], gains[1])
    hidden_half = hidden.astype(jnp.bfloat16)
    upward = jnp.dot(hidden_half, w_upward, preferred_element_type=jnp.float32)
    activated, gelu_pull = jax.vjp(exact_gelu, upward)
    active_half = activated.astype(jnp.bfloat16)
    downward = jnp.dot(active_half, w_downward, preferred_element_type=jnp.float32)
    result, norm_two_pull = jax.vjp(layer_norm, hidden + downward, gains[2], gains[3])
    block_out = result.astype(jnp.bfloat16).reshape(row_count, token_count, D)
    cotangent = output_grad.reshape(-1, D).astype(jnp.float32)
    delta_two, delta_gain_two, delta_shift_two = norm_two_pull(cotangent)
    delta_down = delta_two.astype(jnp.bfloat16)
    grad_down = contract_rows(active_half, delta_down)
    delta_active = contract_cols(delta_down, w_downward)
    (delta_upward,) = gelu_pull(delta_active)
    delta_up = delta_upward.astype(jnp.bfloat16)
    grad_up = contract_rows(hidden_half, delta_up)
    delta_hidden = delta_two + contract_cols(delta_up, w_upward)
    delta_one, delta_gain_one, delta_shift_one = norm_one_pull(delta_hidden)
    delta_attn = delta_one.astype(jnp.bfloat16)
    grad_output = contract_rows(context_tok, delta_attn)
    delta_context = (
        contract_cols(delta_attn, w_output).astype(jnp.bfloat16).reshape(row_count, token_count, D)
    )
    delta_heads = lax.all_to_all(delta_context, "sp", split_axis=2, concat_axis=1, tiled=True)
    delta_projected = lax.map(back_rows, (heads, logsum, delta_heads, segment_ids, lengths))
    delta_joint = lax.all_to_all(
        delta_projected, "sp", split_axis=1, concat_axis=3, tiled=True
    ).reshape(-1, 3 * D)
    grad_joint = contract_rows(flat_tokens, delta_joint)
    input_grad = (delta_one + contract_cols(delta_joint, w_joint)).reshape(
        row_count, token_count, D
    )
    grad_blocks = jnp.concatenate(
        [
            into_blocks(grad_joint[:, :D]),
            into_blocks(grad_joint[:, D : 2 * D]),
            into_blocks(grad_joint[:, 2 * D :]),
            into_blocks(grad_output),
            into_blocks(grad_up),
            into_blocks(grad_down),
        ],
        axis=0,
    )
    vector_grad = jnp.concatenate(
        [delta_gain_one, delta_shift_one, delta_gain_two, delta_shift_two]
    )
    vector_total = lax.psum(vector_grad, ("dp", "sp"))
    piece_len = vector_values.shape[0]
    vector_piece = lax.dynamic_slice_in_dim(
        vector_total, lax.axis_index("dp") * piece_len, piece_len
    )
    slot_index = jnp.arange(holding * lax.axis_size("dp"), dtype=jnp.int32)
    owned = lax.psum_scatter(
        pick_blocks(grad_blocks, slot_index, owner_slot, 1, 0),
        "dp",
        scatter_dimension=0,
        tiled=True,
    )
    owned = lax.psum(owned.astype(jnp.bfloat16), "sp").astype(jnp.float32)
    moment_one, moment_two, left_new, right_new, weights_new = soap_update(
        owned,
        slot_weights,
        first_moment,
        second_moment,
        left_stats,
        right_stats,
        left_basis,
        right_basis,
    )
    vector_one, vector_two, vector_new = adam_update(
        vector_piece, vector_values, vector_first, vector_second
    )
    return (
        block_out,
        input_grad,
        moment_one,
        moment_two,
        left_new,
        right_new,
        weights_new,
        weights_new.astype(jnp.bfloat16),
        vector_one,
        vector_two,
        vector_new,
    )


PITCH = BLK + 16
MESH = pl.DeviceIdType.MESH
NZ = 4


def in_hbm(value):
    return pltpu.with_memory_space_constraint(value, pltpu.HBM)


def place():
    dp = lax.axis_index("dp")
    sp = lax.axis_index("sp")
    return dp // 2, dp % 2, sp // 2, sp % 2


def greet(z, y, x, c):
    barrier = pltpu.get_barrier_semaphore()
    dp = z * 2 + y
    sp = x * 2 + c

    def signal(target):
        pl.semaphore_signal(barrier, 1, device_id=target, device_id_type=MESH)

    for step in range(1, 4):
        signal((dp, (sp + step) % 4))
    signal((z * 2 + 1 - y, sp))

    @pl.when(z < NZ - 1)
    def _():
        signal((dp + 2, sp))

    @pl.when(z > 0)
    def _():
        signal((dp - 2, sp))

    pl.semaphore_wait(barrier, 4 + (z < NZ - 1).astype(jnp.int32) + (z > 0).astype(jnp.int32))


PIECES = {
    "A0": (BLK + 16, False, True),
    "A1": (BLK // 2, False, False),
    "O0": (BLK // 2, True, True),
    "O1": (BLK // 4, True, True),
}
STEPS = (
    ("own", "O1"), ("rows", 1), ("own", "O0"), ("own", "A1"), ("z", "O1", 1, 1, 0), ("z", "O1", 1, -1, 0),
    ("y", "O1", 0, 0), ("z", "O0", 1, 1, 0), ("own", "A0"), ("z", "O0", 2, 1, 0), ("y", "O0", 0, 0),
    ("z", "O0", 1, -1, 0), ("z", "O1", 2, -1, 0), ("y", "O1", 1, -1), ("z", "O1", 3, -1, 0), ("z", "A1", 1, 1, 0),
    ("z", "O1", 2, 1, 0), ("y", "O1", 1, 1), ("z", "O0", 3, 1, 0), ("z", "A0", 1, -1, 0), ("y", "O1", 2, -1),
    ("y", "O0", 1, 1), ("z", "O1", 3, 1, 0), ("y", "O0", 2, 1), ("x", "O0", 3, 1, 0), ("x", "O1", 3, -1, 0),
    ("x", "O1", 1, 1, 0), ("z", "A1", 1, -1, 0), ("x", "O0", 1, -1, 0), ("z", "A0", 1, 1, 0),
    ("x", "O1", 1, -1, 1), ("y", "O1", 3, -1), ("y", "A1", 0, 0), ("z", "A0", 2, 1, 0), ("x", "O0", 2, 1, 0),
    ("y", "O1", 2, 1), ("rows", 0), ("z", "O0", 2, -1, 0), ("x", "O0", 2, 1, 1), ("z", "A0", 2, -1, 0),
    ("x", "O1", 0, 0, 1), ("z", "A1", 1, 1, 1), ("x", "O0", 1, 1, 1), ("z", "O0", 3, -1, 0), ("z", "A1", 1, -1, 1),
    ("y", "O0", 2, -1), ("y", "O0", 3, 1), ("y", "A0", 1, -1), ("x", "O1", 2, 1, 1), ("x", "O1", 3, 1, 0),
    ("x", "O0", 0, 0, 1), ("y", "O0", 3, -1), ("z", "A0", 3, 1, 0), ("y", "O1", 3, 1), ("z", "A0", 3, -1, 0),
    ("x", "O0", 1, 1, 0), ("x", "O1", 3, -1, 1), ("y", "O0", 1, -1), ("z", "A1", 2, -1, 0), ("y", "A0", 0, 0),
    ("x", "O1", 2, -1, 1), ("y", "A0", 2, -1), ("z", "A1", 2, -1, 1), ("x", "O0", 2, -1, 0), ("z", "A1", 3, -1, 0),
    ("x", "O0", 3, -1, 0), ("x", "O0", 3, -1, 1), ("z", "A1", 2, 1, 1), ("y", "A0", 2, 1), ("z", "A1", 2, 1, 0),
    ("x", "O0", 3, 1, 1), ("x", "O1", 2, -1, 0), ("z", "A1", 3, 1, 1), ("x", "O1", 2, 1, 0), ("x", "O0", 2, -1, 1),
    ("y", "A0", 3, -1), ("y", "A0", 1, 1), ("y", "A0", 3, 1), ("x", "O1", 3, 1, 1), ("x", "O1", 1, -1, 0),
    ("x", "O1", 1, 1, 1), ("x", "O0", 1, -1, 1), ("z", "A1", 3, -1, 1), ("z", "A1", 3, 1, 0),
)


def piece_view(ref, name, x_of, c_of, base):
    height = PIECES[name][0]
    if name == "A0":
        return ref.at[base + c_of, pl.ds(0, height)]
    if name == "A1":
        slot, row = base + 2, height * c_of
    elif name == "O0":
        slot, row = base + 4 + x_of, height * c_of
    else:
        slot, row = base + 3, 2 * height * x_of + height * c_of
    return ref.at[slot, pl.ds(pl.multiple_of(row, height), height)]


def gather_kernel(weights, vector, tokens, grads, out, token_row, grad_row, wide, narrow, *sems):
    z, y, x, c = place()
    dp = z * 2 + y
    sp = x * 2 + c
    sems = list(sems)
    load_sem, keep_sem, row_send, row_recv, row_keep = [sems.pop(0) for _ in range(5)]
    ways = ("up", "down", "y", "mate", "x", "pass")
    send_sem = {(way, name): sems.pop(0) for way in ways for name in PIECES if PIECES[name][1] or way not in ways[4:]}
    recv_sem = {(way, name): sems.pop(0) for way in ways[2:] for name in PIECES if PIECES[name][1] or way not in ways[4:]}
    targets = {
        "up": (dp + 2, sp), "down": (dp - 2, sp), "y": (z * 2 + 1 - y, sp),
        "x": (dp, (1 - x) * 2 + c), "mate": (dp, x * 2 + 1 - c), "pass": (dp, x * 2 + 1 - c),
    }
    def load_of(i):
        return pltpu.make_async_copy(weights.at[i], wide.at[i], load_sem.at[i])

    for i in (c, 2, 3, 4 + x, 1 - c, 5 - x):
        load_of(i).start()
    keeps = [
        pltpu.make_async_copy(tokens.at[sp], token_row.at[sp], row_keep.at[0]),
        pltpu.make_async_copy(grads.at[sp], grad_row.at[sp], row_keep.at[1]),
    ]
    for keep in keeps:
        keep.start()
    gains = jnp.broadcast_to(vector[...], (16, BLK)).astype(jnp.bfloat16)
    greet(z, y, x, c)

    def row_copy(which, source, landing, step, arrival):
        peer = (sp + step) % 4
        at = peer if arrival else sp
        return pltpu.make_async_remote_copy(
            src_ref=source.at[peer], dst_ref=landing.at[at],
            send_sem=row_send.at[which, step - 1], recv_sem=row_recv.at[which, at],
            device_id=(dp, peer), device_id_type=MESH,
        )

    def round_block(i):
        load_of(i).wait()
        narrow[i, :BLK, :] = wide[i].astype(jnp.bfloat16)
        narrow[i, BLK:, :] = gains

    for i in (c, 2, 3, 4 + x):
        round_block(i)
    own = [pltpu.make_async_copy(narrow.at[i], out.at[dp * 6 + i], keep_sem.at[i]) for i in range(6)]
    started = []

    def item_of(way, name, holder, x_of, c_of, fresh=False):
        landing = piece_view(out, name, x_of, c_of, holder * 6)
        arrives = way if way in ("mate", "x", "pass") else "y"
        return pltpu.make_async_remote_copy(
            src_ref=piece_view(narrow, name, x_of, c_of, 0) if fresh else landing, dst_ref=landing,
            send_sem=send_sem[way, name].at[holder], recv_sem=recv_sem[arrives, name].at[holder],
            device_id=targets[way], device_id_type=MESH,
        )

    def send(way, name, holder, valid, x_of=x, fresh=False):
        if way in ("up", "down"):
            room = z < NZ - 1 if way == "up" else z > 0
            valid = room if valid is None else valid & room
        item = item_of(way, name, holder, x_of, c, fresh)
        if valid is None:
            item.start()
        else:
            pl.when(valid)(item.start)
        started.append((item, valid))

    def arrive(way, name, holder, valid, x_of, c_of):
        item = item_of(way, name, holder, x_of, c_of)
        if valid is None:
            item.wait_recv()
        else:
            pl.when(valid)(item.wait_recv)

    def origin_of(sign, far):
        origin = z + sign * far
        if far == 0:
            return origin, None
        return origin, ((origin >= 0) if sign < 0 else (origin <= NZ - 1))

    for step in STEPS:
        kind, name = step[0], step[1]
        if kind == "own":
            for way in ("up", "down", "y"):
                send(way, name, dp, None, fresh=True)
        elif kind == "rows":
            source, landing = ((tokens, token_row), (grads, grad_row))[name]
            for hop in (2, 3, 1):
                row_copy(name, source, landing, hop, False).start()
        else:
            origin, inside = origin_of(step[3], step[2])
            if kind == "x":
                holder = origin * 2 + (y if step[4] == 0 else 1 - y)
                arrive("x", name, holder, inside, 1 - x, c)
                send("pass", name, holder, inside, 1 - x)
                continue
            holder = origin * 2 + (y if kind == "z" and step[4] == 0 else 1 - y)
            arrive("y", name, holder, inside, x, c)
            if kind == "z":
                if step[2] < NZ - 1:
                    send("up" if step[3] < 0 else "down", name, holder, inside)
                if PIECES[name][2] and step[4] == 0:
                    send("y", name, holder, inside)
            elif not PIECES[name][2]:
                send("up", name, holder, inside)
                send("down", name, holder, inside)
            if PIECES[name][1]:
                send("x", name, holder, inside)
            send("mate", name, holder, inside)
        if kind == "own" and name == "A0":
            for i in (1 - c, 5 - x):
                round_block(i)
            for item in own:
                item.start()

    for far in range(NZ):
        for sign in (0,) if far == 0 else (-1, 1):
            origin, inside = origin_of(sign, far)
            for column in (1,) if far == 0 else (0, 1):
                holder = origin * 2 + (y if column == 0 else 1 - y)
                for name in PIECES:
                    arrive("mate", name, holder, inside, x, 1 - c)
                    if PIECES[name][1]:
                        arrive("pass", name, holder, inside, 1 - x, 1 - c)
    for hop in (2, 3, 1):
        for which, source, landing in ((0, tokens, token_row), (1, grads, grad_row)):
            row_copy(which, source, landing, hop, True).wait_recv()
            row_copy(which, source, landing, hop, False).wait_send()
    for item, valid in started:
        if valid is None:
            item.wait_send()
        else:
            pl.when(valid)(item.wait_send)
    for item in own + keeps:
        item.wait()


def gather_all(weights, vector, tokens, grads):
    anywhere = pl.BlockSpec(memory_space=pl.ANY)
    dma = pltpu.SemaphoreType.DMA
    carried = sum(1 for name in PIECES if PIECES[name][1])
    flows = (4 * len(PIECES) + 2 * carried) + (2 * len(PIECES) + 2 * carried)
    return pl.pallas_call(
        gather_kernel,
        name="gather_all",
        out_shape=[
            pltpu.HBM((48, PITCH, BLK), jnp.bfloat16),
            pltpu.HBM(tokens.shape, jnp.bfloat16),
            pltpu.HBM(grads.shape, jnp.bfloat16),
        ],
        in_specs=[anywhere, pl.BlockSpec(memory_space=pltpu.VMEM), anywhere, anywhere],
        out_specs=[anywhere, anywhere, anywhere],
        scratch_shapes=[
            pltpu.VMEM((6, BLK, BLK), jnp.float32),
            pltpu.VMEM((6, PITCH, BLK), jnp.bfloat16),
            dma((6,)), dma((6,)), dma((2, 3)), dma((2, 4)), dma((2,)),
        ]
        + [dma((8,))] * flows,
        compiler_params=pltpu.CompilerParams(
            collective_id=0, has_side_effects=True, vmem_limit_bytes=24 << 20
        ),
    )(in_hbm(weights), vector.reshape(1, BLK), in_hbm(tokens), in_hbm(grads))


ROW = 512
PAIR = 128
SPAN = 384
EPS = 1e-06


def gelu_of(u):
    bell = jnp.exp(-0.5 * u * u)
    t = 1.0 / (1.0 + (0.3275911 / math.sqrt(2.0)) * jnp.abs(u))
    tail = 0.5 * 1.061405429
    for term in (-1.453152027, 1.421413741, -0.284496736, 0.254829592):
        tail = tail * t + 0.5 * term
    tail = tail * t * bell
    below = jnp.where(u >= 0.0, 1.0 - tail, tail)
    return (u * below).astype(jnp.bfloat16), below + u * (bell * (1.0 / math.sqrt(2.0 * math.pi)))


def dot_nn(a, b):
    return lax.dot_general(a, b, (((1,), (0,)), ((), ())), preferred_element_type=jnp.float32)


def dot_nt(a, b):
    return lax.dot_general(a, b, (((1,), (1,)), ((), ())), preferred_element_type=jnp.float32)


def dot_tn(a, b):
    return lax.dot_general(a, b, (((0,), (0,)), ((), ())), preferred_element_type=jnp.float32)


def layer_kernel(
    owner, weights, tokens, dy_ref, segments, grads, block_out, input_half,
    wqkv, wo, w1, w2, gains, qkv, probs, shares, held, context, hidden, hidden16, norm1, act, slope, dz, dz16,
    dqkv, dup, stage, flipped, flipped_hidden, ups, vecs, spread, w_sem, g_sem, v_sem,
):
    half = jnp.bfloat16
    sp = lax.axis_index("sp")

    def weight_copies():
        copies = []
        for which, ref in enumerate((wqkv.at[0], wqkv.at[1], wqkv.at[2], wo)):
            for r in range(2):
                for q in range(2):
                    copies.append((which * 4 + r * 2 + q, ref, r, q))
        for r in range(2):
            for q in range(8):
                copies.append((16 + r * 8 + q, w1.at[q // 2], r, q % 2))
        for r in range(8):
            for q in range(2):
                copies.append((32 + r * 2 + q, w2.at[r // 2], r % 2, q))
        return [
            pltpu.make_async_copy(
                weights.at[owner[b], pl.ds(0, BLK)],
                ref.at[pl.ds(r * BLK, BLK), pl.ds(q * BLK, BLK)],
                w_sem.at[b],
            )
            for b, ref, r, q in copies
        ]

    copies = weight_copies()
    gain_copies = [
        pltpu.make_async_copy(
            weights.at[6 * d, pl.ds(BLK, 16)], gains.at[d // 2, :, pl.ds((d % 2) * BLK, BLK)], g_sem.at[d]
        )
        for d in range(8)
    ]
    for item in copies[:16] + gain_copies + copies[16:]:
        item.start()

    seg_row = segments[pl.ds(sp, 1), :].astype(jnp.float32)
    spread[...] = jnp.transpose(jnp.broadcast_to(seg_row, (PAIR, ROW)))

    for item in copies[:12]:
        item.wait()
    x = tokens[...]
    flipped[...] = jnp.transpose(x)
    for part in range(3):
        block = dot_nn(x, wqkv[part])
        if part == 0:
            block = block * 0.125
        block = block.astype(half)
        for p in range(6):
            qkv[part * 6 + p] = block[:, p * PAIR : (p + 1) * PAIR]

    lane = lax.broadcasted_iota(jnp.int32, (1, PAIR), 1)
    lows = (lane < 64, lane >= 64)

    def visible(part):
        keys = segments[pl.ds(sp, 1), pl.ds(part * PAIR, SPAN)].astype(jnp.float32)
        own = spread[pl.ds(part * 256, 256), pl.ds(0, 1)]
        return own == keys

    def attend(p, carry):
        q2, k2, v2 = qkv[p], qkv[6 + p], qkv[12 + p]
        for part in range(2):
            mask = visible(part)
            qs = q2[part * 256 : part * 256 + 256]
            ks = k2[part * PAIR : part * PAIR + SPAN]
            vs = v2[part * PAIR : part * PAIR + SPAN]
            outs = []
            for h in range(2):
                scores = dot_nt(jnp.where(lows[h], qs, jnp.zeros_like(qs)), ks)
                scores = jnp.where(mask, scores, -1e30)
                raised = jnp.exp(scores - jnp.max(scores, axis=1, keepdims=True)).astype(half)
                probs[p, 2 * part + h] = raised
                outs.append(dot_nn(raised, jnp.where(lows[h], vs, jnp.ones_like(vs))))
            inverse = 1.0 / pltpu.roll(jnp.where(lows[0], outs[1], outs[0]), 64, 1)
            shares[p, pl.ds(part * 256, 256)] = inverse
            context[p, pl.ds(part * 256, 256)] = (jnp.where(lows[0], outs[0], outs[1]) * inverse).astype(half)
        return carry

    lax.fori_loop(0, 6, attend, 0, unroll=6)

    for item in copies[12:16] + gain_copies:
        item.wait()
    joined = jnp.concatenate([context[p] for p in range(6)], axis=1)

    def gain(k):
        return gains[k, pl.ds(0, 1), :].astype(jnp.float32)

    def normalise(z):
        centre = jnp.mean(z, axis=1, keepdims=True)
        z = z - centre
        inverse = lax.rsqrt(jnp.mean(z * z, axis=1, keepdims=True) + EPS)
        return z * inverse, inverse

    dz[...] = dot_nn(joined, wo[...])

    def norm_one(t, carry):
        rows = pl.ds(pl.multiple_of(t * 128, 128), 128)
        hat, inverse = normalise(tokens[rows, :].astype(jnp.float32) + dz[rows, :])
        norm1[rows, :] = hat
        spread[rows, :] = jnp.where(lane == 1, inverse, spread[rows, :])
        value = hat * gain(0) + gain(1)
        hidden[rows, :] = value
        hidden16[rows, :] = value.astype(half)
        return carry

    lax.fori_loop(0, 4, norm_one, 0)
    for item in copies[16:]:
        item.wait()

    flipped_hidden[...] = jnp.transpose(hidden16[...])
    ups[0] = dot_nn(hidden16[...], w1[0])
    for j in range(5):
        if j < 3:
            ups[(j + 1) % 2] = dot_nn(hidden16[...], w1[j + 1])
        if j < 4:
            act[j], slope[j] = gelu_of(ups[j % 2])
        if j > 0:
            hidden[...] += dot_nn(act[j - 1], w2[j - 1])

    vecs[...] = jnp.zeros_like(vecs)

    def fold(value):
        return jnp.sum(value.reshape(-1, 8, D), axis=0)

    def norm_back(hat, inverse, delta, gain_row):
        e = delta * gain_row
        return (
            e - jnp.mean(e, axis=1, keepdims=True) - hat * jnp.mean(e * hat, axis=1, keepdims=True)
        ) * inverse

    def norm_two(t, carry):
        rows = pl.ds(pl.multiple_of(t * 128, 128), 128)
        hat, inverse = normalise(hidden[rows, :])
        block_out[rows, :] = (hat * gain(2) + gain(3)).astype(half)
        delta = dy_ref[rows, :].astype(jnp.float32)
        vecs[2] += fold(delta * hat)
        vecs[3] += fold(delta)
        back = norm_back(hat, inverse, delta, gain(2))
        dz[rows, :] = back
        dz16[rows, :] = back.astype(half)
        return carry

    lax.fori_loop(0, 4, norm_two, 0)

    def out_copy(slot, b, r, q):
        return pltpu.make_async_copy(
            stage.at[slot, pl.ds(r * BLK, BLK), pl.ds(q * BLK, BLK)],
            grads.at[owner[b], pl.ds(0, BLK)],
            v_sem.at[slot, r * 2 + q],
        )

    def flush(slot, blocks):
        for r in range(2):
            for q in range(2):
                out_copy(slot, blocks(r, q), r, q).start()

    def drain(slot):
        for r in range(2):
            for q in range(2):
                out_copy(slot, 0, r, q).wait()

    def backward(pair, carry):
        @pl.when(pair > 0)
        def _():
            for slot in range(4):
                drain(slot)

        ddown = dz16[...]
        for k in range(2):
            j = 2 * pair + k
            delta = (dot_nt(ddown, w2[j]) * slope[j]).astype(half)
            stage[2 * k] = dot_tn(act[j], ddown).astype(half)
            stage[2 * k + 1] = dot_nn(flipped_hidden[...], delta).astype(half)
            dz[...] += dot_nt(delta, w1[j])
        for k in range(2):
            j = 2 * pair + k
            flush(2 * k, lambda r, q: 32 + (2 * j + r) * 2 + q)
            flush(2 * k + 1, lambda r, q: 16 + r * 8 + 2 * j + q)
        return carry

    lax.fori_loop(0, 2, backward, 0)

    def norm_one_back(t, carry):
        rows = pl.ds(pl.multiple_of(t * 128, 128), 128)
        hat = norm1[rows, :]
        delta = dz[rows, :]
        vecs[0] += fold(delta * hat)
        vecs[1] += fold(delta)
        back = norm_back(hat, spread[rows, pl.ds(1, 1)], delta, gain(0))
        dz[rows, :] = back
        dz16[rows, :] = back.astype(half)
        return carry

    lax.fori_loop(0, 4, norm_one_back, 0)

    for slot in range(4):
        drain(slot)
    dattn = dz16[...]
    stage[0] = dot_tn(joined, dattn).astype(half)
    flush(0, lambda r, q: 12 + r * 2 + q)
    dcontext = dot_nt(dattn, wo[...]).astype(half)
    for p in range(6):
        held[p] = context[p]
        context[p] = dcontext[:, p * PAIR : (p + 1) * PAIR]

    def attend_back(p, carry):
        q2, k2, v2, d2 = qkv[p], qkv[6 + p], qkv[12 + p], context[p]
        dup[...] = jnp.zeros_like(dup)
        for part in range(2):
            window = pl.ds(part * PAIR, SPAN)
            qs = q2[part * 256 : part * 256 + 256]
            ds = d2[part * 256 : part * 256 + 256]
            ks = k2[part * PAIR : part * PAIR + SPAN]
            vs = v2[part * PAIR : part * PAIR + SPAN]
            dvs, dqs, dks = [], [], []
            share = shares[p, pl.ds(part * 256, 256)]
            scaled = (ds.astype(jnp.float32) * share).astype(half)
            weight = scaled.astype(jnp.float32) * held[p, pl.ds(part * 256, 256)].astype(jnp.float32)
            for h in range(2):
                raised = probs[p, 2 * part + h]
                dprob = dot_nt(jnp.where(lows[h], scaled, jnp.zeros_like(scaled)), vs)
                centre = jnp.sum(jnp.where(lows[h], weight, 0.0), axis=1, keepdims=True)
                dscore = (raised.astype(jnp.float32) * (dprob - centre)).astype(half)
                dvs.append(dot_tn(raised, scaled))
                dqs.append(dot_nn(dscore, ks))
                dks.append(dot_tn(dscore, qs))
            dqkv[p, pl.ds(part * 256, 256)] = (
                jnp.where(lows[0], dqs[0], dqs[1]) * 0.125
            ).astype(half)
            dup[0, window] += jnp.where(lows[0], dks[0], dks[1])
            dup[1, window] += jnp.where(lows[0], dvs[0], dvs[1])
        dqkv[6 + p] = dup[0].astype(half)
        dqkv[12 + p] = dup[1].astype(half)
        return carry

    lax.fori_loop(0, 6, attend_back, 0, unroll=6)

    for part in range(3):
        delta = jnp.concatenate([dqkv[part * 6 + p] for p in range(6)], axis=1)
        stage[1 + part] = dot_nn(flipped[...], delta).astype(half)
        flush(1 + part, lambda r, q: part * 4 + r * 2 + q)
        dz[...] += dot_nt(delta, wqkv[part])

    input_half[...] = dz[...].astype(half)
    for k in range(4):
        row = jnp.sum(vecs[k], axis=0, keepdims=True)
        vecs16 = jnp.broadcast_to(row, (16, D)).astype(half)
        gains[k] = vecs16
    for k in range(4):
        for q in range(2):
            for s in range(2):
                pltpu.make_async_copy(
                    gains.at[k, :, pl.ds(q * BLK, BLK)],
                    grads.at[6 * (2 * k + q) + s, pl.ds(BLK, 16)],
                    w_sem.at[(2 * k + q) * 2 + s],
                ).start()
    for k in range(4):
        for q in range(2):
            for s in range(2):
                pltpu.make_async_copy(
                    gains.at[k, :, pl.ds(q * BLK, BLK)],
                    grads.at[6 * (2 * k + q) + s, pl.ds(BLK, 16)],
                    w_sem.at[(2 * k + q) * 2 + s],
                ).wait()
    for slot in range(4):
        drain(slot)


def run_layer(owner_slot, gathered, token_row, grad_row, segment_ids):
    half, full = jnp.bfloat16, jnp.float32
    anywhere = pl.BlockSpec(memory_space=pltpu.HBM)
    vmem = pl.BlockSpec(memory_space=pltpu.VMEM)
    dma = pltpu.SemaphoreType.DMA
    return pl.pallas_call(
        layer_kernel,
        name="run_layer",
        out_shape=[
            jax.ShapeDtypeStruct((48, PITCH, BLK), half),
            jax.ShapeDtypeStruct((ROW, D), half),
            jax.ShapeDtypeStruct((ROW, D), half),
        ],
        in_specs=[pl.BlockSpec(memory_space=pltpu.SMEM), anywhere, vmem, vmem, vmem],
        out_specs=[anywhere, vmem, vmem],
        scratch_shapes=[
            pltpu.VMEM((3, D, D), half),
            pltpu.VMEM((D, D), half),
            pltpu.VMEM((4, D, D), half),
            pltpu.VMEM((4, D, D), half),
            pltpu.VMEM((4, 16, D), half),
            pltpu.VMEM((18, ROW, PAIR), half),
            pltpu.VMEM((6, 4, 256, SPAN), half),
            pltpu.VMEM((6, ROW, PAIR), full),
            pltpu.VMEM((6, ROW, PAIR), half),
            pltpu.VMEM((6, ROW, PAIR), half),
            pltpu.VMEM((ROW, D), full),
            pltpu.VMEM((ROW, D), half),
            pltpu.VMEM((ROW, D), full),
            pltpu.VMEM((4, ROW, D), half),
            pltpu.VMEM((4, ROW, D), full),
            pltpu.VMEM((ROW, D), full),
            pltpu.VMEM((ROW, D), half),
            pltpu.VMEM((18, ROW, PAIR), half),
            pltpu.VMEM((2, ROW, PAIR), full),
            pltpu.VMEM((4, D, D), half),
            pltpu.VMEM((D, ROW), half),
            pltpu.VMEM((D, ROW), half),
            pltpu.VMEM((2, ROW, D), full),
            pltpu.VMEM((4, 8, D), full),
            pltpu.VMEM((ROW, PAIR), full),
            dma((48,)),
            dma((8,)),
            dma((4, 4)),
        ],
        compiler_params=pltpu.CompilerParams(vmem_limit_bytes=58 << 20),
    )(owner_slot, gathered, token_row, grad_row, segment_ids)


BLANK = BLK + 16
HALF = BLK // 2
STREAMS = {
    "A0": (BLANK, 0, True, True),
    "A1": (HALF, 0, True, True),
    "A2": (HALF, HALF, True, False),
    "O": (HALF, 0, False, True),
    "XO": (HALF, 0, False, True),
}
TASKS = (
    ("Y", "A1", 3), ("Z", "A2", 0, 1), ("Y", "A0", 0), ("X", "O", 0, 1), ("Z", "A2", 0, 0), ("X", "O", 2, 1),
    ("X", "O", 1, 0), ("Y", "A0", 1), ("Z", "A2", 1, 1), ("Y", "A0", 2), ("Z", "A2", 2, 0), ("X", "O", 0, 0),
    ("X", "O", 3, 0), ("Y", "O", 0), ("C", "A0", 0), ("Z", "A2", 2, 1), ("X", "O", 1, 1), ("Y", "O", 2),
    ("Y", "A0", 3), ("X", "O", 3, 1), ("X", "O", 2, 0), ("C", "A0", 1), ("R", 1), ("Y", "O", 1), ("Y", "A1", 0),
    ("C", "A1", 3), ("Z", "A2", 3, 1), ("Y", "O", 3), ("C", "O", 0), ("R", 0), ("C", "A0", 2), ("Y", "A1", 1),
    ("C", "A0", 3), ("C", "O", 2), ("Y", "A1", 2), ("C", "O", 1), ("F", "A0"), ("F1", "A2"), ("C", "A1", 0),
    ("C", "O", 3), ("Z", "A2", 3, 0), ("F", "O"), ("Z", "A2", 1, 0), ("C", "A1", 1), ("C", "A1", 2), ("F", "A2"),
    ("L", "O"), ("F", "A1"), ("L", "A0"), ("L", "A2"), ("L", "A1"),
)


def reduce_kernel(grads, rows_a, rows_b, total, land_a, land_b, *scratch):
    z, y, x, c = place()
    dp = z * 2 + y
    sp = x * 2 + c
    names = list(STREAMS)
    moving = [name for name in names if name != "XO"]
    planes = [name for name in moving if STREAMS[name][2]]
    scratch = list(scratch)

    def take(keys):
        return {key: scratch.pop(0) for key in keys}

    mine, core, side, line, last = take(names), take(names), take(moving), take(moving), take(planes)
    cross, = take(["cross"]).values()
    load_sem, core_send, core_recv = take(names), take(names), take(names)
    y_send, y_recv, z_send, z_recv = take(moving), take(moving), take(moving), take(moving)
    x_send, x_recv, last_send, last_recv, give_send, give_recv, keep_sem, row_send, row_recv, row_keep = scratch
    high = z // 2
    order = (3 - 3 * high, 2 - high, 1 - z + 4 * high, z)
    twin = (dp, (1 - x) * 2 + c)
    mate = (dp, x * 2 + 1 - c)
    beside = (z * 2 + 1 - y, sp)
    inner = (z > 0) & (z < NZ - 1)

    def view(ref, name, dest, core_of):
        base = dest * 6
        if name == "A0":
            return ref.at[base + core_of, pl.ds(0, BLANK)]
        if name in ("A1", "A2"):
            return ref.at[base + 2 + core_of, pl.ds(STREAMS[name][1], HALF)]
        slot = base + (4 + x if name == "O" else 5 - x)
        return ref.at[slot, pl.ds(pl.multiple_of(core_of * HALF, HALF), HALF)]

    def remote(src, dst, send, recv, target):
        return pltpu.make_async_remote_copy(
            src_ref=src, dst_ref=dst, send_sem=send, recv_sem=recv,
            device_id=target, device_id_type=MESH,
        )

    def load(name, dest):
        return pltpu.make_async_copy(view(grads, name, dest, c), mine[name].at[dest], load_sem[name].at[dest])

    def to_mate(name, dest):
        return remote(
            view(grads, name, dest, 1 - c), core[name].at[dest],
            core_send[name].at[dest], core_recv[name].at[dest], mate,
        )

    def to_twin(dest):
        return remote(mine["XO"].at[dest], cross.at[dest], x_send.at[dest], x_recv.at[dest], twin)

    def to_side(name, goal):
        at = goal if STREAMS[name][3] else 0
        return remote(
            mine[name].at[goal * 2 + 1 - y], side[name].at[at],
            y_send[name].at[at], y_recv[name].at[at], beside,
        )

    def row_copy(which, source, landing, step, arrival):
        peer = (sp + step) % 4
        at = peer if arrival else sp
        return remote(
            source.at[peer], landing.at[at],
            row_send.at[which, step - 1], row_recv.at[which, at], (dp, peer),
        )

    def column_of(flag):
        return y if flag == 0 else 1 - y

    def dest_of(task):
        if task[0] in ("X", "Z"):
            return order[task[2]] * 2 + column_of(task[3])
        return order[task[2]] * 2 + (1 - y if task[0] == "Y" else y)

    sequence = [
        ("XO" if task[0] == "X" else task[1], dest_of(task)) for task in TASKS if task[0] in ("X", "Y", "C", "Z")
    ]
    for name, dest in sequence:
        load(name, dest).start()
    keeps = [
        pltpu.make_async_copy(rows_a.at[sp], land_a.at[sp], row_keep.at[0]),
        pltpu.make_async_copy(rows_b.at[sp], land_b.at[sp], row_keep.at[1]),
    ]
    for keep in keeps:
        keep.start()
    greet(z, y, x, c)
    for name, dest in sequence:
        to_mate(name, dest).start()

    def merge(name, dest):
        load(name, dest).wait()
        to_mate(name, dest).wait_recv()
        value = mine[name][dest] + core[name][dest]
        if name == "O":
            to_twin(dest).wait_recv()
            value = value + cross[dest]
        mine[name][dest] = value

    def hop(name, goal, column, way, target):
        lane = goal if STREAMS[name][3] else goal * 2 + column
        return remote(
            mine[name].at[goal * 2 + column], line[name].at[way, lane],
            z_send[name].at[lane], z_recv[name].at[way, lane], target,
        )

    def along(name, goal, column):
        dest = goal * 2 + column
        upward = (goal > z).astype(jnp.int32)
        step = 2 * upward - 1
        way = 1 - upward
        item = hop(name, goal, column, way, (dp + 2 * step, sp))
        lane = goal if STREAMS[name][3] else dest

        @pl.when(inner)
        def _():
            item.wait_recv()
            mine[name][dest] = mine[name][dest] + line[name][way, lane]

        item.start()

    def settle(name, column):
        dest = z * 2 + column
        lane = z if STREAMS[name][3] else dest
        for way, valid, step in ((0, z > 0, 1), (1, z < NZ - 1, -1)):
            @pl.when(valid)
            def _():
                hop(name, z, column, way, (dp - 2 * step, sp)).wait_recv()
                mine[name][dest] = mine[name][dest] + line[name][way, lane]

    def swap_last(name):
        at = planes.index(name)
        return remote(mine[name].at[dp], last[name], last_send.at[at], last_recv.at[at], twin)

    def place_of(name, core_of):
        return view(total, name, 0, core_of)

    gift_at = {name: at for at, name in enumerate(planes + ["O", "twin", "XO"])}

    def give(name, key, target, source, core_of):
        at = gift_at[key]
        return remote(source, place_of(name, core_of), give_send.at[at], give_recv.at[at], target)

    gifts, kept = [], []

    def hand_on(name, key, target, source):
        item = give(name, key, target, source, c)
        item.start()
        gifts.append(item)

    def keep_here(name, source):
        item = pltpu.make_async_copy(source, place_of(name, c), keep_sem.at[gift_at[name]])
        item.start()
        kept.append(item)

    for task in TASKS:
        kind, name = task[0], task[1]
        if kind == "R":
            source, landing = ((rows_a, land_a), (rows_b, land_b))[name]
            for step in (2, 3, 1):
                row_copy(name, source, landing, step, False).start()
        elif kind == "X":
            merge("XO", dest_of(task))
            to_twin(dest_of(task)).start()
        elif kind == "Y":
            merge(name, dest_of(task))
            to_side(name, order[task[2]]).start()
        elif kind == "C":
            dest = dest_of(task)
            merge(name, dest)
            to_side(name, order[task[2]]).wait_recv()
            mine[name][dest] = mine[name][dest] + side[name][order[task[2]]]
            if task[2] < 3:
                along(name, order[task[2]], y)
        elif kind == "Z":
            merge(name, dest_of(task))
            if task[2] < 3:
                along(name, order[task[2]], column_of(task[3]))
        elif kind == "F1":
            settle(name, 1 - y)
            to_side(name, z).start()
        elif kind == "F":
            settle(name, y)
            if not STREAMS[name][3]:
                to_side(name, z).wait_recv()
                mine[name][dp] = mine[name][dp] + side[name][0]
            if name in planes:
                swap_last(name).start()
            else:
                hand_on(name, "twin", twin, mine[name].at[dp])
                hand_on(name, "O", mate, mine[name].at[dp])
                keep_here(name, mine[name].at[dp])
        elif kind == "L":
            if name in planes:
                swap_last(name).wait_recv()
                core[name][dp] = mine[name][dp] + last[name][...]
                hand_on(name, name, mate, core[name].at[dp])
                keep_here(name, core[name].at[dp])
            else:
                give("XO", "twin", twin, place_of("XO", c), c).wait_recv()
                hand_on("XO", "XO", mate, place_of("XO", c))

    for name in planes + ["O", "XO"]:
        give(name, name, mate, place_of(name, 1 - c), 1 - c).wait_recv()
    for step in (2, 3, 1):
        for which, source, landing in ((0, rows_a, land_a), (1, rows_b, land_b)):
            row_copy(which, source, landing, step, True).wait_recv()
            row_copy(which, source, landing, step, False).wait_send()
    for name, dest in sequence:
        to_mate(name, dest).wait_send()
    for i in range(4):
        for column in (0, 1):
            to_twin(order[i] * 2 + column).wait_send()
        for name in moving:
            if STREAMS[name][3]:
                to_side(name, order[i]).wait_send()
                if i < 3:
                    hop(name, order[i], y, 0, twin).wait_send()
            elif i < 3:
                for column in (0, 1):
                    hop(name, order[i], column, 0, twin).wait_send()
            else:
                to_side(name, z).wait_send()
    for name in planes:
        swap_last(name).wait_send()
    for item in gifts:
        item.wait_send()
    for item in kept + keeps:
        item.wait()


def reduce_all(grads, rows_a, rows_b):
    anywhere = pl.BlockSpec(memory_space=pl.ANY)
    half = jnp.bfloat16
    dma = pltpu.SemaphoreType.DMA
    moving = [name for name in STREAMS if name != "XO"]
    planes = [name for name in moving if STREAMS[name][2]]

    def buffers(shapes):
        return [pltpu.VMEM((*lead, STREAMS[name][0], BLK), half) for name, lead in shapes]

    first = {name: STREAMS[name][3] for name in moving}
    return pl.pallas_call(
        reduce_kernel,
        name="reduce_all",
        out_shape=[
            jax.ShapeDtypeStruct((6, PITCH, BLK), half),
            pltpu.HBM(rows_a.shape, half),
            pltpu.HBM(rows_b.shape, half),
        ],
        in_specs=[anywhere] * 3,
        out_specs=[anywhere] * 3,
        scratch_shapes=buffers([(name, (8,)) for name in STREAMS] * 2)
        + buffers([(name, (4 if first[name] else 1,)) for name in moving])
        + buffers([(name, (2, 4 if first[name] else 8)) for name in moving])
        + buffers([(name, ()) for name in planes])
        + buffers([("O", (8,))])
        + [dma((8,))] * (3 * len(STREAMS))
        + [dma((4 if first[name] else 1,)) for name in moving] * 2
        + [dma((4 if first[name] else 8,)) for name in moving]
        + [dma((2, 4 if first[name] else 8)) for name in moving]
        + [
            dma((8,)), dma((8,)), dma((len(planes),)), dma((len(planes),)), dma((len(planes) + 3,)),
            dma((len(planes) + 3,)), dma((len(planes) + 1,)), dma((2, 3)), dma((2, 4)), dma((2,)),
        ],
        compiler_params=pltpu.CompilerParams(
            collective_id=1, has_side_effects=True, vmem_limit_bytes=28 << 20
        ),
    )(in_hbm(grads), in_hbm(rows_a), in_hbm(rows_b))


CORRECT = 1.0 - 0.5**STEP
GROUP = 2


def update_kernel(
    total, weights, first, second, left_old, right_old, left_rot, right_rot, vec, vec_first, vec_second, land_a,
    land_b, moment_one, moment_two, left_new, right_new, weights_new, weights_half, vector_one, vector_two, vector_new,
    rows_a, rows_b, held, narrow, wide, stage, stage_half, left, right, out_sem, in_sem, sems,
):
    half = jnp.bfloat16
    take_a = pltpu.make_async_copy(land_a, held, sems.at[0])
    give_a = pltpu.make_async_copy(held, rows_a, sems.at[3])
    take_b = pltpu.make_async_copy(land_b, narrow, sems.at[1])
    give_b = pltpu.make_async_copy(wide, rows_b, sems.at[2])
    count = weights.shape[0]

    def state_of(i):
        return [
            pltpu.make_async_copy(old.at[i], now.at[i], in_sem.at[i, k])
            for k, (old, now) in enumerate(((left_old, left), (right_old, right)))
        ]

    for i in range(count):
        for item in state_of(i):
            item.start()
    take_b.start()
    take_a.start()
    slope = total[0, pl.ds(BLK, 1), :].astype(jnp.float32).reshape(BLK)
    vec_one = 0.5 * vec_first[...] + 0.5 * slope
    vec_two = 0.5 * vec_second[...] + 0.5 * slope * slope
    vector_one[...] = vec_one
    vector_two[...] = vec_two
    vector_new[...] = vec[...] - rate_vector * (
        (vec_one / CORRECT) / (jnp.sqrt(vec_two / CORRECT) + 1e-08)
    )
    targets = (left_new, right_new, moment_one, moment_two, weights_new)

    def outputs(i):
        copies = [
            pltpu.make_async_copy(stage.at[k, i], target.at[i], out_sem.at[i, k])
            for k, target in enumerate(targets)
        ]
        return copies + [pltpu.make_async_copy(stage_half.at[i], weights_half.at[i], out_sem.at[i, 5])]

    def blocks(pair, carry):
        for i in [pair * GROUP + k for k in range(GROUP)]:
            for item in state_of(i):
                item.wait()
        for i in [pair * GROUP + k for k in range(GROUP)]:
            grad = total[i, :BLK, :]
            rot_l = left_rot[i].astype(half)
            rot_r = right_rot[i].astype(half)
            turned = dot_nn(dot_tn(rot_l, grad).astype(half), rot_r)
            stage[0, i] = 0.95 * left[i] + 0.05 * dot_nt(grad, grad)
            one = 0.5 * first[i] + 0.5 * turned
            two = 0.5 * second[i] + 0.5 * turned * turned
            stage[2, i] = one
            stage[3, i] = two
            spread = two * (1.0 / CORRECT)
            ratio = (one * (1.0 / CORRECT)) / (spread * lax.rsqrt(spread) + 1e-08)
            stage[1, i] = 0.95 * right[i] + 0.05 * dot_tn(grad, grad)
            stepped = dot_nt(dot_nn(rot_l, ratio.astype(half)).astype(half), rot_r)
            fresh = weights[i] - rate_matrix * stepped
            stage[4, i] = fresh
            stage_half[i] = fresh.astype(half)
        for i in [pair * GROUP + k for k in range(GROUP)]:
            for item in outputs(i):
                item.start()

        @pl.when(pair == 0)
        def _():
            take_a.wait()
            give_a.start()
            take_b.wait()
            for r in range(narrow.shape[0]):
                wide[r] = narrow[r].astype(jnp.float32)
            give_b.start()

        return carry

    lax.fori_loop(0, weights.shape[0] // GROUP, blocks, 0)
    for i in range(weights.shape[0]):
        for item in outputs(i):
            item.wait()
    give_a.wait()
    give_b.wait()


def update_all(
    total, weights, first, second, left, right, left_rot, right_rot, vec, vec_first, vec_second, land_a, land_b
):
    full = jnp.float32
    vmem = pl.BlockSpec(memory_space=pltpu.VMEM)
    anywhere = pl.BlockSpec(memory_space=pl.ANY)
    vector = jax.ShapeDtypeStruct((BLK,), full)
    matrix = pltpu.HBM(weights.shape, full)
    return pl.pallas_call(
        update_kernel,
        name="update_all",
        out_shape=[matrix] * 5 + [pltpu.HBM(weights.shape, jnp.bfloat16)] + [vector] * 3
        + [pltpu.HBM(land_a.shape, jnp.bfloat16), pltpu.HBM(land_b.shape, full)],
        in_specs=[vmem] * 4 + [anywhere] * 2 + [vmem] * 5 + [anywhere] * 2,
        out_specs=[anywhere] * 6 + [vmem] * 3 + [anywhere] * 2,
        scratch_shapes=[
            pltpu.VMEM(land_a.shape, jnp.bfloat16),
            pltpu.VMEM(land_b.shape, jnp.bfloat16),
            pltpu.VMEM(land_b.shape, full),
            pltpu.VMEM((5, *weights.shape), full),
            pltpu.VMEM(weights.shape, jnp.bfloat16),
            pltpu.VMEM(weights.shape, full),
            pltpu.VMEM(weights.shape, full),
            pltpu.SemaphoreType.DMA((weights.shape[0], 6)),
            pltpu.SemaphoreType.DMA((weights.shape[0], 2)),
            pltpu.SemaphoreType.DMA((4,)),
        ],
        compiler_params=pltpu.CompilerParams(vmem_limit_bytes=38 << 20),
    )(
        total, weights, first, second, in_hbm(left), in_hbm(right), left_rot, right_rot,
        vec, vec_first, vec_second, in_hbm(land_a), in_hbm(land_b),
    )


def fast_device(
    tokens, output_grad, segment_ids, lengths, owner_slot, slot_weights, first_moment, second_moment,
    left_stats, right_stats, left_basis, right_basis, vector_values, vector_first, vector_second,
):
    gathered, token_row, grad_row = gather_all(slot_weights, vector_values, tokens, output_grad)
    placed, block_row, input_row = run_layer(
        owner_slot, gathered, token_row.reshape(-1, D), grad_row.reshape(-1, D), segment_ids
    )
    total, block_land, input_land = reduce_all(
        placed, block_row.reshape(tokens.shape), input_row.reshape(tokens.shape)
    )
    updated = update_all(
        total, slot_weights, first_moment, second_moment, left_stats, right_stats, left_basis, right_basis,
        vector_values, vector_first, vector_second, block_land, input_land,
    )
    vectors = [value.reshape(-1) for value in updated[6:9]]
    return (updated[9], updated[10], *updated[:6], *vectors)


def solution(mesh):
    in_specs = (
        P("dp", "sp", None),
        P("dp", "sp", None),
        P("dp", None),
        P("dp", None),
        P(),
        P("dp", None, None),
        P("dp", None, None),
        P("dp", None, None),
        P("dp", None, None),
        P("dp", None, None),
        P("dp", None, None),
        P("dp", None, None),
        P("dp"),
        P("dp"),
        P("dp"),
    )
    out_specs = (
        P("dp", "sp", None),
        P("dp", "sp", None),
        P("dp", None, None),
        P("dp", None, None),
        P("dp", None, None),
        P("dp", None, None),
        P("dp", None, None),
        P("dp", None, None),
        P("dp"),
        P("dp"),
        P("dp"),
    )
    chosen = fast_device if dict(mesh.shape) == {"dp": 8, "sp": 4} else per_device
    return jax.shard_map(
        chosen, mesh=mesh, in_specs=in_specs, out_specs=out_specs, check_vma=False
    )
```

```python
import math

import jax
import jax.numpy as jnp
from jax import lax
from jax.experimental import pallas as pl
from jax.experimental.pallas import tpu as pltpu
from jax.sharding import PartitionSpec as P

D = 768
HD = 64
FF = 3072
BLK = 384
STEP = 4


highest = lax.Precision.HIGHEST
rate_matrix = 0.04
rate_vector = 0.2


def layer_norm(summed, gain, shift):
    centre = jnp.mean(summed, axis=-1, keepdims=True)
    centred = summed - centre
    spread = jnp.mean(centred * centred, axis=-1, keepdims=True)
    return centred * lax.rsqrt(spread + 1e-06) * gain + shift


def exact_gelu(values):
    return jax.nn.gelu(values, approximate=False)


def passage_mask(segment_row, length_row):
    starts = jnp.cumsum(length_row) - length_row
    number = length_row.shape[0]
    onehot = (segment_row[:, None] == jnp.arange(number, dtype=jnp.int32)[None, :]).astype(
        jnp.int32
    )
    opening = jnp.sum(onehot * starts[None, :], axis=1)
    closing = opening + jnp.sum(onehot * length_row[None, :], axis=1)
    places = jnp.arange(segment_row.shape[0], dtype=jnp.int32)
    return (places[None, :] >= opening[:, None]) & (places[None, :] < closing[:, None])


def into_blocks(matrix):
    height, breadth = matrix.shape
    return (
        matrix.reshape(height // BLK, BLK, breadth // BLK, BLK)
        .transpose(0, 2, 1, 3)
        .reshape(-1, BLK, BLK)
    )


def from_blocks(blocks, height, breadth):
    return (
        blocks.reshape(height // BLK, breadth // BLK, BLK, BLK)
        .transpose(0, 2, 1, 3)
        .reshape(height, breadth)
    )


def split_blocks(blocks):
    square = (D // BLK) ** 2
    broad = D * FF // (BLK * BLK)
    w_query = from_blocks(blocks[0:square], D, D)
    w_key = from_blocks(blocks[square : 2 * square], D, D)
    w_value = from_blocks(blocks[2 * square : 3 * square], D, D)
    w_output = from_blocks(blocks[3 * square : 4 * square], D, D)
    w_upward = from_blocks(blocks[4 * square : 4 * square + broad], D, FF)
    w_downward = from_blocks(blocks[4 * square + broad : 4 * square + 2 * broad], FF, D)
    return (w_query, w_key, w_value, w_output, w_upward, w_downward)


def contract_rows(left_mat, right_mat):
    return lax.dot_general(
        left_mat, right_mat, (((0,), (0,)), ((), ())), preferred_element_type=jnp.float32
    )


def contract_cols(left_mat, right_mat):
    return lax.dot_general(
        left_mat, right_mat, (((1,), (1,)), ((), ())), preferred_element_type=jnp.float32
    )


def soap_update(
    gradient, weights, moment_old, second_old, left_old, right_old, left_rot, right_rot
):
    left_next = 0.95 * left_old + 0.05 * jnp.einsum(
        "nij,nkj->nik", gradient, gradient, precision=highest
    )
    right_next = 0.95 * right_old + 0.05 * jnp.einsum(
        "nji,njk->nik", gradient, gradient, precision=highest
    )
    turned = jnp.einsum("nji,njk->nik", left_rot, gradient, precision=highest)
    turned = jnp.einsum("nij,njk->nik", turned, right_rot, precision=highest)
    moment_next = 0.5 * moment_old + 0.5 * turned
    second_next = 0.5 * second_old + 0.5 * turned * turned
    correct = 1.0 - 0.5**STEP
    ratio = moment_next / correct / (jnp.sqrt(second_next / correct) + 1e-08)
    stepped = jnp.einsum("nij,njk->nik", left_rot, ratio, precision=highest)
    stepped = jnp.einsum("nij,nkj->nik", stepped, right_rot, precision=highest)
    return (moment_next, second_next, left_next, right_next, weights - rate_matrix * stepped)


def adam_update(gradient, values, moment_old, second_old):
    moment_next = 0.5 * moment_old + 0.5 * gradient
    second_next = 0.5 * second_old + 0.5 * gradient * gradient
    correct = 1.0 - 0.5**STEP
    ratio = moment_next / correct / (jnp.sqrt(second_next / correct) + 1e-08)
    return (moment_next, second_next, values - rate_vector * ratio)


def masked_scores(joint_row, segment_row, length_row):
    positions = joint_row.shape[0]
    query = joint_row[:, 0].reshape(positions, -1, HD)
    keyed = joint_row[:, 1].reshape(positions, -1, HD)
    valued = joint_row[:, 2].reshape(positions, -1, HD)
    scores = jnp.einsum("qhd,khd->hqk", query, keyed, preferred_element_type=jnp.float32) * 0.125
    visible = passage_mask(segment_row, length_row)
    return (jnp.where(visible[None], scores, -1e30), query, keyed, valued)


def attend_rows(item):
    joint_row, segment_row, length_row = item
    scores, query, keyed, valued = masked_scores(joint_row, segment_row, length_row)
    largest = jnp.max(scores, axis=-1, keepdims=True)
    raised = jnp.exp(scores - largest)
    totals = jnp.sum(raised, axis=-1, keepdims=True)
    probs = raised / totals
    logsum = (largest + jnp.log(totals))[..., 0]
    context = jnp.einsum(
        "hqk,khd->qhd", probs.astype(jnp.bfloat16), valued, preferred_element_type=jnp.float32
    )
    return (context.reshape(joint_row.shape[0], -1).astype(jnp.bfloat16), logsum)


def back_rows(item):
    joint_row, logsum, delta_context, segment_row, length_row = item
    positions = joint_row.shape[0]
    scores, query, keyed, valued = masked_scores(joint_row, segment_row, length_row)
    probs = jnp.exp(scores - logsum[..., None])
    delta_ctx = delta_context.reshape(positions, -1, HD)
    delta_value = jnp.einsum(
        "hqk,qhd->khd", probs.astype(jnp.bfloat16), delta_ctx, preferred_element_type=jnp.float32
    )
    delta_prob = jnp.einsum("qhd,khd->hqk", delta_ctx, valued, preferred_element_type=jnp.float32)
    weighted = jnp.sum(probs * delta_prob, axis=-1, keepdims=True)
    delta_score = (probs * (delta_prob - weighted)).astype(jnp.bfloat16)
    delta_query = (
        jnp.einsum("hqk,khd->qhd", delta_score, keyed, preferred_element_type=jnp.float32) * 0.125
    )
    delta_key = (
        jnp.einsum("hqk,qhd->khd", delta_score, query, preferred_element_type=jnp.float32) * 0.125
    )
    stacked = jnp.stack(
        [
            delta_query.reshape(positions, -1),
            delta_key.reshape(positions, -1),
            delta_value.reshape(positions, -1),
        ],
        axis=1,
    )
    return stacked.astype(jnp.bfloat16)


def pick_blocks(source, slot_index, owner_slot, fanout, part_index):
    matches = owner_slot[None, :] == slot_index[:, None]
    present = jnp.any(matches, axis=1).astype(jnp.float32)
    chosen = jnp.sum(
        matches.astype(jnp.int32) * jnp.arange(owner_slot.shape[0], dtype=jnp.int32)[None, :],
        axis=1,
    )
    picked = jnp.take(source, chosen * fanout + part_index, axis=0)
    return picked * present[:, None, None]


def per_device(
    tokens,
    output_grad,
    segment_ids,
    lengths,
    owner_slot,
    slot_weights,
    first_moment,
    second_moment,
    left_stats,
    right_stats,
    left_basis,
    right_basis,
    vector_values,
    vector_first,
    vector_second,
):
    holding = slot_weights.shape[0]
    row_count = tokens.shape[0]
    token_count = tokens.shape[1]
    gathered, vector_half = (
        lax.all_gather(slot_weights.astype(jnp.bfloat16), "dp", axis=0, tiled=True),
        lax.all_gather(vector_values.astype(jnp.bfloat16), "dp", axis=0, tiled=True),
    )
    blocks = jnp.take(gathered, owner_slot, axis=0)
    w_query, w_key, w_value, w_output, w_upward, w_downward = split_blocks(blocks)
    w_joint = jnp.concatenate([w_query, w_key, w_value], axis=1)
    gains = vector_half.astype(jnp.float32).reshape(4, D)
    flat_tokens = tokens.reshape(-1, D)
    projected = jnp.dot(flat_tokens, w_joint, preferred_element_type=jnp.float32).astype(
        jnp.bfloat16
    )
    projected = projected.reshape(row_count, token_count, 3, D)
    heads = lax.all_to_all(projected, "sp", split_axis=3, concat_axis=1, tiled=True)
    context, logsum = lax.map(attend_rows, (heads, segment_ids, lengths))
    context_tok = lax.all_to_all(context, "sp", split_axis=1, concat_axis=2, tiled=True).reshape(
        -1, D
    )
    attended = jnp.dot(context_tok, w_output, preferred_element_type=jnp.float32)
    summed_one = flat_tokens.astype(jnp.float32) + attended
    hidden, norm_one_pull = jax.vjp(layer_norm, summed_one, gains[0], gains[1])
    hidden_half = hidden.astype(jnp.bfloat16)
    upward = jnp.dot(hidden_half, w_upward, preferred_element_type=jnp.float32)
    activated, gelu_pull = jax.vjp(exact_gelu, upward)
    active_half = activated.astype(jnp.bfloat16)
    downward = jnp.dot(active_half, w_downward, preferred_element_type=jnp.float32)
    result, norm_two_pull = jax.vjp(layer_norm, hidden + downward, gains[2], gains[3])
    block_out = result.astype(jnp.bfloat16).reshape(row_count, token_count, D)
    cotangent = output_grad.reshape(-1, D).astype(jnp.float32)
    delta_two, delta_gain_two, delta_shift_two = norm_two_pull(cotangent)
    delta_down = delta_two.astype(jnp.bfloat16)
    grad_down = contract_rows(active_half, delta_down)
    delta_active = contract_cols(delta_down, w_downward)
    (delta_upward,) = gelu_pull(delta_active)
    delta_up = delta_upward.astype(jnp.bfloat16)
    grad_up = contract_rows(hidden_half, delta_up)
    delta_hidden = delta_two + contract_cols(delta_up, w_upward)
    delta_one, delta_gain_one, delta_shift_one = norm_one_pull(delta_hidden)
    delta_attn = delta_one.astype(jnp.bfloat16)
    grad_output = contract_rows(context_tok, delta_attn)
    delta_context = (
        contract_cols(delta_attn, w_output).astype(jnp.bfloat16).reshape(row_count, token_count, D)
    )
    delta_heads = lax.all_to_all(delta_context, "sp", split_axis=2, concat_axis=1, tiled=True)
    delta_projected = lax.map(back_rows, (heads, logsum, delta_heads, segment_ids, lengths))
    delta_joint = lax.all_to_all(
        delta_projected, "sp", split_axis=1, concat_axis=3, tiled=True
    ).reshape(-1, 3 * D)
    grad_joint = contract_rows(flat_tokens, delta_joint)
    input_grad = (delta_one + contract_cols(delta_joint, w_joint)).reshape(
        row_count, token_count, D
    )
    grad_blocks = jnp.concatenate(
        [
            into_blocks(grad_joint[:, :D]),
            into_blocks(grad_joint[:, D : 2 * D]),
            into_blocks(grad_joint[:, 2 * D :]),
            into_blocks(grad_output),
            into_blocks(grad_up),
            into_blocks(grad_down),
        ],
        axis=0,
    )
    vector_grad = jnp.concatenate(
        [delta_gain_one, delta_shift_one, delta_gain_two, delta_shift_two]
    )
    vector_total = lax.psum(vector_grad, ("dp", "sp"))
    piece_len = vector_values.shape[0]
    vector_piece = lax.dynamic_slice_in_dim(
        vector_total, lax.axis_index("dp") * piece_len, piece_len
    )
    slot_index = jnp.arange(holding * lax.axis_size("dp"), dtype=jnp.int32)
    owned = lax.psum_scatter(
        pick_blocks(grad_blocks, slot_index, owner_slot, 1, 0),
        "dp",
        scatter_dimension=0,
        tiled=True,
    )
    owned = lax.psum(owned.astype(jnp.bfloat16), "sp").astype(jnp.float32)
    moment_one, moment_two, left_new, right_new, weights_new = soap_update(
        owned,
        slot_weights,
        first_moment,
        second_moment,
        left_stats,
        right_stats,
        left_basis,
        right_basis,
    )
    vector_one, vector_two, vector_new = adam_update(
        vector_piece, vector_values, vector_first, vector_second
    )
    return (
        block_out,
        input_grad,
        moment_one,
        moment_two,
        left_new,
        right_new,
        weights_new,
        weights_new.astype(jnp.bfloat16),
        vector_one,
        vector_two,
        vector_new,
    )


PITCH = BLK + 16
MESH = pl.DeviceIdType.MESH
NZ = 4


def in_hbm(value):
    return pltpu.with_memory_space_constraint(value, pltpu.HBM)


def place():
    dp = lax.axis_index("dp")
    sp = lax.axis_index("sp")
    return dp // 2, dp % 2, sp // 2, sp % 2


def greet(z, y, x, c):
    barrier = pltpu.get_barrier_semaphore()
    dp = z * 2 + y
    sp = x * 2 + c

    def signal(target):
        pl.semaphore_signal(barrier, 1, device_id=target, device_id_type=MESH)

    for step in range(1, 4):
        signal((dp, (sp + step) % 4))
    signal((z * 2 + 1 - y, sp))

    @pl.when(z < NZ - 1)
    def _():
        signal((dp + 2, sp))

    @pl.when(z > 0)
    def _():
        signal((dp - 2, sp))

    pl.semaphore_wait(barrier, 4 + (z < NZ - 1).astype(jnp.int32) + (z > 0).astype(jnp.int32))


PIECES = {
    "A0": (BLK + 16, False, True),
    "A1": (BLK // 2, False, False),
    "O0": (BLK // 2, True, True),
    "O1": (BLK // 4, True, True),
}
STEPS = (
    ("own", "O1"), ("rows", 1), ("own", "O0"), ("own", "A1"), ("z", "O1", 1, 1, 0), ("z", "O1", 1, -1, 0),
    ("y", "O1", 0, 0), ("z", "O0", 1, 1, 0), ("own", "A0"), ("z", "O0", 2, 1, 0), ("y", "O0", 0, 0),
    ("z", "O0", 1, -1, 0), ("z", "O1", 2, -1, 0), ("y", "O1", 1, -1), ("z", "O1", 3, -1, 0), ("z", "A1", 1, 1, 0),
    ("z", "O1", 2, 1, 0), ("y", "O1", 1, 1), ("z", "O0", 3, 1, 0), ("z", "A0", 1, -1, 0), ("y", "O1", 2, -1),
    ("y", "O0", 1, 1), ("z", "O1", 3, 1, 0), ("y", "O0", 2, 1), ("x", "O0", 3, 1, 0), ("x", "O1", 3, -1, 0),
    ("x", "O1", 1, 1, 0), ("z", "A1", 1, -1, 0), ("x", "O0", 1, -1, 0), ("z", "A0", 1, 1, 0),
    ("x", "O1", 1, -1, 1), ("y", "O1", 3, -1), ("y", "A1", 0, 0), ("z", "A0", 2, 1, 0), ("x", "O0", 2, 1, 0),
    ("y", "O1", 2, 1), ("rows", 0), ("z", "O0", 2, -1, 0), ("x", "O0", 2, 1, 1), ("z", "A0", 2, -1, 0),
    ("x", "O1", 0, 0, 1), ("z", "A1", 1, 1, 1), ("x", "O0", 1, 1, 1), ("z", "O0", 3, -1, 0), ("z", "A1", 1, -1, 1),
    ("y", "O0", 2, -1), ("y", "O0", 3, 1), ("y", "A0", 1, -1), ("x", "O1", 2, 1, 1), ("x", "O1", 3, 1, 0),
    ("x", "O0", 0, 0, 1), ("y", "O0", 3, -1), ("z", "A0", 3, 1, 0), ("y", "O1", 3, 1), ("z", "A0", 3, -1, 0),
    ("x", "O0", 1, 1, 0), ("x", "O1", 3, -1, 1), ("y", "O0", 1, -1), ("z", "A1", 2, -1, 0), ("y", "A0", 0, 0),
    ("x", "O1", 2, -1, 1), ("y", "A0", 2, -1), ("z", "A1", 2, -1, 1), ("x", "O0", 2, -1, 0), ("z", "A1", 3, -1, 0),
    ("x", "O0", 3, -1, 0), ("x", "O0", 3, -1, 1), ("z", "A1", 2, 1, 1), ("y", "A0", 2, 1), ("z", "A1", 2, 1, 0),
    ("x", "O0", 3, 1, 1), ("x", "O1", 2, -1, 0), ("z", "A1", 3, 1, 1), ("x", "O1", 2, 1, 0), ("x", "O0", 2, -1, 1),
    ("y", "A0", 3, -1), ("y", "A0", 1, 1), ("y", "A0", 3, 1), ("x", "O1", 3, 1, 1), ("x", "O1", 1, -1, 0),
    ("x", "O1", 1, 1, 1), ("x", "O0", 1, -1, 1), ("z", "A1", 3, -1, 1), ("z", "A1", 3, 1, 0),
)


def piece_view(ref, name, x_of, c_of, base):
    height = PIECES[name][0]
    if name == "A0":
        return ref.at[base + c_of, pl.ds(0, height)]
    if name == "A1":
        slot, row = base + 2, height * c_of
    elif name == "O0":
        slot, row = base + 4 + x_of, height * c_of
    else:
        slot, row = base + 3, 2 * height * x_of + height * c_of
    return ref.at[slot, pl.ds(pl.multiple_of(row, height), height)]


def gather_kernel(weights, vector, tokens, grads, out, token_row, grad_row, wide, narrow, *sems):
    z, y, x, c = place()
    dp = z * 2 + y
    sp = x * 2 + c
    sems = list(sems)
    load_sem, keep_sem, row_send, row_recv, row_keep = [sems.pop(0) for _ in range(5)]
    ways = ("up", "down", "y", "mate", "x", "pass")
    send_sem = {(way, name): sems.pop(0) for way in ways for name in PIECES if PIECES[name][1] or way not in ways[4:]}
    recv_sem = {(way, name): sems.pop(0) for way in ways[2:] for name in PIECES if PIECES[name][1] or way not in ways[4:]}
    targets = {
        "up": (dp + 2, sp), "down": (dp - 2, sp), "y": (z * 2 + 1 - y, sp),
        "x": (dp, (1 - x) * 2 + c), "mate": (dp, x * 2 + 1 - c), "pass": (dp, x * 2 + 1 - c),
    }
    def load_of(i):
        return pltpu.make_async_copy(weights.at[i], wide.at[i], load_sem.at[i])

    for i in (c, 2, 3, 4 + x, 1 - c, 5 - x):
        load_of(i).start()
    keeps = [
        pltpu.make_async_copy(tokens.at[sp], token_row.at[sp], row_keep.at[0]),
        pltpu.make_async_copy(grads.at[sp], grad_row.at[sp], row_keep.at[1]),
    ]
    for keep in keeps:
        keep.start()
    gains = jnp.broadcast_to(vector[...], (16, BLK)).astype(jnp.bfloat16)
    greet(z, y, x, c)

    def row_copy(which, source, landing, step, arrival):
        peer = (sp + step) % 4
        at = peer if arrival else sp
        return pltpu.make_async_remote_copy(
            src_ref=source.at[peer], dst_ref=landing.at[at],
            send_sem=row_send.at[which, step - 1], recv_sem=row_recv.at[which, at],
            device_id=(dp, peer), device_id_type=MESH,
        )

    def round_block(i):
        load_of(i).wait()
        narrow[i, :BLK, :] = wide[i].astype(jnp.bfloat16)
        narrow[i, BLK:, :] = gains

    for i in (c, 2, 3, 4 + x):
        round_block(i)
    own = [pltpu.make_async_copy(narrow.at[i], out.at[dp * 6 + i], keep_sem.at[i]) for i in range(6)]
    started = []

    def item_of(way, name, holder, x_of, c_of, fresh=False):
        landing = piece_view(out, name, x_of, c_of, holder * 6)
        arrives = way if way in ("mate", "x", "pass") else "y"
        return pltpu.make_async_remote_copy(
            src_ref=piece_view(narrow, name, x_of, c_of, 0) if fresh else landing, dst_ref=landing,
            send_sem=send_sem[way, name].at[holder], recv_sem=recv_sem[arrives, name].at[holder],
            device_id=targets[way], device_id_type=MESH,
        )

    def send(way, name, holder, valid, x_of=x, fresh=False):
        if way in ("up", "down"):
            room = z < NZ - 1 if way == "up" else z > 0
            valid = room if valid is None else valid & room
        item = item_of(way, name, holder, x_of, c, fresh)
        if valid is None:
            item.start()
        else:
            pl.when(valid)(item.start)
        started.append((item, valid))

    def arrive(way, name, holder, valid, x_of, c_of):
        item = item_of(way, name, holder, x_of, c_of)
        if valid is None:
            item.wait_recv()
        else:
            pl.when(valid)(item.wait_recv)

    def origin_of(sign, far):
        origin = z + sign * far
        if far == 0:
            return origin, None
        return origin, ((origin >= 0) if sign < 0 else (origin <= NZ - 1))

    for step in STEPS:
        kind, name = step[0], step[1]
        if kind == "own":
            for way in ("up", "down", "y"):
                send(way, name, dp, None, fresh=True)
        elif kind == "rows":
            source, landing = ((tokens, token_row), (grads, grad_row))[name]
            for hop in (2, 3, 1):
                row_copy(name, source, landing, hop, False).start()
        else:
            origin, inside = origin_of(step[3], step[2])
            if kind == "x":
                holder = origin * 2 + (y if step[4] == 0 else 1 - y)
                arrive("x", name, holder, inside, 1 - x, c)
                send("pass", name, holder, inside, 1 - x)
                continue
            holder = origin * 2 + (y if kind == "z" and step[4] == 0 else 1 - y)
            arrive("y", name, holder, inside, x, c)
            if kind == "z":
                if step[2] < NZ - 1:
                    send("up" if step[3] < 0 else "down", name, holder, inside)
                if PIECES[name][2] and step[4] == 0:
                    send("y", name, holder, inside)
            elif not PIECES[name][2]:
                send("up", name, holder, inside)
                send("down", name, holder, inside)
            if PIECES[name][1]:
                send("x", name, holder, inside)
            send("mate", name, holder, inside)
        if kind == "own" and name == "A0":
            for i in (1 - c, 5 - x):
                round_block(i)
            for item in own:
                item.start()

    for far in range(NZ):
        for sign in (0,) if far == 0 else (-1, 1):
            origin, inside = origin_of(sign, far)
            for column in (1,) if far == 0 else (0, 1):
                holder = origin * 2 + (y if column == 0 else 1 - y)
                for name in PIECES:
                    arrive("mate", name, holder, inside, x, 1 - c)
                    if PIECES[name][1]:
                        arrive("pass", name, holder, inside, 1 - x, 1 - c)
    for hop in (2, 3, 1):
        for which, source, landing in ((0, tokens, token_row), (1, grads, grad_row)):
            row_copy(which, source, landing, hop, True).wait_recv()
            row_copy(which, source, landing, hop, False).wait_send()
    for item, valid in started:
        if valid is None:
            item.wait_send()
        else:
            pl.when(valid)(item.wait_send)
    for item in own + keeps:
        item.wait()


def gather_all(weights, vector, tokens, grads):
    anywhere = pl.BlockSpec(memory_space=pl.ANY)
    dma = pltpu.SemaphoreType.DMA
    carried = sum(1 for name in PIECES if PIECES[name][1])
    flows = (4 * len(PIECES) + 2 * carried) + (2 * len(PIECES) + 2 * carried)
    return pl.pallas_call(
        gather_kernel,
        name="gather_all",
        out_shape=[
            pltpu.HBM((48, PITCH, BLK), jnp.bfloat16),
            pltpu.HBM(tokens.shape, jnp.bfloat16),
            pltpu.HBM(grads.shape, jnp.bfloat16),
        ],
        in_specs=[anywhere, pl.BlockSpec(memory_space=pltpu.VMEM), anywhere, anywhere],
        out_specs=[anywhere, anywhere, anywhere],
        scratch_shapes=[
            pltpu.VMEM((6, BLK, BLK), jnp.float32),
            pltpu.VMEM((6, PITCH, BLK), jnp.bfloat16),
            dma((6,)), dma((6,)), dma((2, 3)), dma((2, 4)), dma((2,)),
        ]
        + [dma((8,))] * flows,
        compiler_params=pltpu.CompilerParams(
            collective_id=0, has_side_effects=True, vmem_limit_bytes=24 << 20
        ),
    )(in_hbm(weights), vector.reshape(1, BLK), in_hbm(tokens), in_hbm(grads))


ROW = 512
PAIR = 128
SPAN = 384
EPS = 1e-06


def gelu_of(u):
    bell = jnp.exp(-0.5 * u * u)
    t = 1.0 / (1.0 + (0.3275911 / math.sqrt(2.0)) * jnp.abs(u))
    tail = 0.5 * 1.061405429
    for term in (-1.453152027, 1.421413741, -0.284496736, 0.254829592):
        tail = tail * t + 0.5 * term
    tail = tail * t * bell
    below = jnp.where(u >= 0.0, 1.0 - tail, tail)
    return (u * below).astype(jnp.bfloat16), below + u * (bell * (1.0 / math.sqrt(2.0 * math.pi)))


def dot_nn(a, b):
    return lax.dot_general(a, b, (((1,), (0,)), ((), ())), preferred_element_type=jnp.float32)


def dot_nt(a, b):
    return lax.dot_general(a, b, (((1,), (1,)), ((), ())), preferred_element_type=jnp.float32)


def dot_tn(a, b):
    return lax.dot_general(a, b, (((0,), (0,)), ((), ())), preferred_element_type=jnp.float32)


def layer_kernel(
    owner, weights, tokens, dy_ref, segments, grads, block_out, input_half,
    wqkv, wo, w1, w2, gains, qkv, probs, shares, held, context, hidden, hidden16, norm1, act, slope, dz, dz16,
    dqkv, dup, stage, flipped, flipped_hidden, ups, vecs, spread, w_sem, g_sem, v_sem,
):
    half = jnp.bfloat16
    sp = lax.axis_index("sp")

    def weight_copies():
        copies = []
        for which, ref in enumerate((wqkv.at[0], wqkv.at[1], wqkv.at[2], wo)):
            for r in range(2):
                for q in range(2):
                    copies.append((which * 4 + r * 2 + q, ref, r, q))
        for r in range(2):
            for q in range(8):
                copies.append((16 + r * 8 + q, w1.at[q // 2], r, q % 2))
        for r in range(8):
            for q in range(2):
                copies.append((32 + r * 2 + q, w2.at[r // 2], r % 2, q))
        return [
            pltpu.make_async_copy(
                weights.at[owner[b], pl.ds(0, BLK)],
                ref.at[pl.ds(r * BLK, BLK), pl.ds(q * BLK, BLK)],
                w_sem.at[b],
            )
            for b, ref, r, q in copies
        ]

    copies = weight_copies()
    gain_copies = [
        pltpu.make_async_copy(
            weights.at[6 * d, pl.ds(BLK, 16)], gains.at[d // 2, :, pl.ds((d % 2) * BLK, BLK)], g_sem.at[d]
        )
        for d in range(8)
    ]
    for item in copies[:16] + gain_copies + copies[16:]:
        item.start()

    seg_row = segments[pl.ds(sp, 1), :].astype(jnp.float32)
    spread[...] = jnp.transpose(jnp.broadcast_to(seg_row, (PAIR, ROW)))

    for item in copies[:12]:
        item.wait()
    x = tokens[...]
    flipped[...] = jnp.transpose(x)
    for part in range(3):
        block = dot_nn(x, wqkv[part])
        if part == 0:
            block = block * 0.125
        block = block.astype(half)
        for p in range(6):
            qkv[part * 6 + p] = block[:, p * PAIR : (p + 1) * PAIR]

    lane = lax.broadcasted_iota(jnp.int32, (1, PAIR), 1)
    lows = (lane < 64, lane >= 64)

    def visible(part):
        keys = segments[pl.ds(sp, 1), pl.ds(part * PAIR, SPAN)].astype(jnp.float32)
        own = spread[pl.ds(part * 256, 256), pl.ds(0, 1)]
        return own == keys

    def attend(p, carry):
        q2, k2, v2 = qkv[p], qkv[6 + p], qkv[12 + p]
        for part in range(2):
            mask = visible(part)
            qs = q2[part * 256 : part * 256 + 256]
            ks = k2[part * PAIR : part * PAIR + SPAN]
            vs = v2[part * PAIR : part * PAIR + SPAN]
            outs = []
            for h in range(2):
                scores = dot_nt(jnp.where(lows[h], qs, jnp.zeros_like(qs)), ks)
                scores = jnp.where(mask, scores, -1e30)
                raised = jnp.exp(scores - jnp.max(scores, axis=1, keepdims=True)).astype(half)
                probs[p, 2 * part + h] = raised
                outs.append(dot_nn(raised, jnp.where(lows[h], vs, jnp.ones_like(vs))))
            inverse = 1.0 / pltpu.roll(jnp.where(lows[0], outs[1], outs[0]), 64, 1)
            shares[p, pl.ds(part * 256, 256)] = inverse
            context[p, pl.ds(part * 256, 256)] = (jnp.where(lows[0], outs[0], outs[1]) * inverse).astype(half)
        return carry

    lax.fori_loop(0, 6, attend, 0, unroll=3)

    for item in copies[12:16] + gain_copies:
        item.wait()
    joined = jnp.concatenate([context[p] for p in range(6)], axis=1)

    def gain(k):
        return gains[k, pl.ds(0, 1), :].astype(jnp.float32)

    def normalise(z):
        centre = jnp.mean(z, axis=1, keepdims=True)
        z = z - centre
        inverse = lax.rsqrt(jnp.mean(z * z, axis=1, keepdims=True) + EPS)
        return z * inverse, inverse

    dz[...] = dot_nn(joined, wo[...])

    def norm_one(t, carry):
        rows = pl.ds(pl.multiple_of(t * 128, 128), 128)
        hat, inverse = normalise(tokens[rows, :].astype(jnp.float32) + dz[rows, :])
        norm1[rows, :] = hat
        spread[rows, :] = jnp.where(lane == 1, inverse, spread[rows, :])
        value = hat * gain(0) + gain(1)
        hidden[rows, :] = value
        hidden16[rows, :] = value.astype(half)
        return carry

    lax.fori_loop(0, 4, norm_one, 0)
    for item in copies[16:]:
        item.wait()

    flipped_hidden[...] = jnp.transpose(hidden16[...])
    ups[0] = dot_nn(hidden16[...], w1[0])
    for j in range(5):
        if j < 3:
            ups[(j + 1) % 2] = dot_nn(hidden16[...], w1[j + 1])
        if j < 4:
            act[j], slope[j] = gelu_of(ups[j % 2])
        if j > 0:
            hidden[...] += dot_nn(act[j - 1], w2[j - 1])

    vecs[...] = jnp.zeros_like(vecs)

    def fold(value):
        return jnp.sum(value.reshape(-1, 8, D), axis=0)

    def norm_back(hat, inverse, delta, gain_row):
        e = delta * gain_row
        return (
            e - jnp.mean(e, axis=1, keepdims=True) - hat * jnp.mean(e * hat, axis=1, keepdims=True)
        ) * inverse

    def norm_two(t, carry):
        rows = pl.ds(pl.multiple_of(t * 128, 128), 128)
        hat, inverse = normalise(hidden[rows, :])
        block_out[rows, :] = (hat * gain(2) + gain(3)).astype(half)
        delta = dy_ref[rows, :].astype(jnp.float32)
        vecs[2] += fold(delta * hat)
        vecs[3] += fold(delta)
        back = norm_back(hat, inverse, delta, gain(2))
        dz[rows, :] = back
        dz16[rows, :] = back.astype(half)
        return carry

    lax.fori_loop(0, 4, norm_two, 0)

    def out_copy(slot, b, r, q):
        return pltpu.make_async_copy(
            stage.at[slot, pl.ds(r * BLK, BLK), pl.ds(q * BLK, BLK)],
            grads.at[owner[b], pl.ds(0, BLK)],
            v_sem.at[slot, r * 2 + q],
        )

    def flush(slot, blocks):
        for r in range(2):
            for q in range(2):
                out_copy(slot, blocks(r, q), r, q).start()

    def drain(slot):
        for r in range(2):
            for q in range(2):
                out_copy(slot, 0, r, q).wait()

    def backward(pair, carry):
        @pl.when(pair > 0)
        def _():
            for slot in range(4):
                drain(slot)

        ddown = dz16[...]
        for k in range(2):
            j = 2 * pair + k
            delta = (dot_nt(ddown, w2[j]) * slope[j]).astype(half)
            stage[2 * k] = dot_tn(act[j], ddown).astype(half)
            stage[2 * k + 1] = dot_nn(flipped_hidden[...], delta).astype(half)
            dz[...] += dot_nt(delta, w1[j])
        for k in range(2):
            j = 2 * pair + k
            flush(2 * k, lambda r, q: 32 + (2 * j + r) * 2 + q)
            flush(2 * k + 1, lambda r, q: 16 + r * 8 + 2 * j + q)
        return carry

    lax.fori_loop(0, 2, backward, 0)

    def norm_one_back(t, carry):
        rows = pl.ds(pl.multiple_of(t * 128, 128), 128)
        hat = norm1[rows, :]
        delta = dz[rows, :]
        vecs[0] += fold(delta * hat)
        vecs[1] += fold(delta)
        back = norm_back(hat, spread[rows, pl.ds(1, 1)], delta, gain(0))
        dz[rows, :] = back
        dz16[rows, :] = back.astype(half)
        return carry

    lax.fori_loop(0, 4, norm_one_back, 0)

    for slot in range(4):
        drain(slot)
    dattn = dz16[...]
    stage[0] = dot_tn(joined, dattn).astype(half)
    flush(0, lambda r, q: 12 + r * 2 + q)
    dcontext = dot_nt(dattn, wo[...]).astype(half)
    for p in range(6):
        held[p] = context[p]
        context[p] = dcontext[:, p * PAIR : (p + 1) * PAIR]

    def attend_back(p, carry):
        q2, k2, v2, d2 = qkv[p], qkv[6 + p], qkv[12 + p], context[p]
        dup[...] = jnp.zeros_like(dup)
        for part in range(2):
            window = pl.ds(part * PAIR, SPAN)
            qs = q2[part * 256 : part * 256 + 256]
            ds = d2[part * 256 : part * 256 + 256]
            ks = k2[part * PAIR : part * PAIR + SPAN]
            vs = v2[part * PAIR : part * PAIR + SPAN]
            dvs, dqs, dks = [], [], []
            share = shares[p, pl.ds(part * 256, 256)]
            scaled = (ds.astype(jnp.float32) * share).astype(half)
            weight = scaled.astype(jnp.float32) * held[p, pl.ds(part * 256, 256)].astype(jnp.float32)
            for h in range(2):
                raised = probs[p, 2 * part + h]
                dprob = dot_nt(jnp.where(lows[h], scaled, jnp.zeros_like(scaled)), vs)
                centre = jnp.sum(jnp.where(lows[h], weight, 0.0), axis=1, keepdims=True)
                dscore = (raised.astype(jnp.float32) * (dprob - centre)).astype(half)
                dvs.append(dot_tn(raised, scaled))
                dqs.append(dot_nn(dscore, ks))
                dks.append(dot_tn(dscore, qs))
            dqkv[p, pl.ds(part * 256, 256)] = (
                jnp.where(lows[0], dqs[0], dqs[1]) * 0.125
            ).astype(half)
            dup[0, window] += jnp.where(lows[0], dks[0], dks[1])
            dup[1, window] += jnp.where(lows[0], dvs[0], dvs[1])
        dqkv[6 + p] = dup[0].astype(half)
        dqkv[12 + p] = dup[1].astype(half)
        return carry

    lax.fori_loop(0, 6, attend_back, 0, unroll=3)

    for part in range(3):
        delta = jnp.concatenate([dqkv[part * 6 + p] for p in range(6)], axis=1)
        stage[1 + part] = dot_nn(flipped[...], delta).astype(half)
        flush(1 + part, lambda r, q: part * 4 + r * 2 + q)
        dz[...] += dot_nt(delta, wqkv[part])

    input_half[...] = dz[...].astype(half)
    for k in range(4):
        row = jnp.sum(vecs[k], axis=0, keepdims=True)
        vecs16 = jnp.broadcast_to(row, (16, D)).astype(half)
        gains[k] = vecs16
    for k in range(4):
        for q in range(2):
            for s in range(2):
                pltpu.make_async_copy(
                    gains.at[k, :, pl.ds(q * BLK, BLK)],
                    grads.at[6 * (2 * k + q) + s, pl.ds(BLK, 16)],
                    w_sem.at[(2 * k + q) * 2 + s],
                ).start()
    for k in range(4):
        for q in range(2):
            for s in range(2):
                pltpu.make_async_copy(
                    gains.at[k, :, pl.ds(q * BLK, BLK)],
                    grads.at[6 * (2 * k + q) + s, pl.ds(BLK, 16)],
                    w_sem.at[(2 * k + q) * 2 + s],
                ).wait()
    for slot in range(4):
        drain(slot)


def run_layer(owner_slot, gathered, token_row, grad_row, segment_ids):
    half, full = jnp.bfloat16, jnp.float32
    anywhere = pl.BlockSpec(memory_space=pltpu.HBM)
    vmem = pl.BlockSpec(memory_space=pltpu.VMEM)
    dma = pltpu.SemaphoreType.DMA
    return pl.pallas_call(
        layer_kernel,
        name="run_layer",
        out_shape=[
            jax.ShapeDtypeStruct((48, PITCH, BLK), half),
            jax.ShapeDtypeStruct((ROW, D), half),
            jax.ShapeDtypeStruct((ROW, D), half),
        ],
        in_specs=[pl.BlockSpec(memory_space=pltpu.SMEM), anywhere, vmem, vmem, vmem],
        out_specs=[anywhere, vmem, vmem],
        scratch_shapes=[
            pltpu.VMEM((3, D, D), half),
            pltpu.VMEM((D, D), half),
            pltpu.VMEM((4, D, D), half),
            pltpu.VMEM((4, D, D), half),
            pltpu.VMEM((4, 16, D), half),
            pltpu.VMEM((18, ROW, PAIR), half),
            pltpu.VMEM((6, 4, 256, SPAN), half),
            pltpu.VMEM((6, ROW, PAIR), full),
            pltpu.VMEM((6, ROW, PAIR), half),
            pltpu.VMEM((6, ROW, PAIR), half),
            pltpu.VMEM((ROW, D), full),
            pltpu.VMEM((ROW, D), half),
            pltpu.VMEM((ROW, D), full),
            pltpu.VMEM((4, ROW, D), half),
            pltpu.VMEM((4, ROW, D), full),
            pltpu.VMEM((ROW, D), full),
            pltpu.VMEM((ROW, D), half),
            pltpu.VMEM((18, ROW, PAIR), half),
            pltpu.VMEM((2, ROW, PAIR), full),
            pltpu.VMEM((4, D, D), half),
            pltpu.VMEM((D, ROW), half),
            pltpu.VMEM((D, ROW), half),
            pltpu.VMEM((2, ROW, D), full),
            pltpu.VMEM((4, 8, D), full),
            pltpu.VMEM((ROW, PAIR), full),
            dma((48,)),
            dma((8,)),
            dma((4, 4)),
        ],
        compiler_params=pltpu.CompilerParams(vmem_limit_bytes=58 << 20),
    )(owner_slot, gathered, token_row, grad_row, segment_ids)


BLANK = BLK + 16
HALF = BLK // 2
STREAMS = {
    "A0": (BLANK, 0, True, True),
    "A1": (HALF, 0, True, True),
    "A2": (HALF, HALF, True, False),
    "O": (HALF, 0, False, True),
    "XO": (HALF, 0, False, True),
}
TASKS = (
    ("Y", "A1", 3), ("Z", "A2", 0, 1), ("Y", "A0", 0), ("X", "O", 0, 1), ("Z", "A2", 0, 0), ("X", "O", 2, 1),
    ("X", "O", 1, 0), ("Y", "A0", 1), ("Z", "A2", 1, 1), ("Y", "A0", 2), ("Z", "A2", 2, 0), ("X", "O", 0, 0),
    ("X", "O", 3, 0), ("Y", "O", 0), ("C", "A0", 0), ("Z", "A2", 2, 1), ("X", "O", 1, 1), ("Y", "O", 2),
    ("Y", "A0", 3), ("X", "O", 3, 1), ("X", "O", 2, 0), ("C", "A0", 1), ("R", 1), ("Y", "O", 1), ("Y", "A1", 0),
    ("C", "A1", 3), ("Z", "A2", 3, 1), ("Y", "O", 3), ("C", "O", 0), ("R", 0), ("C", "A0", 2), ("Y", "A1", 1),
    ("C", "A0", 3), ("C", "O", 2), ("Y", "A1", 2), ("C", "O", 1), ("F", "A0"), ("F1", "A2"), ("C", "A1", 0),
    ("C", "O", 3), ("Z", "A2", 3, 0), ("F", "O"), ("Z", "A2", 1, 0), ("C", "A1", 1), ("C", "A1", 2), ("F", "A2"),
    ("L", "O"), ("F", "A1"), ("L", "A0"), ("L", "A2"), ("L", "A1"),
)


def reduce_kernel(grads, rows_a, rows_b, total, land_a, land_b, *scratch):
    z, y, x, c = place()
    dp = z * 2 + y
    sp = x * 2 + c
    names = list(STREAMS)
    moving = [name for name in names if name != "XO"]
    planes = [name for name in moving if STREAMS[name][2]]
    scratch = list(scratch)

    def take(keys):
        return {key: scratch.pop(0) for key in keys}

    mine, core, side, line, last = take(names), take(names), take(moving), take(moving), take(planes)
    cross, = take(["cross"]).values()
    load_sem, core_send, core_recv = take(names), take(names), take(names)
    y_send, y_recv, z_send, z_recv = take(moving), take(moving), take(moving), take(moving)
    x_send, x_recv, last_send, last_recv, give_send, give_recv, keep_sem, row_send, row_recv, row_keep = scratch
    high = z // 2
    order = (3 - 3 * high, 2 - high, 1 - z + 4 * high, z)
    twin = (dp, (1 - x) * 2 + c)
    mate = (dp, x * 2 + 1 - c)
    beside = (z * 2 + 1 - y, sp)
    inner = (z > 0) & (z < NZ - 1)

    def view(ref, name, dest, core_of):
        base = dest * 6
        if name == "A0":
            return ref.at[base + core_of, pl.ds(0, BLANK)]
        if name in ("A1", "A2"):
            return ref.at[base + 2 + core_of, pl.ds(STREAMS[name][1], HALF)]
        slot = base + (4 + x if name == "O" else 5 - x)
        return ref.at[slot, pl.ds(pl.multiple_of(core_of * HALF, HALF), HALF)]

    def remote(src, dst, send, recv, target):
        return pltpu.make_async_remote_copy(
            src_ref=src, dst_ref=dst, send_sem=send, recv_sem=recv,
            device_id=target, device_id_type=MESH,
        )

    def load(name, dest):
        return pltpu.make_async_copy(view(grads, name, dest, c), mine[name].at[dest], load_sem[name].at[dest])

    def to_mate(name, dest):
        return remote(
            view(grads, name, dest, 1 - c), core[name].at[dest],
            core_send[name].at[dest], core_recv[name].at[dest], mate,
        )

    def to_twin(dest):
        return remote(mine["XO"].at[dest], cross.at[dest], x_send.at[dest], x_recv.at[dest], twin)

    def to_side(name, goal):
        at = goal if STREAMS[name][3] else 0
        return remote(
            mine[name].at[goal * 2 + 1 - y], side[name].at[at],
            y_send[name].at[at], y_recv[name].at[at], beside,
        )

    def row_copy(which, source, landing, step, arrival):
        peer = (sp + step) % 4
        at = peer if arrival else sp
        return remote(
            source.at[peer], landing.at[at],
            row_send.at[which, step - 1], row_recv.at[which, at], (dp, peer),
        )

    def column_of(flag):
        return y if flag == 0 else 1 - y

    def dest_of(task):
        if task[0] in ("X", "Z"):
            return order[task[2]] * 2 + column_of(task[3])
        return order[task[2]] * 2 + (1 - y if task[0] == "Y" else y)

    sequence = [
        ("XO" if task[0] == "X" else task[1], dest_of(task)) for task in TASKS if task[0] in ("X", "Y", "C", "Z")
    ]
    for name, dest in sequence:
        load(name, dest).start()
    keeps = [
        pltpu.make_async_copy(rows_a.at[sp], land_a.at[sp], row_keep.at[0]),
        pltpu.make_async_copy(rows_b.at[sp], land_b.at[sp], row_keep.at[1]),
    ]
    for keep in keeps:
        keep.start()
    greet(z, y, x, c)
    for name, dest in sequence:
        to_mate(name, dest).start()

    def merge(name, dest):
        load(name, dest).wait()
        to_mate(name, dest).wait_recv()
        value = mine[name][dest] + core[name][dest]
        if name == "O":
            to_twin(dest).wait_recv()
            value = value + cross[dest]
        mine[name][dest] = value

    def hop(name, goal, column, way, target):
        lane = goal if STREAMS[name][3] else goal * 2 + column
        return remote(
            mine[name].at[goal * 2 + column], line[name].at[way, lane],
            z_send[name].at[lane], z_recv[name].at[way, lane], target,
        )

    def along(name, goal, column):
        dest = goal * 2 + column
        upward = (goal > z).astype(jnp.int32)
        step = 2 * upward - 1
        way = 1 - upward
        item = hop(name, goal, column, way, (dp + 2 * step, sp))
        lane = goal if STREAMS[name][3] else dest

        @pl.when(inner)
        def _():
            item.wait_recv()
            mine[name][dest] = mine[name][dest] + line[name][way, lane]

        item.start()

    def settle(name, column):
        dest = z * 2 + column
        lane = z if STREAMS[name][3] else dest
        for way, valid, step in ((0, z > 0, 1), (1, z < NZ - 1, -1)):
            @pl.when(valid)
            def _():
                hop(name, z, column, way, (dp - 2 * step, sp)).wait_recv()
                mine[name][dest] = mine[name][dest] + line[name][way, lane]

    def swap_last(name):
        at = planes.index(name)
        return remote(mine[name].at[dp], last[name], last_send.at[at], last_recv.at[at], twin)

    def place_of(name, core_of):
        return view(total, name, 0, core_of)

    gift_at = {name: at for at, name in enumerate(planes + ["O", "twin", "XO"])}

    def give(name, key, target, source, core_of):
        at = gift_at[key]
        return remote(source, place_of(name, core_of), give_send.at[at], give_recv.at[at], target)

    gifts, kept = [], []

    def hand_on(name, key, target, source):
        item = give(name, key, target, source, c)
        item.start()
        gifts.append(item)

    def keep_here(name, source):
        item = pltpu.make_async_copy(source, place_of(name, c), keep_sem.at[gift_at[name]])
        item.start()
        kept.append(item)

    for task in TASKS:
        kind, name = task[0], task[1]
        if kind == "R":
            source, landing = ((rows_a, land_a), (rows_b, land_b))[name]
            for step in (2, 3, 1):
                row_copy(name, source, landing, step, False).start()
        elif kind == "X":
            merge("XO", dest_of(task))
            to_twin(dest_of(task)).start()
        elif kind == "Y":
            merge(name, dest_of(task))
            to_side(name, order[task[2]]).start()
        elif kind == "C":
            dest = dest_of(task)
            merge(name, dest)
            to_side(name, order[task[2]]).wait_recv()
            mine[name][dest] = mine[name][dest] + side[name][order[task[2]]]
            if task[2] < 3:
                along(name, order[task[2]], y)
        elif kind == "Z":
            merge(name, dest_of(task))
            if task[2] < 3:
                along(name, order[task[2]], column_of(task[3]))
        elif kind == "F1":
            settle(name, 1 - y)
            to_side(name, z).start()
        elif kind == "F":
            settle(name, y)
            if not STREAMS[name][3]:
                to_side(name, z).wait_recv()
                mine[name][dp] = mine[name][dp] + side[name][0]
            if name in planes:
                swap_last(name).start()
            else:
                hand_on(name, "twin", twin, mine[name].at[dp])
                hand_on(name, "O", mate, mine[name].at[dp])
                keep_here(name, mine[name].at[dp])
        elif kind == "L":
            if name in planes:
                swap_last(name).wait_recv()
                core[name][dp] = mine[name][dp] + last[name][...]
                hand_on(name, name, mate, core[name].at[dp])
                keep_here(name, core[name].at[dp])
            else:
                give("XO", "twin", twin, place_of("XO", c), c).wait_recv()
                hand_on("XO", "XO", mate, place_of("XO", c))

    for name in planes + ["O", "XO"]:
        give(name, name, mate, place_of(name, 1 - c), 1 - c).wait_recv()
    for step in (2, 3, 1):
        for which, source, landing in ((0, rows_a, land_a), (1, rows_b, land_b)):
            row_copy(which, source, landing, step, True).wait_recv()
            row_copy(which, source, landing, step, False).wait_send()
    for name, dest in sequence:
        to_mate(name, dest).wait_send()
    for i in range(4):
        for column in (0, 1):
            to_twin(order[i] * 2 + column).wait_send()
        for name in moving:
            if STREAMS[name][3]:
                to_side(name, order[i]).wait_send()
                if i < 3:
                    hop(name, order[i], y, 0, twin).wait_send()
            elif i < 3:
                for column in (0, 1):
                    hop(name, order[i], column, 0, twin).wait_send()
            else:
                to_side(name, z).wait_send()
    for name in planes:
        swap_last(name).wait_send()
    for item in gifts:
        item.wait_send()
    for item in kept + keeps:
        item.wait()


def reduce_all(grads, rows_a, rows_b):
    anywhere = pl.BlockSpec(memory_space=pl.ANY)
    half = jnp.bfloat16
    dma = pltpu.SemaphoreType.DMA
    moving = [name for name in STREAMS if name != "XO"]
    planes = [name for name in moving if STREAMS[name][2]]

    def buffers(shapes):
        return [pltpu.VMEM((*lead, STREAMS[name][0], BLK), half) for name, lead in shapes]

    first = {name: STREAMS[name][3] for name in moving}
    return pl.pallas_call(
        reduce_kernel,
        name="reduce_all",
        out_shape=[
            jax.ShapeDtypeStruct((6, PITCH, BLK), half),
            pltpu.HBM(rows_a.shape, half),
            pltpu.HBM(rows_b.shape, half),
        ],
        in_specs=[anywhere] * 3,
        out_specs=[anywhere] * 3,
        scratch_shapes=buffers([(name, (8,)) for name in STREAMS] * 2)
        + buffers([(name, (4 if first[name] else 1,)) for name in moving])
        + buffers([(name, (2, 4 if first[name] else 8)) for name in moving])
        + buffers([(name, ()) for name in planes])
        + buffers([("O", (8,))])
        + [dma((8,))] * (3 * len(STREAMS))
        + [dma((4 if first[name] else 1,)) for name in moving] * 2
        + [dma((4 if first[name] else 8,)) for name in moving]
        + [dma((2, 4 if first[name] else 8)) for name in moving]
        + [
            dma((8,)), dma((8,)), dma((len(planes),)), dma((len(planes),)), dma((len(planes) + 3,)),
            dma((len(planes) + 3,)), dma((len(planes) + 1,)), dma((2, 3)), dma((2, 4)), dma((2,)),
        ],
        compiler_params=pltpu.CompilerParams(
            collective_id=1, has_side_effects=True, vmem_limit_bytes=28 << 20
        ),
    )(in_hbm(grads), in_hbm(rows_a), in_hbm(rows_b))


CORRECT = 1.0 - 0.5**STEP
GROUP = 2


def update_kernel(
    total, weights, first, second, left_old, right_old, left_rot, right_rot, vec, vec_first, vec_second, land_a,
    land_b, moment_one, moment_two, left_new, right_new, weights_new, weights_half, vector_one, vector_two, vector_new,
    rows_a, rows_b, held, narrow, wide, stage, stage_half, left, right, out_sem, in_sem, sems,
):
    half = jnp.bfloat16
    take_a = pltpu.make_async_copy(land_a, held, sems.at[0])
    give_a = pltpu.make_async_copy(held, rows_a, sems.at[3])
    take_b = pltpu.make_async_copy(land_b, narrow, sems.at[1])
    give_b = pltpu.make_async_copy(wide, rows_b, sems.at[2])
    count = weights.shape[0]

    def state_of(i):
        return [
            pltpu.make_async_copy(old.at[i], now.at[i], in_sem.at[i, k])
            for k, (old, now) in enumerate(((left_old, left), (right_old, right)))
        ]

    for i in range(count):
        for item in state_of(i):
            item.start()
    take_b.start()
    take_a.start()
    slope = total[0, pl.ds(BLK, 1), :].astype(jnp.float32).reshape(BLK)
    vec_one = 0.5 * vec_first[...] + 0.5 * slope
    vec_two = 0.5 * vec_second[...] + 0.5 * slope * slope
    vector_one[...] = vec_one
    vector_two[...] = vec_two
    vector_new[...] = vec[...] - rate_vector * (
        (vec_one / CORRECT) / (jnp.sqrt(vec_two / CORRECT) + 1e-08)
    )
    targets = (left_new, right_new, moment_one, moment_two, weights_new)

    def outputs(i):
        copies = [
            pltpu.make_async_copy(stage.at[k, i], target.at[i], out_sem.at[i, k])
            for k, target in enumerate(targets)
        ]
        return copies + [pltpu.make_async_copy(stage_half.at[i], weights_half.at[i], out_sem.at[i, 5])]

    def blocks(pair, carry):
        for i in [pair * GROUP + k for k in range(GROUP)]:
            for item in state_of(i):
                item.wait()
        for i in [pair * GROUP + k for k in range(GROUP)]:
            grad = total[i, :BLK, :]
            rot_l = left_rot[i].astype(half)
            rot_r = right_rot[i].astype(half)
            turned = dot_nn(dot_tn(rot_l, grad).astype(half), rot_r)
            stage[0, i] = 0.95 * left[i] + 0.05 * dot_nt(grad, grad)
            one = 0.5 * first[i] + 0.5 * turned
            two = 0.5 * second[i] + 0.5 * turned * turned
            stage[2, i] = one
            stage[3, i] = two
            spread = two * (1.0 / CORRECT)
            ratio = (one * (1.0 / CORRECT)) / (spread * lax.rsqrt(spread) + 1e-08)
            stage[1, i] = 0.95 * right[i] + 0.05 * dot_tn(grad, grad)
            stepped = dot_nt(dot_nn(rot_l, ratio.astype(half)).astype(half), rot_r)
            fresh = weights[i] - rate_matrix * stepped
            stage[4, i] = fresh
            stage_half[i] = fresh.astype(half)
        for i in [pair * GROUP + k for k in range(GROUP)]:
            for item in outputs(i):
                item.start()

        @pl.when(pair == 0)
        def _():
            take_a.wait()
            give_a.start()
            take_b.wait()
            for r in range(narrow.shape[0]):
                wide[r] = narrow[r].astype(jnp.float32)
            give_b.start()

        return carry

    lax.fori_loop(0, weights.shape[0] // GROUP, blocks, 0)
    for i in range(weights.shape[0]):
        for item in outputs(i):
            item.wait()
    give_a.wait()
    give_b.wait()


def update_all(
    total, weights, first, second, left, right, left_rot, right_rot, vec, vec_first, vec_second, land_a, land_b
):
    full = jnp.float32
    vmem = pl.BlockSpec(memory_space=pltpu.VMEM)
    anywhere = pl.BlockSpec(memory_space=pl.ANY)
    vector = jax.ShapeDtypeStruct((BLK,), full)
    matrix = pltpu.HBM(weights.shape, full)
    return pl.pallas_call(
        update_kernel,
        name="update_all",
        out_shape=[matrix] * 5 + [pltpu.HBM(weights.shape, jnp.bfloat16)] + [vector] * 3
        + [pltpu.HBM(land_a.shape, jnp.bfloat16), pltpu.HBM(land_b.shape, full)],
        in_specs=[vmem] * 4 + [anywhere] * 2 + [vmem] * 5 + [anywhere] * 2,
        out_specs=[anywhere] * 6 + [vmem] * 3 + [anywhere] * 2,
        scratch_shapes=[
            pltpu.VMEM(land_a.shape, jnp.bfloat16),
            pltpu.VMEM(land_b.shape, jnp.bfloat16),
            pltpu.VMEM(land_b.shape, full),
            pltpu.VMEM((5, *weights.shape), full),
            pltpu.VMEM(weights.shape, jnp.bfloat16),
            pltpu.VMEM(weights.shape, full),
            pltpu.VMEM(weights.shape, full),
            pltpu.SemaphoreType.DMA((weights.shape[0], 6)),
            pltpu.SemaphoreType.DMA((weights.shape[0], 2)),
            pltpu.SemaphoreType.DMA((4,)),
        ],
        compiler_params=pltpu.CompilerParams(vmem_limit_bytes=38 << 20),
    )(
        total, weights, first, second, in_hbm(left), in_hbm(right), left_rot, right_rot,
        vec, vec_first, vec_second, in_hbm(land_a), in_hbm(land_b),
    )


def fast_device(
    tokens, output_grad, segment_ids, lengths, owner_slot, slot_weights, first_moment, second_moment,
    left_stats, right_stats, left_basis, right_basis, vector_values, vector_first, vector_second,
):
    gathered, token_row, grad_row = gather_all(slot_weights, vector_values, tokens, output_grad)
    placed, block_row, input_row = run_layer(
        owner_slot, gathered, token_row.reshape(-1, D), grad_row.reshape(-1, D), segment_ids
    )
    total, block_land, input_land = reduce_all(
        placed, block_row.reshape(tokens.shape), input_row.reshape(tokens.shape)
    )
    updated = update_all(
        total, slot_weights, first_moment, second_moment, left_stats, right_stats, left_basis, right_basis,
        vector_values, vector_first, vector_second, block_land, input_land,
    )
    vectors = [value.reshape(-1) for value in updated[6:9]]
    return (updated[9], updated[10], *updated[:6], *vectors)


def solution(mesh):
    in_specs = (
        P("dp", "sp", None),
        P("dp", "sp", None),
        P("dp", None),
        P("dp", None),
        P(),
        P("dp", None, None),
        P("dp", None, None),
        P("dp", None, None),
        P("dp", None, None),
        P("dp", None, None),
        P("dp", None, None),
        P("dp", None, None),
        P("dp"),
        P("dp"),
        P("dp"),
    )
    out_specs = (
        P("dp", "sp", None),
        P("dp", "sp", None),
        P("dp", None, None),
        P("dp", None, None),
        P("dp", None, None),
        P("dp", None, None),
        P("dp", None, None),
        P("dp", None, None),
        P("dp"),
        P("dp"),
        P("dp"),
    )
    chosen = fast_device if dict(mesh.shape) == {"dp": 8, "sp": 4} else per_device
    return jax.shard_map(
        chosen, mesh=mesh, in_specs=in_specs, out_specs=out_specs, check_vma=False
    )
```

```python
import math

import jax
import jax.numpy as jnp
from jax import lax
from jax.experimental import pallas as pl
from jax.experimental.pallas import tpu as pltpu
from jax.sharding import PartitionSpec as P

D = 768
HD = 64
FF = 3072
BLK = 384
STEP = 4


highest = lax.Precision.HIGHEST
rate_matrix = 0.04
rate_vector = 0.2


def layer_norm(summed, gain, shift):
    centre = jnp.mean(summed, axis=-1, keepdims=True)
    centred = summed - centre
    spread = jnp.mean(centred * centred, axis=-1, keepdims=True)
    return centred * lax.rsqrt(spread + 1e-06) * gain + shift


def exact_gelu(values):
    return jax.nn.gelu(values, approximate=False)


def passage_mask(segment_row, length_row):
    starts = jnp.cumsum(length_row) - length_row
    number = length_row.shape[0]
    onehot = (segment_row[:, None] == jnp.arange(number, dtype=jnp.int32)[None, :]).astype(
        jnp.int32
    )
    opening = jnp.sum(onehot * starts[None, :], axis=1)
    closing = opening + jnp.sum(onehot * length_row[None, :], axis=1)
    places = jnp.arange(segment_row.shape[0], dtype=jnp.int32)
    return (places[None, :] >= opening[:, None]) & (places[None, :] < closing[:, None])


def into_blocks(matrix):
    height, breadth = matrix.shape
    return (
        matrix.reshape(height // BLK, BLK, breadth // BLK, BLK)
        .transpose(0, 2, 1, 3)
        .reshape(-1, BLK, BLK)
    )


def from_blocks(blocks, height, breadth):
    return (
        blocks.reshape(height // BLK, breadth // BLK, BLK, BLK)
        .transpose(0, 2, 1, 3)
        .reshape(height, breadth)
    )


def split_blocks(blocks):
    square = (D // BLK) ** 2
    broad = D * FF // (BLK * BLK)
    w_query = from_blocks(blocks[0:square], D, D)
    w_key = from_blocks(blocks[square : 2 * square], D, D)
    w_value = from_blocks(blocks[2 * square : 3 * square], D, D)
    w_output = from_blocks(blocks[3 * square : 4 * square], D, D)
    w_upward = from_blocks(blocks[4 * square : 4 * square + broad], D, FF)
    w_downward = from_blocks(blocks[4 * square + broad : 4 * square + 2 * broad], FF, D)
    return (w_query, w_key, w_value, w_output, w_upward, w_downward)


def contract_rows(left_mat, right_mat):
    return lax.dot_general(
        left_mat, right_mat, (((0,), (0,)), ((), ())), preferred_element_type=jnp.float32
    )


def contract_cols(left_mat, right_mat):
    return lax.dot_general(
        left_mat, right_mat, (((1,), (1,)), ((), ())), preferred_element_type=jnp.float32
    )


def soap_update(
    gradient, weights, moment_old, second_old, left_old, right_old, left_rot, right_rot
):
    left_next = 0.95 * left_old + 0.05 * jnp.einsum(
        "nij,nkj->nik", gradient, gradient, precision=highest
    )
    right_next = 0.95 * right_old + 0.05 * jnp.einsum(
        "nji,njk->nik", gradient, gradient, precision=highest
    )
    turned = jnp.einsum("nji,njk->nik", left_rot, gradient, precision=highest)
    turned = jnp.einsum("nij,njk->nik", turned, right_rot, precision=highest)
    moment_next = 0.5 * moment_old + 0.5 * turned
    second_next = 0.5 * second_old + 0.5 * turned * turned
    correct = 1.0 - 0.5**STEP
    ratio = moment_next / correct / (jnp.sqrt(second_next / correct) + 1e-08)
    stepped = jnp.einsum("nij,njk->nik", left_rot, ratio, precision=highest)
    stepped = jnp.einsum("nij,nkj->nik", stepped, right_rot, precision=highest)
    return (moment_next, second_next, left_next, right_next, weights - rate_matrix * stepped)


def adam_update(gradient, values, moment_old, second_old):
    moment_next = 0.5 * moment_old + 0.5 * gradient
    second_next = 0.5 * second_old + 0.5 * gradient * gradient
    correct = 1.0 - 0.5**STEP
    ratio = moment_next / correct / (jnp.sqrt(second_next / correct) + 1e-08)
    return (moment_next, second_next, values - rate_vector * ratio)


def masked_scores(joint_row, segment_row, length_row):
    positions = joint_row.shape[0]
    query = joint_row[:, 0].reshape(positions, -1, HD)
    keyed = joint_row[:, 1].reshape(positions, -1, HD)
    valued = joint_row[:, 2].reshape(positions, -1, HD)
    scores = jnp.einsum("qhd,khd->hqk", query, keyed, preferred_element_type=jnp.float32) * 0.125
    visible = passage_mask(segment_row, length_row)
    return (jnp.where(visible[None], scores, -1e30), query, keyed, valued)


def attend_rows(item):
    joint_row, segment_row, length_row = item
    scores, query, keyed, valued = masked_scores(joint_row, segment_row, length_row)
    largest = jnp.max(scores, axis=-1, keepdims=True)
    raised = jnp.exp(scores - largest)
    totals = jnp.sum(raised, axis=-1, keepdims=True)
    probs = raised / totals
    logsum = (largest + jnp.log(totals))[..., 0]
    context = jnp.einsum(
        "hqk,khd->qhd", probs.astype(jnp.bfloat16), valued, preferred_element_type=jnp.float32
    )
    return (context.reshape(joint_row.shape[0], -1).astype(jnp.bfloat16), logsum)


def back_rows(item):
    joint_row, logsum, delta_context, segment_row, length_row = item
    positions = joint_row.shape[0]
    scores, query, keyed, valued = masked_scores(joint_row, segment_row, length_row)
    probs = jnp.exp(scores - logsum[..., None])
    delta_ctx = delta_context.reshape(positions, -1, HD)
    delta_value = jnp.einsum(
        "hqk,qhd->khd", probs.astype(jnp.bfloat16), delta_ctx, preferred_element_type=jnp.float32
    )
    delta_prob = jnp.einsum("qhd,khd->hqk", delta_ctx, valued, preferred_element_type=jnp.float32)
    weighted = jnp.sum(probs * delta_prob, axis=-1, keepdims=True)
    delta_score = (probs * (delta_prob - weighted)).astype(jnp.bfloat16)
    delta_query = (
        jnp.einsum("hqk,khd->qhd", delta_score, keyed, preferred_element_type=jnp.float32) * 0.125
    )
    delta_key = (
        jnp.einsum("hqk,qhd->khd", delta_score, query, preferred_element_type=jnp.float32) * 0.125
    )
    stacked = jnp.stack(
        [
            delta_query.reshape(positions, -1),
            delta_key.reshape(positions, -1),
            delta_value.reshape(positions, -1),
        ],
        axis=1,
    )
    return stacked.astype(jnp.bfloat16)


def pick_blocks(source, slot_index, owner_slot, fanout, part_index):
    matches = owner_slot[None, :] == slot_index[:, None]
    present = jnp.any(matches, axis=1).astype(jnp.float32)
    chosen = jnp.sum(
        matches.astype(jnp.int32) * jnp.arange(owner_slot.shape[0], dtype=jnp.int32)[None, :],
        axis=1,
    )
    picked = jnp.take(source, chosen * fanout + part_index, axis=0)
    return picked * present[:, None, None]


def per_device(
    tokens,
    output_grad,
    segment_ids,
    lengths,
    owner_slot,
    slot_weights,
    first_moment,
    second_moment,
    left_stats,
    right_stats,
    left_basis,
    right_basis,
    vector_values,
    vector_first,
    vector_second,
):
    holding = slot_weights.shape[0]
    row_count = tokens.shape[0]
    token_count = tokens.shape[1]
    gathered, vector_half = (
        lax.all_gather(slot_weights.astype(jnp.bfloat16), "dp", axis=0, tiled=True),
        lax.all_gather(vector_values.astype(jnp.bfloat16), "dp", axis=0, tiled=True),
    )
    blocks = jnp.take(gathered, owner_slot, axis=0)
    w_query, w_key, w_value, w_output, w_upward, w_downward = split_blocks(blocks)
    w_joint = jnp.concatenate([w_query, w_key, w_value], axis=1)
    gains = vector_half.astype(jnp.float32).reshape(4, D)
    flat_tokens = tokens.reshape(-1, D)
    projected = jnp.dot(flat_tokens, w_joint, preferred_element_type=jnp.float32).astype(
        jnp.bfloat16
    )
    projected = projected.reshape(row_count, token_count, 3, D)
    heads = lax.all_to_all(projected, "sp", split_axis=3, concat_axis=1, tiled=True)
    context, logsum = lax.map(attend_rows, (heads, segment_ids, lengths))
    context_tok = lax.all_to_all(context, "sp", split_axis=1, concat_axis=2, tiled=True).reshape(
        -1, D
    )
    attended = jnp.dot(context_tok, w_output, preferred_element_type=jnp.float32)
    summed_one = flat_tokens.astype(jnp.float32) + attended
    hidden, norm_one_pull = jax.vjp(layer_norm, summed_one, gains[0], gains[1])
    hidden_half = hidden.astype(jnp.bfloat16)
    upward = jnp.dot(hidden_half, w_upward, preferred_element_type=jnp.float32)
    activated, gelu_pull = jax.vjp(exact_gelu, upward)
    active_half = activated.astype(jnp.bfloat16)
    downward = jnp.dot(active_half, w_downward, preferred_element_type=jnp.float32)
    result, norm_two_pull = jax.vjp(layer_norm, hidden + downward, gains[2], gains[3])
    block_out = result.astype(jnp.bfloat16).reshape(row_count, token_count, D)
    cotangent = output_grad.reshape(-1, D).astype(jnp.float32)
    delta_two, delta_gain_two, delta_shift_two = norm_two_pull(cotangent)
    delta_down = delta_two.astype(jnp.bfloat16)
    grad_down = contract_rows(active_half, delta_down)
    delta_active = contract_cols(delta_down, w_downward)
    (delta_upward,) = gelu_pull(delta_active)
    delta_up = delta_upward.astype(jnp.bfloat16)
    grad_up = contract_rows(hidden_half, delta_up)
    delta_hidden = delta_two + contract_cols(delta_up, w_upward)
    delta_one, delta_gain_one, delta_shift_one = norm_one_pull(delta_hidden)
    delta_attn = delta_one.astype(jnp.bfloat16)
    grad_output = contract_rows(context_tok, delta_attn)
    delta_context = (
        contract_cols(delta_attn, w_output).astype(jnp.bfloat16).reshape(row_count, token_count, D)
    )
    delta_heads = lax.all_to_all(delta_context, "sp", split_axis=2, concat_axis=1, tiled=True)
    delta_projected = lax.map(back_rows, (heads, logsum, delta_heads, segment_ids, lengths))
    delta_joint = lax.all_to_all(
        delta_projected, "sp", split_axis=1, concat_axis=3, tiled=True
    ).reshape(-1, 3 * D)
    grad_joint = contract_rows(flat_tokens, delta_joint)
    input_grad = (delta_one + contract_cols(delta_joint, w_joint)).reshape(
        row_count, token_count, D
    )
    grad_blocks = jnp.concatenate(
        [
            into_blocks(grad_joint[:, :D]),
            into_blocks(grad_joint[:, D : 2 * D]),
            into_blocks(grad_joint[:, 2 * D :]),
            into_blocks(grad_output),
            into_blocks(grad_up),
            into_blocks(grad_down),
        ],
        axis=0,
    )
    vector_grad = jnp.concatenate(
        [delta_gain_one, delta_shift_one, delta_gain_two, delta_shift_two]
    )
    vector_total = lax.psum(vector_grad, ("dp", "sp"))
    piece_len = vector_values.shape[0]
    vector_piece = lax.dynamic_slice_in_dim(
        vector_total, lax.axis_index("dp") * piece_len, piece_len
    )
    slot_index = jnp.arange(holding * lax.axis_size("dp"), dtype=jnp.int32)
    owned = lax.psum_scatter(
        pick_blocks(grad_blocks, slot_index, owner_slot, 1, 0),
        "dp",
        scatter_dimension=0,
        tiled=True,
    )
    owned = lax.psum(owned.astype(jnp.bfloat16), "sp").astype(jnp.float32)
    moment_one, moment_two, left_new, right_new, weights_new = soap_update(
        owned,
        slot_weights,
        first_moment,
        second_moment,
        left_stats,
        right_stats,
        left_basis,
        right_basis,
    )
    vector_one, vector_two, vector_new = adam_update(
        vector_piece, vector_values, vector_first, vector_second
    )
    return (
        block_out,
        input_grad,
        moment_one,
        moment_two,
        left_new,
        right_new,
        weights_new,
        weights_new.astype(jnp.bfloat16),
        vector_one,
        vector_two,
        vector_new,
    )


PITCH = BLK + 16
MESH = pl.DeviceIdType.MESH
NZ = 4


def in_hbm(value):
    return pltpu.with_memory_space_constraint(value, pltpu.HBM)


def place():
    dp = lax.axis_index("dp")
    sp = lax.axis_index("sp")
    return dp // 2, dp % 2, sp // 2, sp % 2


def greet(z, y, x, c):
    barrier = pltpu.get_barrier_semaphore()
    dp = z * 2 + y
    sp = x * 2 + c

    def signal(target):
        pl.semaphore_signal(barrier, 1, device_id=target, device_id_type=MESH)

    for step in range(1, 4):
        signal((dp, (sp + step) % 4))
    signal((z * 2 + 1 - y, sp))

    @pl.when(z < NZ - 1)
    def _():
        signal((dp + 2, sp))

    @pl.when(z > 0)
    def _():
        signal((dp - 2, sp))

    pl.semaphore_wait(barrier, 4 + (z < NZ - 1).astype(jnp.int32) + (z > 0).astype(jnp.int32))


PIECES = {
    "A0": (BLK + 16, False, True),
    "A1": (BLK // 2, False, False),
    "O0": (BLK // 2, True, True),
    "O1": (BLK // 4, True, True),
}
STEPS = (
    ("own", "O1"), ("rows", 1), ("own", "O0"), ("own", "A1"), ("z", "O1", 1, 1, 0), ("z", "O1", 1, -1, 0),
    ("y", "O1", 0, 0), ("z", "O0", 1, 1, 0), ("own", "A0"), ("z", "O0", 2, 1, 0), ("y", "O0", 0, 0),
    ("z", "O0", 1, -1, 0), ("z", "O1", 2, -1, 0), ("y", "O1", 1, -1), ("z", "O1", 3, -1, 0), ("z", "A1", 1, 1, 0),
    ("z", "O1", 2, 1, 0), ("y", "O1", 1, 1), ("z", "O0", 3, 1, 0), ("z", "A0", 1, -1, 0), ("y", "O1", 2, -1),
    ("y", "O0", 1, 1), ("z", "O1", 3, 1, 0), ("y", "O0", 2, 1), ("x", "O0", 3, 1, 0), ("x", "O1", 3, -1, 0),
    ("x", "O1", 1, 1, 0), ("z", "A1", 1, -1, 0), ("x", "O0", 1, -1, 0), ("z", "A0", 1, 1, 0),
    ("x", "O1", 1, -1, 1), ("y", "O1", 3, -1), ("y", "A1", 0, 0), ("z", "A0", 2, 1, 0), ("x", "O0", 2, 1, 0),
    ("y", "O1", 2, 1), ("rows", 0), ("z", "O0", 2, -1, 0), ("x", "O0", 2, 1, 1), ("z", "A0", 2, -1, 0),
    ("x", "O1", 0, 0, 1), ("z", "A1", 1, 1, 1), ("x", "O0", 1, 1, 1), ("z", "O0", 3, -1, 0), ("z", "A1", 1, -1, 1),
    ("y", "O0", 2, -1), ("y", "O0", 3, 1), ("y", "A0", 1, -1), ("x", "O1", 2, 1, 1), ("x", "O1", 3, 1, 0),
    ("x", "O0", 0, 0, 1), ("y", "O0", 3, -1), ("z", "A0", 3, 1, 0), ("y", "O1", 3, 1), ("z", "A0", 3, -1, 0),
    ("x", "O0", 1, 1, 0), ("x", "O1", 3, -1, 1), ("y", "O0", 1, -1), ("z", "A1", 2, -1, 0), ("y", "A0", 0, 0),
    ("x", "O1", 2, -1, 1), ("y", "A0", 2, -1), ("z", "A1", 2, -1, 1), ("x", "O0", 2, -1, 0), ("z", "A1", 3, -1, 0),
    ("x", "O0", 3, -1, 0), ("x", "O0", 3, -1, 1), ("z", "A1", 2, 1, 1), ("y", "A0", 2, 1), ("z", "A1", 2, 1, 0),
    ("x", "O0", 3, 1, 1), ("x", "O1", 2, -1, 0), ("z", "A1", 3, 1, 1), ("x", "O1", 2, 1, 0), ("x", "O0", 2, -1, 1),
    ("y", "A0", 3, -1), ("y", "A0", 1, 1), ("y", "A0", 3, 1), ("x", "O1", 3, 1, 1), ("x", "O1", 1, -1, 0),
    ("x", "O1", 1, 1, 1), ("x", "O0", 1, -1, 1), ("z", "A1", 3, -1, 1), ("z", "A1", 3, 1, 0),
)


def piece_view(ref, name, x_of, c_of, base):
    height = PIECES[name][0]
    if name == "A0":
        return ref.at[base + c_of, pl.ds(0, height)]
    if name == "A1":
        slot, row = base + 2, height * c_of
    elif name == "O0":
        slot, row = base + 4 + x_of, height * c_of
    else:
        slot, row = base + 3, 2 * height * x_of + height * c_of
    return ref.at[slot, pl.ds(pl.multiple_of(row, height), height)]


def gather_kernel(weights, vector, tokens, grads, out, token_row, grad_row, wide, narrow, gain_row, *sems):
    z, y, x, c = place()
    dp = z * 2 + y
    sp = x * 2 + c
    sems = list(sems)
    load_sem, keep_sem, row_send, row_recv, row_keep = [sems.pop(0) for _ in range(5)]
    ways = ("up", "down", "y", "mate", "x", "pass")
    send_sem = {(way, name): sems.pop(0) for way in ways for name in PIECES if PIECES[name][1] or way not in ways[4:]}
    recv_sem = {(way, name): sems.pop(0) for way in ways[2:] for name in PIECES if PIECES[name][1] or way not in ways[4:]}
    targets = {
        "up": (dp + 2, sp), "down": (dp - 2, sp), "y": (z * 2 + 1 - y, sp),
        "x": (dp, (1 - x) * 2 + c), "mate": (dp, x * 2 + 1 - c), "pass": (dp, x * 2 + 1 - c),
    }
    take_gains = pltpu.make_async_copy(vector, gain_row, load_sem.at[6])
    take_gains.start()

    def load_of(i):
        return pltpu.make_async_copy(weights.at[i], wide.at[i], load_sem.at[i])

    for i in (c, 2, 3, 4 + x, 1 - c, 5 - x):
        load_of(i).start()
    keeps = [
        pltpu.make_async_copy(tokens.at[sp], token_row.at[sp], row_keep.at[0]),
        pltpu.make_async_copy(grads.at[sp], grad_row.at[sp], row_keep.at[1]),
    ]
    for keep in keeps:
        keep.start()
    greet(z, y, x, c)
    take_gains.wait()
    gains = jnp.broadcast_to(gain_row[...].reshape(1, BLK), (16, BLK)).astype(jnp.bfloat16)

    def row_copy(which, source, landing, step, arrival):
        peer = (sp + step) % 4
        at = peer if arrival else sp
        return pltpu.make_async_remote_copy(
            src_ref=source.at[peer], dst_ref=landing.at[at],
            send_sem=row_send.at[which, step - 1], recv_sem=row_recv.at[which, at],
            device_id=(dp, peer), device_id_type=MESH,
        )

    def round_block(i):
        load_of(i).wait()
        narrow[i, :BLK, :] = wide[i].astype(jnp.bfloat16)
        narrow[i, BLK:, :] = gains

    for i in (c, 2, 3, 4 + x):
        round_block(i)
    own = [pltpu.make_async_copy(narrow.at[i], out.at[dp * 6 + i], keep_sem.at[i]) for i in range(6)]
    started = []

    def item_of(way, name, holder, x_of, c_of, fresh=False):
        landing = piece_view(out, name, x_of, c_of, holder * 6)
        arrives = way if way in ("mate", "x", "pass") else "y"
        return pltpu.make_async_remote_copy(
            src_ref=piece_view(narrow, name, x_of, c_of, 0) if fresh else landing, dst_ref=landing,
            send_sem=send_sem[way, name].at[holder], recv_sem=recv_sem[arrives, name].at[holder],
            device_id=targets[way], device_id_type=MESH,
        )

    def send(way, name, holder, valid, x_of=x, fresh=False):
        if way in ("up", "down"):
            room = z < NZ - 1 if way == "up" else z > 0
            valid = room if valid is None else valid & room
        item = item_of(way, name, holder, x_of, c, fresh)
        if valid is None:
            item.start()
        else:
            pl.when(valid)(item.start)
        started.append((item, valid))

    def arrive(way, name, holder, valid, x_of, c_of):
        item = item_of(way, name, holder, x_of, c_of)
        if valid is None:
            item.wait_recv()
        else:
            pl.when(valid)(item.wait_recv)

    def origin_of(sign, far):
        origin = z + sign * far
        if far == 0:
            return origin, None
        return origin, ((origin >= 0) if sign < 0 else (origin <= NZ - 1))

    for step in STEPS:
        kind, name = step[0], step[1]
        if kind == "own":
            for way in ("up", "down", "y"):
                send(way, name, dp, None, fresh=True)
        elif kind == "rows":
            source, landing = ((tokens, token_row), (grads, grad_row))[name]
            for hop in (2, 3, 1):
                row_copy(name, source, landing, hop, False).start()
        else:
            origin, inside = origin_of(step[3], step[2])
            if kind == "x":
                holder = origin * 2 + (y if step[4] == 0 else 1 - y)
                arrive("x", name, holder, inside, 1 - x, c)
                send("pass", name, holder, inside, 1 - x)
                continue
            holder = origin * 2 + (y if kind == "z" and step[4] == 0 else 1 - y)
            arrive("y", name, holder, inside, x, c)
            if kind == "z":
                if step[2] < NZ - 1:
                    send("up" if step[3] < 0 else "down", name, holder, inside)
                if PIECES[name][2] and step[4] == 0:
                    send("y", name, holder, inside)
            elif not PIECES[name][2]:
                send("up", name, holder, inside)
                send("down", name, holder, inside)
            if PIECES[name][1]:
                send("x", name, holder, inside)
            send("mate", name, holder, inside)
        if kind == "own" and name == "A0":
            for i in (1 - c, 5 - x):
                round_block(i)
            for item in own:
                item.start()

    for far in range(NZ):
        for sign in (0,) if far == 0 else (-1, 1):
            origin, inside = origin_of(sign, far)
            for column in (1,) if far == 0 else (0, 1):
                holder = origin * 2 + (y if column == 0 else 1 - y)
                for name in PIECES:
                    arrive("mate", name, holder, inside, x, 1 - c)
                    if PIECES[name][1]:
                        arrive("pass", name, holder, inside, 1 - x, 1 - c)
    for hop in (2, 3, 1):
        for which, source, landing in ((0, tokens, token_row), (1, grads, grad_row)):
            row_copy(which, source, landing, hop, True).wait_recv()
            row_copy(which, source, landing, hop, False).wait_send()
    for item, valid in started:
        if valid is None:
            item.wait_send()
        else:
            pl.when(valid)(item.wait_send)
    for item in own + keeps:
        item.wait()


def gather_all(weights, vector, tokens, grads):
    anywhere = pl.BlockSpec(memory_space=pl.ANY)
    dma = pltpu.SemaphoreType.DMA
    carried = sum(1 for name in PIECES if PIECES[name][1])
    flows = (4 * len(PIECES) + 2 * carried) + (2 * len(PIECES) + 2 * carried)
    return pl.pallas_call(
        gather_kernel,
        name="gather_all",
        out_shape=[
            pltpu.HBM((48, PITCH, BLK), jnp.bfloat16),
            pltpu.HBM(tokens.shape, jnp.bfloat16),
            pltpu.HBM(grads.shape, jnp.bfloat16),
        ],
        in_specs=[anywhere] * 4,
        out_specs=[anywhere] * 3,
        scratch_shapes=[
            pltpu.VMEM((6, BLK, BLK), jnp.float32),
            pltpu.VMEM((6, PITCH, BLK), jnp.bfloat16),
            pltpu.VMEM((BLK,), jnp.float32),
            dma((7,)), dma((6,)), dma((2, 3)), dma((2, 4)), dma((2,)),
        ]
        + [dma((8,))] * flows,
        compiler_params=pltpu.CompilerParams(
            collective_id=0, has_side_effects=True, vmem_limit_bytes=24 << 20
        ),
    )(in_hbm(weights), in_hbm(vector), in_hbm(tokens), in_hbm(grads))


ROW = 512
PAIR = 128
SPAN = 384
EPS = 1e-06


def gelu_of(u):
    bell = jnp.exp(-0.5 * u * u)
    t = 1.0 / (1.0 + (0.3275911 / math.sqrt(2.0)) * jnp.abs(u))
    tail = 0.5 * 1.061405429
    for term in (-1.453152027, 1.421413741, -0.284496736, 0.254829592):
        tail = tail * t + 0.5 * term
    tail = tail * t * bell
    below = jnp.where(u >= 0.0, 1.0 - tail, tail)
    return (u * below).astype(jnp.bfloat16), below + u * (bell * (1.0 / math.sqrt(2.0 * math.pi)))


def dot_nn(a, b):
    return lax.dot_general(a, b, (((1,), (0,)), ((), ())), preferred_element_type=jnp.float32)


def dot_nt(a, b):
    return lax.dot_general(a, b, (((1,), (1,)), ((), ())), preferred_element_type=jnp.float32)


def dot_tn(a, b):
    return lax.dot_general(a, b, (((0,), (0,)), ((), ())), preferred_element_type=jnp.float32)


def layer_kernel(
    owner, weights, tokens, dy_ref, segments, grads, block_out, input_half,
    wqkv, wo, w1, w2, gains, qkv, probs, shares, held, context, hidden, hidden16, norm1, act, slope, dz, dz16,
    dqkv, dup, stage, flipped, flipped_hidden, ups, vecs, spread, w_sem, g_sem, v_sem,
):
    half = jnp.bfloat16
    sp = lax.axis_index("sp")

    def weight_copies():
        copies = []
        for which, ref in enumerate((wqkv.at[0], wqkv.at[1], wqkv.at[2], wo)):
            for r in range(2):
                for q in range(2):
                    copies.append((which * 4 + r * 2 + q, ref, r, q))
        for r in range(2):
            for q in range(8):
                copies.append((16 + r * 8 + q, w1.at[q // 2], r, q % 2))
        for r in range(8):
            for q in range(2):
                copies.append((32 + r * 2 + q, w2.at[r // 2], r % 2, q))
        return [
            pltpu.make_async_copy(
                weights.at[owner[b], pl.ds(0, BLK)],
                ref.at[pl.ds(r * BLK, BLK), pl.ds(q * BLK, BLK)],
                w_sem.at[b],
            )
            for b, ref, r, q in copies
        ]

    copies = weight_copies()
    gain_copies = [
        pltpu.make_async_copy(
            weights.at[6 * d, pl.ds(BLK, 16)], gains.at[d // 2, :, pl.ds((d % 2) * BLK, BLK)], g_sem.at[d]
        )
        for d in range(8)
    ]
    for item in copies[:16] + gain_copies + copies[16:]:
        item.start()

    seg_row = segments[pl.ds(sp, 1), :].astype(jnp.float32)
    spread[...] = jnp.transpose(jnp.broadcast_to(seg_row, (PAIR, ROW)))

    for item in copies[:12]:
        item.wait()
    x = tokens[...]
    flipped[...] = jnp.transpose(x)
    for part in range(3):
        block = dot_nn(x, wqkv[part])
        if part == 0:
            block = block * 0.125
        block = block.astype(half)
        for p in range(6):
            qkv[part * 6 + p] = block[:, p * PAIR : (p + 1) * PAIR]

    lane = lax.broadcasted_iota(jnp.int32, (1, PAIR), 1)
    lows = (lane < 64, lane >= 64)

    def visible(part):
        keys = segments[pl.ds(sp, 1), pl.ds(part * PAIR, SPAN)].astype(jnp.float32)
        own = spread[pl.ds(part * 256, 256), pl.ds(0, 1)]
        return own == keys

    def attend(p, carry):
        q2, k2, v2 = qkv[p], qkv[6 + p], qkv[12 + p]
        for part in range(2):
            mask = visible(part)
            qs = q2[part * 256 : part * 256 + 256]
            ks = k2[part * PAIR : part * PAIR + SPAN]
            vs = v2[part * PAIR : part * PAIR + SPAN]
            outs = []
            for h in range(2):
                scores = dot_nt(jnp.where(lows[h], qs, jnp.zeros_like(qs)), ks)
                scores = jnp.where(mask, scores, -1e30)
                raised = jnp.exp(scores - jnp.max(scores, axis=1, keepdims=True)).astype(half)
                probs[p, 2 * part + h] = raised
                outs.append(dot_nn(raised, jnp.where(lows[h], vs, jnp.ones_like(vs))))
            inverse = 1.0 / pltpu.roll(jnp.where(lows[0], outs[1], outs[0]), 64, 1)
            shares[p, pl.ds(part * 256, 256)] = inverse
            context[p, pl.ds(part * 256, 256)] = (jnp.where(lows[0], outs[0], outs[1]) * inverse).astype(half)
        return carry

    lax.fori_loop(0, 6, attend, 0, unroll=3)

    for item in copies[12:16] + gain_copies:
        item.wait()
    joined = jnp.concatenate([context[p] for p in range(6)], axis=1)

    def gain(k):
        return gains[k, pl.ds(0, 1), :].astype(jnp.float32)

    def normalise(z):
        centre = jnp.mean(z, axis=1, keepdims=True)
        z = z - centre
        inverse = lax.rsqrt(jnp.mean(z * z, axis=1, keepdims=True) + EPS)
        return z * inverse, inverse

    dz[...] = dot_nn(joined, wo[...])

    def norm_one(t, carry):
        rows = pl.ds(pl.multiple_of(t * 128, 128), 128)
        hat, inverse = normalise(tokens[rows, :].astype(jnp.float32) + dz[rows, :])
        norm1[rows, :] = hat
        spread[rows, :] = jnp.where(lane == 1, inverse, spread[rows, :])
        value = hat * gain(0) + gain(1)
        hidden[rows, :] = value
        hidden16[rows, :] = value.astype(half)
        return carry

    lax.fori_loop(0, 4, norm_one, 0)
    for item in copies[16:]:
        item.wait()

    flipped_hidden[...] = jnp.transpose(hidden16[...])
    ups[0] = dot_nn(hidden16[...], w1[0])
    for j in range(5):
        if j < 3:
            ups[(j + 1) % 2] = dot_nn(hidden16[...], w1[j + 1])
        if j < 4:
            act[j], slope[j] = gelu_of(ups[j % 2])
        if j > 0:
            hidden[...] += dot_nn(act[j - 1], w2[j - 1])

    vecs[...] = jnp.zeros_like(vecs)

    def fold(value):
        return jnp.sum(value.reshape(-1, 8, D), axis=0)

    def norm_back(hat, inverse, delta, gain_row):
        e = delta * gain_row
        return (
            e - jnp.mean(e, axis=1, keepdims=True) - hat * jnp.mean(e * hat, axis=1, keepdims=True)
        ) * inverse

    def norm_two(t, carry):
        rows = pl.ds(pl.multiple_of(t * 128, 128), 128)
        hat, inverse = normalise(hidden[rows, :])
        block_out[rows, :] = (hat * gain(2) + gain(3)).astype(half)
        delta = dy_ref[rows, :].astype(jnp.float32)
        vecs[2] += fold(delta * hat)
        vecs[3] += fold(delta)
        back = norm_back(hat, inverse, delta, gain(2))
        dz[rows, :] = back
        dz16[rows, :] = back.astype(half)
        return carry

    lax.fori_loop(0, 4, norm_two, 0)

    def out_copy(slot, b, r, q):
        return pltpu.make_async_copy(
            stage.at[slot, pl.ds(r * BLK, BLK), pl.ds(q * BLK, BLK)],
            grads.at[owner[b], pl.ds(0, BLK)],
            v_sem.at[slot, r * 2 + q],
        )

    def flush(slot, blocks):
        for r in range(2):
            for q in range(2):
                out_copy(slot, blocks(r, q), r, q).start()

    def drain(slot):
        for r in range(2):
            for q in range(2):
                out_copy(slot, 0, r, q).wait()

    def backward(pair, carry):
        @pl.when(pair > 0)
        def _():
            for slot in range(4):
                drain(slot)

        ddown = dz16[...]
        for k in range(2):
            j = 2 * pair + k
            delta = (dot_nt(ddown, w2[j]) * slope[j]).astype(half)
            stage[2 * k] = dot_tn(act[j], ddown).astype(half)
            stage[2 * k + 1] = dot_nn(flipped_hidden[...], delta).astype(half)
            dz[...] += dot_nt(delta, w1[j])
        for k in range(2):
            j = 2 * pair + k
            flush(2 * k, lambda r, q: 32 + (2 * j + r) * 2 + q)
            flush(2 * k + 1, lambda r, q: 16 + r * 8 + 2 * j + q)
        return carry

    lax.fori_loop(0, 2, backward, 0)

    def norm_one_back(t, carry):
        rows = pl.ds(pl.multiple_of(t * 128, 128), 128)
        hat = norm1[rows, :]
        delta = dz[rows, :]
        vecs[0] += fold(delta * hat)
        vecs[1] += fold(delta)
        back = norm_back(hat, spread[rows, pl.ds(1, 1)], delta, gain(0))
        dz[rows, :] = back
        dz16[rows, :] = back.astype(half)
        return carry

    lax.fori_loop(0, 4, norm_one_back, 0)

    for slot in range(4):
        drain(slot)
    dattn = dz16[...]
    stage[0] = dot_tn(joined, dattn).astype(half)
    flush(0, lambda r, q: 12 + r * 2 + q)
    dcontext = dot_nt(dattn, wo[...]).astype(half)
    for p in range(6):
        held[p] = context[p]
        context[p] = dcontext[:, p * PAIR : (p + 1) * PAIR]

    def attend_back(p, carry):
        q2, k2, v2, d2 = qkv[p], qkv[6 + p], qkv[12 + p], context[p]
        dup[...] = jnp.zeros_like(dup)
        for part in range(2):
            window = pl.ds(part * PAIR, SPAN)
            qs = q2[part * 256 : part * 256 + 256]
            ds = d2[part * 256 : part * 256 + 256]
            ks = k2[part * PAIR : part * PAIR + SPAN]
            vs = v2[part * PAIR : part * PAIR + SPAN]
            dvs, dqs, dks = [], [], []
            share = shares[p, pl.ds(part * 256, 256)]
            scaled = (ds.astype(jnp.float32) * share).astype(half)
            weight = scaled.astype(jnp.float32) * held[p, pl.ds(part * 256, 256)].astype(jnp.float32)
            for h in range(2):
                raised = probs[p, 2 * part + h]
                dprob = dot_nt(jnp.where(lows[h], scaled, jnp.zeros_like(scaled)), vs)
                centre = jnp.sum(jnp.where(lows[h], weight, 0.0), axis=1, keepdims=True)
                dscore = (raised.astype(jnp.float32) * (dprob - centre)).astype(half)
                dvs.append(dot_tn(raised, scaled))
                dqs.append(dot_nn(dscore, ks))
                dks.append(dot_tn(dscore, qs))
            dqkv[p, pl.ds(part * 256, 256)] = (
                jnp.where(lows[0], dqs[0], dqs[1]) * 0.125
            ).astype(half)
            dup[0, window] += jnp.where(lows[0], dks[0], dks[1])
            dup[1, window] += jnp.where(lows[0], dvs[0], dvs[1])
        dqkv[6 + p] = dup[0].astype(half)
        dqkv[12 + p] = dup[1].astype(half)
        return carry

    lax.fori_loop(0, 6, attend_back, 0, unroll=3)

    for part in range(3):
        delta = jnp.concatenate([dqkv[part * 6 + p] for p in range(6)], axis=1)
        stage[1 + part] = dot_nn(flipped[...], delta).astype(half)
        flush(1 + part, lambda r, q: part * 4 + r * 2 + q)
        dz[...] += dot_nt(delta, wqkv[part])

    input_half[...] = dz[...].astype(half)
    for k in range(4):
        row = jnp.sum(vecs[k], axis=0, keepdims=True)
        vecs16 = jnp.broadcast_to(row, (16, D)).astype(half)
        gains[k] = vecs16
    for k in range(4):
        for q in range(2):
            for s in range(2):
                pltpu.make_async_copy(
                    gains.at[k, :, pl.ds(q * BLK, BLK)],
                    grads.at[6 * (2 * k + q) + s, pl.ds(BLK, 16)],
                    w_sem.at[(2 * k + q) * 2 + s],
                ).start()
    for k in range(4):
        for q in range(2):
            for s in range(2):
                pltpu.make_async_copy(
                    gains.at[k, :, pl.ds(q * BLK, BLK)],
                    grads.at[6 * (2 * k + q) + s, pl.ds(BLK, 16)],
                    w_sem.at[(2 * k + q) * 2 + s],
                ).wait()
    for slot in range(4):
        drain(slot)


def run_layer(owner_slot, gathered, token_row, grad_row, segment_ids):
    half, full = jnp.bfloat16, jnp.float32
    anywhere = pl.BlockSpec(memory_space=pltpu.HBM)
    vmem = pl.BlockSpec(memory_space=pltpu.VMEM)
    dma = pltpu.SemaphoreType.DMA
    return pl.pallas_call(
        layer_kernel,
        name="run_layer",
        out_shape=[
            jax.ShapeDtypeStruct((48, PITCH, BLK), half),
            jax.ShapeDtypeStruct((ROW, D), half),
            jax.ShapeDtypeStruct((ROW, D), half),
        ],
        in_specs=[pl.BlockSpec(memory_space=pltpu.SMEM), anywhere, vmem, vmem, vmem],
        out_specs=[anywhere, vmem, vmem],
        scratch_shapes=[
            pltpu.VMEM((3, D, D), half),
            pltpu.VMEM((D, D), half),
            pltpu.VMEM((4, D, D), half),
            pltpu.VMEM((4, D, D), half),
            pltpu.VMEM((4, 16, D), half),
            pltpu.VMEM((18, ROW, PAIR), half),
            pltpu.VMEM((6, 4, 256, SPAN), half),
            pltpu.VMEM((6, ROW, PAIR), full),
            pltpu.VMEM((6, ROW, PAIR), half),
            pltpu.VMEM((6, ROW, PAIR), half),
            pltpu.VMEM((ROW, D), full),
            pltpu.VMEM((ROW, D), half),
            pltpu.VMEM((ROW, D), full),
            pltpu.VMEM((4, ROW, D), half),
            pltpu.VMEM((4, ROW, D), full),
            pltpu.VMEM((ROW, D), full),
            pltpu.VMEM((ROW, D), half),
            pltpu.VMEM((18, ROW, PAIR), half),
            pltpu.VMEM((2, ROW, PAIR), full),
            pltpu.VMEM((4, D, D), half),
            pltpu.VMEM((D, ROW), half),
            pltpu.VMEM((D, ROW), half),
            pltpu.VMEM((2, ROW, D), full),
            pltpu.VMEM((4, 8, D), full),
            pltpu.VMEM((ROW, PAIR), full),
            dma((48,)),
            dma((8,)),
            dma((4, 4)),
        ],
        compiler_params=pltpu.CompilerParams(vmem_limit_bytes=58 << 20),
    )(owner_slot, gathered, token_row, grad_row, segment_ids)


BLANK = BLK + 16
HALF = BLK // 2
STREAMS = {
    "A0": (BLANK, 0, True, True),
    "A1": (HALF, 0, True, True),
    "A2": (HALF, HALF, True, False),
    "O": (HALF, 0, False, True),
    "XO": (HALF, 0, False, True),
}
TASKS = (
    ("Y", "A1", 3), ("Z", "A2", 0, 1), ("Y", "A0", 0), ("X", "O", 0, 1), ("Z", "A2", 0, 0), ("X", "O", 2, 1),
    ("X", "O", 1, 0), ("Y", "A0", 1), ("Z", "A2", 1, 1), ("Y", "A0", 2), ("Z", "A2", 2, 0), ("X", "O", 0, 0),
    ("X", "O", 3, 0), ("Y", "O", 0), ("C", "A0", 0), ("Z", "A2", 2, 1), ("X", "O", 1, 1), ("Y", "O", 2),
    ("Y", "A0", 3), ("X", "O", 3, 1), ("X", "O", 2, 0), ("C", "A0", 1), ("R", 1), ("Y", "O", 1), ("Y", "A1", 0),
    ("C", "A1", 3), ("Z", "A2", 3, 1), ("Y", "O", 3), ("C", "O", 0), ("R", 0), ("C", "A0", 2), ("Y", "A1", 1),
    ("C", "A0", 3), ("C", "O", 2), ("Y", "A1", 2), ("C", "O", 1), ("F", "A0"), ("F1", "A2"), ("C", "A1", 0),
    ("C", "O", 3), ("Z", "A2", 3, 0), ("F", "O"), ("Z", "A2", 1, 0), ("C", "A1", 1), ("C", "A1", 2), ("F", "A2"),
    ("L", "O"), ("F", "A1"), ("L", "A0"), ("L", "A2"), ("L", "A1"),
)


def reduce_kernel(grads, rows_a, rows_b, total, land_a, land_b, *scratch):
    z, y, x, c = place()
    dp = z * 2 + y
    sp = x * 2 + c
    names = list(STREAMS)
    moving = [name for name in names if name != "XO"]
    planes = [name for name in moving if STREAMS[name][2]]
    scratch = list(scratch)

    def take(keys):
        return {key: scratch.pop(0) for key in keys}

    mine, core, side, line, last = take(names), take(names), take(moving), take(moving), take(planes)
    cross, = take(["cross"]).values()
    load_sem, core_send, core_recv = take(names), take(names), take(names)
    y_send, y_recv, z_send, z_recv = take(moving), take(moving), take(moving), take(moving)
    x_send, x_recv, last_send, last_recv, give_send, give_recv, keep_sem, row_send, row_recv, row_keep = scratch
    high = z // 2
    order = (3 - 3 * high, 2 - high, 1 - z + 4 * high, z)
    twin = (dp, (1 - x) * 2 + c)
    mate = (dp, x * 2 + 1 - c)
    beside = (z * 2 + 1 - y, sp)
    inner = (z > 0) & (z < NZ - 1)

    def view(ref, name, dest, core_of):
        base = dest * 6
        if name == "A0":
            return ref.at[base + core_of, pl.ds(0, BLANK)]
        if name in ("A1", "A2"):
            return ref.at[base + 2 + core_of, pl.ds(STREAMS[name][1], HALF)]
        slot = base + (4 + x if name == "O" else 5 - x)
        return ref.at[slot, pl.ds(pl.multiple_of(core_of * HALF, HALF), HALF)]

    def remote(src, dst, send, recv, target):
        return pltpu.make_async_remote_copy(
            src_ref=src, dst_ref=dst, send_sem=send, recv_sem=recv,
            device_id=target, device_id_type=MESH,
        )

    def load(name, dest):
        return pltpu.make_async_copy(view(grads, name, dest, c), mine[name].at[dest], load_sem[name].at[dest])

    def to_mate(name, dest):
        return remote(
            view(grads, name, dest, 1 - c), core[name].at[dest],
            core_send[name].at[dest], core_recv[name].at[dest], mate,
        )

    def to_twin(dest):
        return remote(mine["XO"].at[dest], cross.at[dest], x_send.at[dest], x_recv.at[dest], twin)

    def to_side(name, goal):
        at = goal if STREAMS[name][3] else 0
        return remote(
            mine[name].at[goal * 2 + 1 - y], side[name].at[at],
            y_send[name].at[at], y_recv[name].at[at], beside,
        )

    def row_copy(which, source, landing, step, arrival):
        peer = (sp + step) % 4
        at = peer if arrival else sp
        return remote(
            source.at[peer], landing.at[at],
            row_send.at[which, step - 1], row_recv.at[which, at], (dp, peer),
        )

    def column_of(flag):
        return y if flag == 0 else 1 - y

    def dest_of(task):
        if task[0] in ("X", "Z"):
            return order[task[2]] * 2 + column_of(task[3])
        return order[task[2]] * 2 + (1 - y if task[0] == "Y" else y)

    sequence = [
        ("XO" if task[0] == "X" else task[1], dest_of(task)) for task in TASKS if task[0] in ("X", "Y", "C", "Z")
    ]
    for name, dest in sequence:
        load(name, dest).start()
    keeps = [
        pltpu.make_async_copy(rows_a.at[sp], land_a.at[sp], row_keep.at[0]),
        pltpu.make_async_copy(rows_b.at[sp], land_b.at[sp], row_keep.at[1]),
    ]
    for keep in keeps:
        keep.start()
    greet(z, y, x, c)
    for name, dest in sequence:
        to_mate(name, dest).start()

    def merge(name, dest):
        load(name, dest).wait()
        to_mate(name, dest).wait_recv()
        value = mine[name][dest] + core[name][dest]
        if name == "O":
            to_twin(dest).wait_recv()
            value = value + cross[dest]
        mine[name][dest] = value

    def hop(name, goal, column, way, target):
        lane = goal if STREAMS[name][3] else goal * 2 + column
        return remote(
            mine[name].at[goal * 2 + column], line[name].at[way, lane],
            z_send[name].at[lane], z_recv[name].at[way, lane], target,
        )

    def along(name, goal, column):
        dest = goal * 2 + column
        upward = (goal > z).astype(jnp.int32)
        step = 2 * upward - 1
        way = 1 - upward
        item = hop(name, goal, column, way, (dp + 2 * step, sp))
        lane = goal if STREAMS[name][3] else dest

        @pl.when(inner)
        def _():
            item.wait_recv()
            mine[name][dest] = mine[name][dest] + line[name][way, lane]

        item.start()

    def settle(name, column):
        dest = z * 2 + column
        lane = z if STREAMS[name][3] else dest
        for way, valid, step in ((0, z > 0, 1), (1, z < NZ - 1, -1)):
            @pl.when(valid)
            def _():
                hop(name, z, column, way, (dp - 2 * step, sp)).wait_recv()
                mine[name][dest] = mine[name][dest] + line[name][way, lane]

    def swap_last(name):
        at = planes.index(name)
        return remote(mine[name].at[dp], last[name], last_send.at[at], last_recv.at[at], twin)

    def place_of(name, core_of):
        return view(total, name, 0, core_of)

    gift_at = {name: at for at, name in enumerate(planes + ["O", "twin", "XO"])}

    def give(name, key, target, source, core_of):
        at = gift_at[key]
        return remote(source, place_of(name, core_of), give_send.at[at], give_recv.at[at], target)

    gifts, kept = [], []

    def hand_on(name, key, target, source):
        item = give(name, key, target, source, c)
        item.start()
        gifts.append(item)

    def keep_here(name, source):
        item = pltpu.make_async_copy(source, place_of(name, c), keep_sem.at[gift_at[name]])
        item.start()
        kept.append(item)

    for task in TASKS:
        kind, name = task[0], task[1]
        if kind == "R":
            source, landing = ((rows_a, land_a), (rows_b, land_b))[name]
            for step in (2, 3, 1):
                row_copy(name, source, landing, step, False).start()
        elif kind == "X":
            merge("XO", dest_of(task))
            to_twin(dest_of(task)).start()
        elif kind == "Y":
            merge(name, dest_of(task))
            to_side(name, order[task[2]]).start()
        elif kind == "C":
            dest = dest_of(task)
            merge(name, dest)
            to_side(name, order[task[2]]).wait_recv()
            mine[name][dest] = mine[name][dest] + side[name][order[task[2]]]
            if task[2] < 3:
                along(name, order[task[2]], y)
        elif kind == "Z":
            merge(name, dest_of(task))
            if task[2] < 3:
                along(name, order[task[2]], column_of(task[3]))
        elif kind == "F1":
            settle(name, 1 - y)
            to_side(name, z).start()
        elif kind == "F":
            settle(name, y)
            if not STREAMS[name][3]:
                to_side(name, z).wait_recv()
                mine[name][dp] = mine[name][dp] + side[name][0]
            if name in planes:
                swap_last(name).start()
            else:
                hand_on(name, "twin", twin, mine[name].at[dp])
                hand_on(name, "O", mate, mine[name].at[dp])
                keep_here(name, mine[name].at[dp])
        elif kind == "L":
            if name in planes:
                swap_last(name).wait_recv()
                core[name][dp] = mine[name][dp] + last[name][...]
                hand_on(name, name, mate, core[name].at[dp])
                keep_here(name, core[name].at[dp])
            else:
                give("XO", "twin", twin, place_of("XO", c), c).wait_recv()
                hand_on("XO", "XO", mate, place_of("XO", c))

    for name in planes + ["O", "XO"]:
        give(name, name, mate, place_of(name, 1 - c), 1 - c).wait_recv()
    for step in (2, 3, 1):
        for which, source, landing in ((0, rows_a, land_a), (1, rows_b, land_b)):
            row_copy(which, source, landing, step, True).wait_recv()
            row_copy(which, source, landing, step, False).wait_send()
    for name, dest in sequence:
        to_mate(name, dest).wait_send()
    for i in range(4):
        for column in (0, 1):
            to_twin(order[i] * 2 + column).wait_send()
        for name in moving:
            if STREAMS[name][3]:
                to_side(name, order[i]).wait_send()
                if i < 3:
                    hop(name, order[i], y, 0, twin).wait_send()
            elif i < 3:
                for column in (0, 1):
                    hop(name, order[i], column, 0, twin).wait_send()
            else:
                to_side(name, z).wait_send()
    for name in planes:
        swap_last(name).wait_send()
    for item in gifts:
        item.wait_send()
    for item in kept + keeps:
        item.wait()


def reduce_all(grads, rows_a, rows_b):
    anywhere = pl.BlockSpec(memory_space=pl.ANY)
    half = jnp.bfloat16
    dma = pltpu.SemaphoreType.DMA
    moving = [name for name in STREAMS if name != "XO"]
    planes = [name for name in moving if STREAMS[name][2]]

    def buffers(shapes):
        return [pltpu.VMEM((*lead, STREAMS[name][0], BLK), half) for name, lead in shapes]

    first = {name: STREAMS[name][3] for name in moving}
    return pl.pallas_call(
        reduce_kernel,
        name="reduce_all",
        out_shape=[
            jax.ShapeDtypeStruct((6, PITCH, BLK), half),
            pltpu.HBM(rows_a.shape, half),
            pltpu.HBM(rows_b.shape, half),
        ],
        in_specs=[anywhere] * 3,
        out_specs=[anywhere] * 3,
        scratch_shapes=buffers([(name, (8,)) for name in STREAMS] * 2)
        + buffers([(name, (4 if first[name] else 1,)) for name in moving])
        + buffers([(name, (2, 4 if first[name] else 8)) for name in moving])
        + buffers([(name, ()) for name in planes])
        + buffers([("O", (8,))])
        + [dma((8,))] * (3 * len(STREAMS))
        + [dma((4 if first[name] else 1,)) for name in moving] * 2
        + [dma((4 if first[name] else 8,)) for name in moving]
        + [dma((2, 4 if first[name] else 8)) for name in moving]
        + [
            dma((8,)), dma((8,)), dma((len(planes),)), dma((len(planes),)), dma((len(planes) + 3,)),
            dma((len(planes) + 3,)), dma((len(planes) + 1,)), dma((2, 3)), dma((2, 4)), dma((2,)),
        ],
        compiler_params=pltpu.CompilerParams(
            collective_id=1, has_side_effects=True, vmem_limit_bytes=28 << 20
        ),
    )(in_hbm(grads), in_hbm(rows_a), in_hbm(rows_b))


CORRECT = 1.0 - 0.5**STEP
GROUP = 2


def update_kernel(
    total, weights, first, second, left_old, right_old, left_rot, right_rot, vec, vec_first, vec_second, land_a,
    land_b, moment_one, moment_two, left_new, right_new, weights_new, weights_half, vector_one, vector_two, vector_new,
    rows_a, rows_b, held, narrow, wide, stage, stage_half, left, right, out_sem, in_sem, sems,
):
    half = jnp.bfloat16
    take_a = pltpu.make_async_copy(land_a, held, sems.at[0])
    give_a = pltpu.make_async_copy(held, rows_a, sems.at[3])
    take_b = pltpu.make_async_copy(land_b, narrow, sems.at[1])
    give_b = pltpu.make_async_copy(wide, rows_b, sems.at[2])
    count = weights.shape[0]

    def state_of(i):
        return [
            pltpu.make_async_copy(old.at[i], now.at[i], in_sem.at[i, k])
            for k, (old, now) in enumerate(((left_old, left), (right_old, right)))
        ]

    for i in range(count):
        for item in state_of(i):
            item.start()
    take_b.start()
    take_a.start()
    slope = total[0, pl.ds(BLK, 1), :].astype(jnp.float32).reshape(BLK)
    vec_one = 0.5 * vec_first[...] + 0.5 * slope
    vec_two = 0.5 * vec_second[...] + 0.5 * slope * slope
    vector_one[...] = vec_one
    vector_two[...] = vec_two
    vector_new[...] = vec[...] - rate_vector * (
        (vec_one / CORRECT) / (jnp.sqrt(vec_two / CORRECT) + 1e-08)
    )
    targets = (left_new, right_new, moment_one, moment_two, weights_new)

    def outputs(i):
        copies = [
            pltpu.make_async_copy(stage.at[k, i], target.at[i], out_sem.at[i, k])
            for k, target in enumerate(targets)
        ]
        return copies + [pltpu.make_async_copy(stage_half.at[i], weights_half.at[i], out_sem.at[i, 5])]

    def blocks(pair, carry):
        for i in [pair * GROUP + k for k in range(GROUP)]:
            for item in state_of(i):
                item.wait()
        for i in [pair * GROUP + k for k in range(GROUP)]:
            grad = total[i, :BLK, :]
            rot_l = left_rot[i].astype(half)
            rot_r = right_rot[i].astype(half)
            turned = dot_nn(dot_tn(rot_l, grad).astype(half), rot_r)
            stage[0, i] = 0.95 * left[i] + 0.05 * dot_nt(grad, grad)
            one = 0.5 * first[i] + 0.5 * turned
            two = 0.5 * second[i] + 0.5 * turned * turned
            stage[2, i] = one
            stage[3, i] = two
            spread = two * (1.0 / CORRECT)
            ratio = (one * (1.0 / CORRECT)) / (spread * lax.rsqrt(spread) + 1e-08)
            stage[1, i] = 0.95 * right[i] + 0.05 * dot_tn(grad, grad)
            stepped = dot_nt(dot_nn(rot_l, ratio.astype(half)).astype(half), rot_r)
            fresh = weights[i] - rate_matrix * stepped
            stage[4, i] = fresh
            stage_half[i] = fresh.astype(half)
        for i in [pair * GROUP + k for k in range(GROUP)]:
            for item in outputs(i):
                item.start()

        @pl.when(pair == 0)
        def _():
            take_a.wait()
            give_a.start()
            take_b.wait()
            for r in range(narrow.shape[0]):
                wide[r] = narrow[r].astype(jnp.float32)
            give_b.start()

        return carry

    lax.fori_loop(0, weights.shape[0] // GROUP, blocks, 0)
    for i in range(weights.shape[0]):
        for item in outputs(i):
            item.wait()
    give_a.wait()
    give_b.wait()


def update_all(
    total, weights, first, second, left, right, left_rot, right_rot, vec, vec_first, vec_second, land_a, land_b
):
    full = jnp.float32
    vmem = pl.BlockSpec(memory_space=pltpu.VMEM)
    anywhere = pl.BlockSpec(memory_space=pl.ANY)
    vector = jax.ShapeDtypeStruct((BLK,), full)
    matrix = pltpu.HBM(weights.shape, full)
    return pl.pallas_call(
        update_kernel,
        name="update_all",
        out_shape=[matrix] * 5 + [pltpu.HBM(weights.shape, jnp.bfloat16)] + [vector] * 3
        + [pltpu.HBM(land_a.shape, jnp.bfloat16), pltpu.HBM(land_b.shape, full)],
        in_specs=[vmem] * 4 + [anywhere] * 2 + [vmem] * 5 + [anywhere] * 2,
        out_specs=[anywhere] * 6 + [vmem] * 3 + [anywhere] * 2,
        scratch_shapes=[
            pltpu.VMEM(land_a.shape, jnp.bfloat16),
            pltpu.VMEM(land_b.shape, jnp.bfloat16),
            pltpu.VMEM(land_b.shape, full),
            pltpu.VMEM((5, *weights.shape), full),
            pltpu.VMEM(weights.shape, jnp.bfloat16),
            pltpu.VMEM(weights.shape, full),
            pltpu.VMEM(weights.shape, full),
            pltpu.SemaphoreType.DMA((weights.shape[0], 6)),
            pltpu.SemaphoreType.DMA((weights.shape[0], 2)),
            pltpu.SemaphoreType.DMA((4,)),
        ],
        compiler_params=pltpu.CompilerParams(vmem_limit_bytes=38 << 20),
    )(
        total, weights, first, second, in_hbm(left), in_hbm(right), left_rot, right_rot,
        vec, vec_first, vec_second, in_hbm(land_a), in_hbm(land_b),
    )


def fast_device(
    tokens, output_grad, segment_ids, lengths, owner_slot, slot_weights, first_moment, second_moment,
    left_stats, right_stats, left_basis, right_basis, vector_values, vector_first, vector_second,
):
    gathered, token_row, grad_row = gather_all(slot_weights, vector_values, tokens, output_grad)
    placed, block_row, input_row = run_layer(
        owner_slot, gathered, token_row.reshape(-1, D), grad_row.reshape(-1, D), segment_ids
    )
    total, block_land, input_land = reduce_all(
        placed, block_row.reshape(tokens.shape), input_row.reshape(tokens.shape)
    )
    updated = update_all(
        total, slot_weights, first_moment, second_moment, left_stats, right_stats, left_basis, right_basis,
        vector_values, vector_first, vector_second, block_land, input_land,
    )
    vectors = [value.reshape(-1) for value in updated[6:9]]
    return (updated[9], updated[10], *updated[:6], *vectors)


def solution(mesh):
    in_specs = (
        P("dp", "sp", None),
        P("dp", "sp", None),
        P("dp", None),
        P("dp", None),
        P(),
        P("dp", None, None),
        P("dp", None, None),
        P("dp", None, None),
        P("dp", None, None),
        P("dp", None, None),
        P("dp", None, None),
        P("dp", None, None),
        P("dp"),
        P("dp"),
        P("dp"),
    )
    out_specs = (
        P("dp", "sp", None),
        P("dp", "sp", None),
        P("dp", None, None),
        P("dp", None, None),
        P("dp", None, None),
        P("dp", None, None),
        P("dp", None, None),
        P("dp", None, None),
        P("dp"),
        P("dp"),
        P("dp"),
    )
    chosen = fast_device if dict(mesh.shape) == {"dp": 8, "sp": 4} else per_device
    return jax.shard_map(
        chosen, mesh=mesh, in_specs=in_specs, out_specs=out_specs, check_vma=False
    )
```
